32 devices in a mesh: rep: 16 (over z, x, core), shard: 2 (over y).
Axes of the slice: x: 2, y: 2, z: 4, core: 2. Of those that a mesh axis runs over, the one named last changes fastest.
Arguments:
- tokens: bfloat16 [2, 12288, 768], P(None, ('rep', 'shard')), may hold values from -6 to 6
- cotangent: bfloat16 [2, 12288, 768], P(None, ('rep', 'shard')), may hold values from -6 to 6
- seq_lengths: int32 [2, 16, 2], P(None, 'rep'), may hold values from 0 to 768, as said below
- w_query: bfloat16 [768, 768], P('shard'), may hold values from -0.21875 to 0.21875
- b_query: bfloat16 [768], P('shard'), may hold values from -1.5 to 1.5
- w_key: bfloat16 [768, 768], P('shard'), may hold values from -0.21875 to 0.21875
- w_value: bfloat16 [768, 768], P('shard'), may hold values from -0.21875 to 0.21875
- b_value: bfloat16 [768], P('shard'), may hold values from -0.5 to 0.5
- w_attn: bfloat16 [768, 768], P('shard'), may hold values from -3 to 3
- b_attn: bfloat16 [768], P('shard'), may hold values from -1 to 1
- norm_gain: bfloat16 [768], P('shard'), may hold values from 0.5 to 1.5
- norm_bias: bfloat16 [768], P('shard'), may hold values from -1 to 1
- w_up: bfloat16 [768, 3072], P('shard'), may hold values from -0.21875 to 0.21875
- b_up: bfloat16 [3072], P('shard'), may hold values from -1.5 to 1.5
- w_down: bfloat16 [3072, 768], P('shard'), may hold values from -0.109375 to 0.109375
- b_down: bfloat16 [768], P('shard'), may hold values from -1 to 1
- out_gain: bfloat16 [768], P('shard'), may hold values from 0.5 to 1.5
- out_bias: bfloat16 [768], P('shard'), may hold values from -1 to 1
Outputs:
- layer_out: bfloat16 [2, 12288, 768], P(None, ('rep', 'shard'))
- tokens_grad: bfloat16 [2, 12288, 768], P(None, ('rep', 'shard'))
- grad_w_query: float32 [768, 768], P('shard')
- grad_b_query: float32 [768], P('shard')
- grad_w_key: float32 [768, 768], P('shard')
- grad_w_value: float32 [768, 768], P('shard')
- grad_b_value: float32 [768], P('shard')
- grad_w_attn: float32 [768, 768], P('shard')
- grad_b_attn: float32 [768], P('shard')
- grad_norm_gain: float32 [768], P('shard')
- grad_norm_bias: float32 [768], P('shard')
- grad_w_up: float32 [768, 3072], P('shard')
- grad_b_up: float32 [3072], P('shard')
- grad_w_down: float32 [3072, 768], P('shard')
- grad_b_down: float32 [768], P('shard')
- grad_out_gain: float32 [768], P('shard')
- grad_out_bias: float32 [768], P('shard')
The draws below stay inside these ranges and needn't reach their ends.
Inputs may be any that keep to these rules, and one draw needn't show every extreme that they name: `seq_lengths`: each row gives the lengths of 1 sequence in their order in the group, exactly one sequence of 768 tokens filling the group with a padding length of 0 (1024 exceeds the group); each row sums to 768.
All inputs are finite; a program needn't handle non-finite values.
Results may differ from the reference program's by a relative error of at most 0.02.
Values may be sent and summed in bfloat16 or wider, within the bound.
A program may use at most 192 MiB of HBM per device.

```python
import jax
import jax.numpy as jnp
from jax import lax

D = 768
H = 12
DH = 64
FF = 3072
MB = 2
LEAST_LEN = 1024
GROUP_TOK = 768
SEQ_GROUP = 1
TOKENS = 12288
N_REP = 16


def draw_seq_lengths(key, part):
    shortest = min(LEAST_LEN, GROUP_TOK // SEQ_GROUP)
    spare = GROUP_TOK - SEQ_GROUP * shortest
    cuts = jax.random.randint(key, (MB, N_REP, SEQ_GROUP), 0, spare + 1).astype(jnp.int32)
    first_row = (jnp.arange(MB, dtype=jnp.int32)[:, None, None] == 0) & (jnp.arange(N_REP, dtype=jnp.int32)[None, :, None] == 0)
    cuts = jnp.where(first_row, jnp.int32(spare), cuts)
    cuts = jnp.sort(cuts, axis=-1)
    lower = jnp.zeros((MB, N_REP, 1), jnp.int32)
    upper = jnp.full((MB, N_REP, 1), spare, jnp.int32)
    edges = jnp.concatenate([lower, cuts, upper], axis=-1)
    pieces = edges[:, :, 1:] - edges[:, :, :-1]
    base = jnp.concatenate([jnp.full((SEQ_GROUP,), shortest, jnp.int32), jnp.zeros((1,), jnp.int32)])
    return (pieces + base[None, None, :]).astype(jnp.int32)


def level_of(stream_key, dims, shards, low, largest):
    loudness, own = 1.0, jax.random.fold_in(stream_key, 6)
    for position, blocks in shards:
        draws = jnp.exp(jax.random.uniform(jax.random.fold_in(own, position), (blocks,), jnp.float32, low / len(shards), largest / len(shards)))
        loudness = loudness * jnp.repeat(draws, dims[position] // blocks).reshape([-1 if axis == position else 1 for axis in range(len(dims))])
    return loudness


def noise(own_key, shape, spread, bound, shards=(), kind=jnp.bfloat16):
    level = level_of(own_key, shape, shards, -0.22, 0.18) if shards else 1.0
    result = jax.random.normal(own_key, shape, jnp.float32) * spread * level
    return jnp.minimum(jnp.maximum(result, -bound), bound).astype(kind)


def setup_inputs(seed: int = 0) -> dict:
    seeds = jax.random.split(jax.random.key(seed), 19)
    tokens = noise(seeds[0], (MB, TOKENS, D), 1.0, 6.0, ((1, 32),))
    cotangent = noise(seeds[1], (MB, TOKENS, D), 1.0, 6.0, ((1, 32),))
    seq_lengths = draw_seq_lengths(jax.random.fold_in(seeds[18], 71), 0)
    w_query = noise(seeds[3], (D, D), D ** -0.5, 0.21875, ((0, 2),))
    b_query = noise(seeds[4], (D,), 0.3, 1.5, ((0, 2),))
    w_key = noise(seeds[5], (D, D), D ** -0.5, 0.21875, ((0, 2),))
    w_value = noise(seeds[6], (D, D), D ** -0.5, 0.21875, ((0, 2),))
    b_value = noise(seeds[7], (D,), 0.1, 0.5, ((0, 2),))
    w_attn = noise(seeds[8], (D, D), (max(1, D // 192)) ** -0.5, 3.0, ((0, 2),))
    b_attn = noise(seeds[9], (D,), 0.2, 1.0, ((0, 2),))
    norm_gain = jnp.clip(1.0 + 0.1 * jax.random.normal(seeds[10], (D,), jnp.float32), 0.5, 1.5).astype(jnp.bfloat16)
    norm_bias = noise(seeds[11], (D,), 0.2, 1.0, ((0, 2),))
    w_up = noise(seeds[12], (D, FF), D ** -0.5, 0.21875, ((0, 2),))
    b_up = noise(seeds[13], (FF,), 0.3, 1.5, ((0, 2),))
    w_down = noise(seeds[14], (FF, D), FF ** -0.5, 0.109375, ((0, 2),))
    b_down = noise(seeds[15], (D,), 0.2, 1.0, ((0, 2),))
    out_gain = jnp.clip(1.0 + 0.1 * jax.random.normal(seeds[16], (D,), jnp.float32), 0.5, 1.5).astype(jnp.bfloat16)
    out_bias = noise(seeds[17], (D,), 0.2, 1.0, ((0, 2),))
    return dict(tokens=tokens, cotangent=cotangent, seq_lengths=seq_lengths, w_query=w_query, b_query=b_query, w_key=w_key, w_value=w_value, b_value=b_value, w_attn=w_attn, b_attn=b_attn, norm_gain=norm_gain, norm_bias=norm_bias, w_up=w_up, b_up=b_up, w_down=w_down, b_down=b_down, out_gain=out_gain, out_bias=out_bias)


@jax.custom_vjp
def low(v):
    return lax.optimization_barrier(v.astype(jnp.bfloat16)).astype(jnp.float32)

@jax.custom_vjp
def low_back(v):
    return v

def low_keep(v):
    return (low(v), None)

def low_pass(kept, grad):
    return (grad,)

def back_keep(v):
    return (v, None)

def back_low(kept, grad):
    return (low(grad),)
low.defvjp(low_keep, low_pass)
low_back.defvjp(back_keep, back_low)
EPS = 1e-12
NEG = -1e+30

def matmul(left, right):
    return jnp.dot(left, right, precision=lax.Precision.HIGHEST)

def segment_ids(row, count):
    bounds = jnp.cumsum(row[:-1]).astype(jnp.int32)
    places = jnp.arange(count, dtype=jnp.int32)
    return lax.optimization_barrier(jnp.sum((places[:, None] >= bounds[None, :]).astype(jnp.int32), axis=1)).astype(jnp.int32)

def normalize(rows, gain, bias):
    mean = lax.optimization_barrier(jnp.mean(rows, axis=-1, keepdims=True))
    centered = rows - mean
    inverse = lax.rsqrt(lax.optimization_barrier(jnp.mean(centered * centered, axis=-1, keepdims=True)) + EPS)
    return centered * inverse * gain + bias

def split_heads(rows):
    return rows.reshape(rows.shape[0], H, DH).transpose(1, 0, 2)

def forward(x, weights, ids):
    w_query, b_query, w_key, w_value, b_value, w_attn, b_attn, norm_gain, norm_bias, w_up, b_up, w_down, b_down, out_gain, out_bias = weights
    count = x.shape[0]
    query = low(low_back(matmul(x, w_query) + b_query))
    keys = low(low_back(matmul(x, w_key)))
    values = low(low_back(matmul(x, w_value) + b_value))
    mask = ids[:, None] == ids[None, :]
    scale = DH ** (-0.5)

    def one_head(parts):
        head_query, head_keys, head_values = parts
        scores = low_back(matmul(head_query, head_keys.T) * scale)
        probs = jax.nn.softmax(jnp.where(mask, scores, NEG), axis=-1)
        return matmul(low(probs), head_values)
    mixed = lax.map(jax.checkpoint(one_head), (split_heads(query), split_heads(keys), split_heads(values)))
    attn = low(low_back(mixed.transpose(1, 0, 2).reshape(count, D)))
    projected = low_back(matmul(attn, w_attn) + b_attn)
    hidden = normalize(x + projected, norm_gain, norm_bias)
    pre = low_back(matmul(low(hidden), w_up) + b_up)
    active = low(jax.nn.gelu(pre, approximate=False))
    branch = low_back(matmul(active, w_down) + b_down)
    return normalize(hidden + branch, out_gain, out_bias)

def reference(tokens, cotangent, seq_lengths, w_query, b_query, w_key, w_value, b_value, w_attn, b_attn, norm_gain, norm_bias, w_up, b_up, w_down, b_down, out_gain, out_bias):
    weights = tuple((w.astype(jnp.float32) for w in (w_query, b_query, w_key, w_value, b_value, w_attn, b_attn, norm_gain, norm_bias, w_up, b_up, w_down, b_down, out_gain, out_bias)))
    items = tokens.reshape(MB * N_REP, GROUP_TOK, D)
    slopes = cotangent.reshape(MB * N_REP, GROUP_TOK, D)
    rows = seq_lengths.reshape(MB * N_REP, SEQ_GROUP + 1)

    def step(carry, item):
        x_in, grad_in, row = item
        ids = segment_ids(row, GROUP_TOK)
        valid = (ids < SEQ_GROUP).astype(jnp.float32)

        def run(inputs, params):
            return forward(inputs, params, ids)
        layer, pullback = jax.vjp(run, x_in.astype(jnp.float32), weights)
        x_grad, w_grads = pullback(grad_in.astype(jnp.float32) * valid[:, None])
        carry = jax.tree.map(lambda a, b: a + b, carry, w_grads)
        return (carry, (layer.astype(jnp.bfloat16), x_grad.astype(jnp.bfloat16)))
    start = jax.tree.map(jnp.zeros_like, weights)
    totals, (layers, x_grads) = lax.scan(step, start, (items, slopes, rows))
    return (layers.reshape(MB, TOKENS, D), x_grads.reshape(MB, TOKENS, D), totals[0], totals[1], totals[2], totals[3], totals[4], totals[5], totals[6], totals[7], totals[8], totals[9], totals[10], totals[11], totals[12], totals[13], totals[14])
```

```python
import functools

import jax
import jax.numpy as jnp
from jax import lax
from jax.experimental import pallas as pl
from jax.experimental.pallas import tpu as pltpu
from jax.sharding import PartitionSpec as P

D = 768
H = 12
DH = 64
PAIR = 2 * DH
EPS = 1e-12
BIG = 1e30
SCALE = DH ** (-0.5)
ROWS = 256
f32 = jnp.float32
bf16 = jnp.bfloat16


def mm(left, right):
    return jnp.dot(left, right, preferred_element_type=f32)


def mm_nt(left, right):
    return lax.dot_general(left, right, (((1,), (1,)), ((), ())), preferred_element_type=f32)


def mm_tn(left, right):
    return lax.dot_general(left, right, (((0,), (0,)), ((), ())), preferred_element_type=f32)


def segment_ids(row, count):
    bounds = jnp.cumsum(row[:-1])
    places = jnp.arange(count, dtype=jnp.int32)
    return jnp.sum((places[:, None] >= bounds[None, :]).astype(jnp.int32), axis=1)


def mask_columns(ids):
    first = (ids == 0).astype(f32)[:, None]
    other = 1.0 - first
    lane = lax.broadcasted_iota(jnp.int32, (1, PAIR), 1) % DH
    on_query = jnp.where(lane == 0, -BIG * first, jnp.where(lane == 1, -BIG * other, 0.0))
    on_key = jnp.where(lane == 0, other, jnp.where(lane == 1, first, 0.0))
    return on_query.astype(bf16), on_key.astype(bf16)


def forward_heads(q_ref, k_ref, v_ref, mq_ref, mk_ref, attn_ref, lse_ref):
    lane = lax.broadcasted_iota(jnp.int32, (1, PAIR), 1)
    low = lane < DH
    keys, values, mk = k_ref[...], v_ref[...], mk_ref[...]
    one = jnp.ones_like(values)
    sides = []
    for own in (low, jnp.logical_not(low)):
        sides.append((own, jnp.where(own, keys, mk), jnp.where(own, values, one)))
    count = q_ref.shape[0]
    block = min(ROWS, count)
    for start in range(0, count, block):
        rows = pl.ds(start, block)
        query, mq = q_ref[rows, :] * SCALE, mq_ref[rows, :]
        outs = []
        for own, some_keys, some_values in sides:
            scores = mm_nt(jnp.where(own, query, mq), some_keys)
            top = jnp.max(scores, axis=1, keepdims=True)
            expo = jnp.exp(scores - top).astype(bf16)
            mixed = mm(expo, some_values)
            total = pltpu.roll(mixed, DH, 1)
            outs.append((mixed / total, top + jnp.log(total)))
        attn_ref[rows, :] = jnp.where(low, outs[0][0], outs[1][0]).astype(bf16)
        lse_ref[rows, :] = jnp.where(low, outs[0][1], outs[1][1])


def three_parts(value):
    first = value.astype(bf16).astype(f32)
    rest = value - first
    second = rest.astype(bf16).astype(f32)
    return first, second, rest - second


def backward_heads(
    q_ref, k_ref, v_ref, mq_ref, mk_ref, attn_ref, lse_ref, grad_ref, dq_ref, dk_ref, dv_ref
):
    lane = lax.broadcasted_iota(jnp.int32, (1, PAIR), 1)
    place = lane % DH
    low = lane < DH
    query, mq, grad = q_ref[...] * SCALE, mq_ref[...], grad_ref[...]
    product = grad.astype(f32) * attn_ref[...].astype(f32)
    lse = three_parts(-pltpu.roll(lse_ref[...], DH, 1))
    count_keys = k_ref.shape[0]
    block = min(ROWS, count_keys)
    sides = []
    for own in (low, jnp.logical_not(low)):
        delta = three_parts(-jnp.sum(jnp.where(own, product, 0.0), axis=1, keepdims=True))
        more = jnp.where(place == 2, lse[0], jnp.where(place == 3, lse[1], lse[2]))
        more = jnp.where(place < 2, mq, jnp.where(place < 5, more, 0.0).astype(bf16))
        some_query = jnp.where(own, query, more)
        more = jnp.where(place == 0, delta[0], jnp.where(place == 1, delta[1], delta[2]))
        some_grad = jnp.where(own, grad, jnp.where(place < 3, more, 0.0).astype(bf16))
        sides.append((own, some_query, some_grad, None))
    totals = [None, None]
    for start in range(0, count_keys, block):
        rows = pl.ds(start, block)
        keys, values, mk = k_ref[rows, :], v_ref[rows, :], mk_ref[rows, :]
        ones = jnp.ones_like(values)
        zeros = jnp.zeros_like(values)
        more_keys = jnp.where(place < 2, mk, jnp.where(place < 5, ones, zeros))
        more_values = jnp.where(place < 3, ones, zeros)
        parts = []
        for side in range(2):
            own, some_query, some_grad, _ = sides[side]
            some_keys = jnp.where(own, keys, more_keys)
            some_values = jnp.where(own, values, more_values)
            probs = jnp.exp(mm_nt(some_keys, some_query))
            slope = (probs * mm_nt(some_values, some_grad)).astype(bf16)
            dv = mm(probs.astype(bf16), some_grad)
            dk = mm(slope, some_query)
            dq = mm_tn(slope, some_keys)
            totals[side] = dq if totals[side] is None else totals[side] + dq
            parts.append((dk, dv))
        dk_ref[rows, :] = jnp.where(low, parts[0][0], parts[1][0]).astype(bf16)
        dv_ref[rows, :] = jnp.where(low, parts[0][1], parts[1][1]).astype(bf16)
    dq_ref[...] = (jnp.where(low, totals[0], totals[1]) * SCALE).astype(bf16)


def head_block(rows, offset):
    return pl.BlockSpec((rows, PAIR), lambda i: (0, i + offset))


def fixed_block(rows):
    return pl.BlockSpec((rows, PAIR), lambda i: (0, 0))


def attention_forward(query_array, key_array, offsets, mq, mk):
    count, keys = query_array.shape[0], key_array.shape[0]
    pairs = H * DH // PAIR
    return pl.pallas_call(
        forward_heads,
        grid=(pairs,),
        out_shape=(
            jax.ShapeDtypeStruct((count, D), bf16),
            jax.ShapeDtypeStruct((count, D), f32),
        ),
        in_specs=[
            head_block(count, 0),
            head_block(keys, offsets[0]),
            head_block(keys, offsets[1]),
            fixed_block(count),
            fixed_block(keys),
        ],
        out_specs=(head_block(count, 0), head_block(count, 0)),
        cost_estimate=pl.CostEstimate(
            flops=16 * count * keys * D, bytes_accessed=8 * (count + keys) * D, transcendentals=count * keys * H
        ),
        name="attention_forward",
    )(query_array, key_array, key_array, mq, mk)


def attention_backward(query_array, key_array, offsets, mq, mk, attn, lse, grad):
    count, keys = query_array.shape[0], key_array.shape[0]
    pairs = H * DH // PAIR
    return pl.pallas_call(
        backward_heads,
        grid=(pairs,),
        out_shape=(
            jax.ShapeDtypeStruct((count, D), bf16),
            jax.ShapeDtypeStruct((keys, D), bf16),
            jax.ShapeDtypeStruct((keys, D), bf16),
        ),
        in_specs=[
            head_block(count, 0),
            head_block(keys, offsets[0]),
            head_block(keys, offsets[1]),
            fixed_block(count),
            fixed_block(keys),
            head_block(count, 0),
            head_block(count, 0),
            head_block(count, 0),
        ],
        out_specs=(head_block(count, 0), head_block(keys, 0), head_block(keys, 0)),
        cost_estimate=pl.CostEstimate(
            flops=40 * count * keys * D, bytes_accessed=16 * (count + keys) * D, transcendentals=count * keys * H
        ),
        name="attention_backward",
    )(query_array, key_array, key_array, mq, mk, attn, lse, grad)


def normalize(rows):
    mean = jnp.mean(rows, axis=-1, keepdims=True)
    centered = rows - mean
    inverse = lax.rsqrt(jnp.mean(centered * centered, axis=-1, keepdims=True) + EPS)
    return centered * inverse, inverse


def norm_back(grad, normed, inverse, gain):
    scaled = grad * gain
    first = jnp.mean(scaled, axis=-1, keepdims=True)
    second = jnp.mean(scaled * normed, axis=-1, keepdims=True)
    return inverse * (scaled - first - normed * second)


def swap(value, axis, size, move):
    return lax.ppermute(value, axis, [(i, move(i)) for i in range(size)])


def put(buffer, value, index, axis=0):
    return lax.dynamic_update_slice_in_dim(buffer, value, index * value.shape[axis], axis)


def pick(value, index, parts, axis=0):
    size = value.shape[axis] // parts
    return lax.dynamic_slice_in_dim(value, index * size, size, axis)


class Places:
    def __init__(self):
        self.reps = lax.axis_size("rep")
        self.shards = lax.axis_size("shard")
        self.rep = lax.axis_index("rep")
        self.shard = lax.axis_index("shard")
        self.core = self.rep % 2


def gather_rows(at, own):
    half = own.shape[0] // 2
    out = jnp.zeros((at.shards * own.shape[0],) + own.shape[1:], own.dtype)
    out = put(out, own, at.shard)
    mine = pick(own, at.core, 2)
    for step in range(1, at.shards):
        there = swap(mine, "shard", at.shards, lambda i: (i + at.shards - step) % at.shards)
        other = swap(there, "rep", at.reps, lambda i: i ^ 1)
        block = (at.shard + step) % at.shards * 2
        out = put(out, there, block + at.core)
        out = put(out, other, block + 1 - at.core)
    return out


def reduce_rows(at, grad):
    shards, columns = at.shards, grad.shape[1]
    rows = grad.shape[0] // shards
    value = grad.reshape(shards * 2, rows // 2, columns)
    value = grad.reshape(shards, 2, rows // 2, columns)
    mine = lax.dynamic_index_in_dim(value, at.core, 1, False)
    away = lax.dynamic_index_in_dim(value, 1 - at.core, 1, False).astype(bf16)
    value = mine.astype(f32) + swap(away, "rep", at.reps, lambda i: i ^ 1).astype(f32)
    total = lax.dynamic_index_in_dim(value, at.shard, 0, False)
    for step in range(1, shards):
        away = lax.dynamic_index_in_dim(value, (at.shard + step) % shards, 0, False).astype(bf16)
        total = total + swap(away, "shard", shards, lambda i: (i + step) % shards).astype(f32)
    stages = []
    bit = 2
    while bit < at.reps:
        axis = 0 if total.shape[0] % 32 == 0 else 1
        stages.append((bit, axis))
        up = (at.rep // bit) % 2
        mine, away = pick(total, up, 2, axis), pick(total, 1 - up, 2, axis).astype(bf16)
        move = functools.partial(lambda b, i: i ^ b, bit)
        total = mine + swap(away, "rep", at.reps, move).astype(f32)
        bit *= 2
    total = total.astype(bf16)
    for bit, axis in reversed(stages):
        up = (at.rep // bit) % 2
        move = functools.partial(lambda b, i: i ^ b, bit)
        other = swap(total, "rep", at.reps, move)
        shape = list(total.shape)
        shape[axis] *= 2
        both = jnp.zeros(shape, bf16)
        total = put(put(both, total, up, axis), other, 1 - up, axis)
    other = swap(total, "rep", at.reps, lambda i: i ^ 1)
    first = jnp.where(at.core == 0, total, other)
    second = jnp.where(at.core == 0, other, total)
    return jnp.concatenate([first, second], axis=0).astype(f32)


def spread(at, value):
    micro, shards = value.shape[0], at.shards
    parts = []
    for step in range(micro):
        moves = [(i, (i + step) % micro * (shards // micro) + i // micro) for i in range(shards)]
        part = lax.dynamic_index_in_dim(value, (at.shard + step) % micro, 0, False)
        if any(a != b for a, b in moves):
            part = lax.ppermute(part, "shard", moves)
        parts.append(part)
    return jnp.concatenate(parts, axis=0)


def collect(at, value, micro):
    shards = at.shards
    slots = value.shape[0] // micro
    out = jnp.zeros((micro, slots) + value.shape[1:], value.dtype)
    for step in range(micro):
        moves = [((i + step) % micro * (shards // micro) + i // micro, i) for i in range(shards)]
        part = value[step * slots : (step + 1) * slots]
        if any(a != b for a, b in moves):
            part = lax.ppermute(part, "shard", moves)
        out = lax.dynamic_update_index_in_dim(out, part, (at.shard + step) % micro, 0)
    return out


def body(
    tokens,
    cotangent,
    seq_lengths,
    w_query,
    b_query,
    w_key,
    w_value,
    b_value,
    w_attn,
    b_attn,
    norm_gain,
    norm_bias,
    w_up,
    b_up,
    w_down,
    b_down,
    out_gain,
    out_bias,
):
    at = Places()
    shards = at.shards
    micro, slots = tokens.shape[0], tokens.shape[1]
    span = shards // micro
    count = micro * slots
    x = spread(at, tokens)
    w_three = gather_rows(at, jnp.concatenate([w_query, w_key, w_value], axis=1))
    part = w_query.shape[0]
    wide = b_up.shape[0] // part
    vectors = jnp.concatenate(
        [
            jnp.stack(
                [b_query, b_value, b_attn, norm_gain, norm_bias, b_down, out_gain, out_bias]
            ),
            b_up.reshape(wide, part),
            jnp.zeros((16 - 8 - wide, part), bf16),
        ],
        axis=0,
    )
    table = put(jnp.zeros((shards,) + vectors.shape, bf16), vectors[None], at.shard)
    for step in range(1, shards):
        there = swap(vectors, "shard", shards, lambda i: (i + shards - step) % shards)
        table = put(table, there[None], (at.shard + step) % shards)
    table = table.astype(f32)
    (c_query, c_value, c_attn, c_gain, c_bias, c_down, c_out_gain, c_out_bias) = [
        table[:, i].reshape(1, D) for i in range(8)
    ]
    c_up = table[:, 8 : 8 + wide].reshape(1, D * wide)
    w_proj = gather_rows(at, w_attn)
    full_up = gather_rows(at, w_up)
    full_down = gather_rows(at, w_down)
    slope_in = spread(at, cotangent)

    group = slots * shards
    which, inner = at.shard // span, at.shard % span
    row = lax.dynamic_index_in_dim(seq_lengths[:, 0], which, 0, False)
    ids = segment_ids(row, group)

    def ids_of(device):
        parts = []
        for step in range(micro):
            source = micro * device + (which + micro - step) % micro
            parts.append(lax.dynamic_slice_in_dim(ids, source * slots, slots))
        return jnp.concatenate(parts)

    query_ids = ids_of(inner)
    nseq = seq_lengths.shape[-1] - 1
    valid = (query_ids < nseq).astype(f32)[:, None]
    three = mm(x, w_three) + jnp.concatenate([c_query, jnp.zeros_like(c_query), c_value], axis=1)
    three = three.astype(bf16)
    base = D // PAIR
    offsets = (base, 2 * base)
    key_array = three
    key_ids = [query_ids]
    if span > 1:
        offsets = (0, base)
        own = three[:, D:]
        parts = [own]
        for step in range(1, span):
            moves = [(i, i // span * span + (i + span - step) % span) for i in range(shards)]
            parts.append(lax.ppermute(own, "shard", moves))
            key_ids.append(ids_of((inner + step) % span))
        key_array = jnp.concatenate(parts, axis=0)
    mq, _ = mask_columns(query_ids)
    _, mk = mask_columns(jnp.concatenate(key_ids))
    attn, lse = attention_forward(three, key_array, offsets, mq, mk)

    normed_one, inverse_one = normalize(x.astype(f32) + mm(attn, w_proj) + c_attn)
    hidden = normed_one * c_gain + c_bias
    hidden_low = hidden.astype(bf16)
    pre = mm(hidden_low, full_up) + c_up
    lower = 0.5 * (1.0 + lax.erf(pre * 0.7071067811865476))
    active = (pre * lower).astype(bf16)
    density = jnp.exp(-0.5 * pre * pre) * 0.3989422804014327
    gelu_slope = lower + pre * density
    normed_two, inverse_two = normalize(hidden + mm(active, full_down) + c_down)
    layer = (normed_two * c_out_gain + c_out_bias).astype(bf16)
    grad_out = slope_in.astype(f32) * valid
    d_out_gain = jnp.sum(grad_out * normed_two, axis=0)
    d_out_bias = jnp.sum(grad_out, axis=0)
    grad_second = norm_back(grad_out, normed_two, inverse_two, c_out_gain)
    grad_branch = grad_second.astype(bf16)
    d_down = jnp.sum(grad_branch.astype(f32), axis=0)
    g_down = mm_tn(active, grad_branch)
    grad_pre = (mm_nt(grad_branch, full_down) * gelu_slope).astype(bf16)
    d_up = jnp.sum(grad_pre.astype(f32), axis=0)
    g_up = mm_tn(hidden_low, grad_pre)
    grad_hidden = mm_nt(grad_pre, full_up) + grad_second
    d_gain = jnp.sum(grad_hidden * normed_one, axis=0)
    d_bias = jnp.sum(grad_hidden, axis=0)
    grad_first = norm_back(grad_hidden, normed_one, inverse_one, c_gain)
    grad_proj = grad_first.astype(bf16)
    d_attn = jnp.sum(grad_proj.astype(f32), axis=0)
    g_attn = mm_tn(attn, grad_proj)
    grad_attn = mm_nt(grad_proj, w_proj).astype(bf16)
    dq, dk, dv = attention_backward(three, key_array, offsets, mq, mk, attn, lse, grad_attn)
    if span > 1:
        both = jnp.concatenate([dk, dv], axis=1)
        total = both[:count].astype(f32)
        for step in range(1, span):
            moves = [(i, i // span * span + (i + step) % span) for i in range(shards)]
            away = both[step * count : (step + 1) * count]
            total = total + lax.ppermute(away, "shard", moves).astype(f32)
        dk, dv = total[:, :D].astype(bf16), total[:, D:].astype(bf16)
    d_three = jnp.concatenate([dq, dk, dv], axis=1)
    d_query = jnp.sum(dq.astype(f32), axis=0)
    d_value = jnp.sum(dv.astype(f32), axis=0)
    g_three = mm_tn(x, d_three)
    back = (grad_first + mm_nt(d_three, w_three)).astype(bf16)

    sums = jnp.concatenate(
        [
            jnp.stack([d_query, d_value, d_attn, d_gain, d_bias, d_down, d_out_gain, d_out_bias]).reshape(
                8, shards, part
            ),
            d_up.reshape(shards, wide, part).transpose(1, 0, 2),
            jnp.zeros((PAIR - 8 - wide, shards, part), f32),
        ],
        axis=0,
    )
    sums = sums.reshape(PAIR, D).T
    r_down = reduce_rows(at, g_down)
    r_up = reduce_rows(at, g_up)
    r_attn = reduce_rows(at, g_attn)
    r_three = reduce_rows(at, jnp.concatenate([g_three, sums], axis=1))
    small = r_three[:, 3 * D :].T
    return (
        collect(at, layer, micro),
        collect(at, back, micro),
        r_three[:, :D],
        small[0],
        r_three[:, D : 2 * D],
        r_three[:, 2 * D : 3 * D],
        small[1],
        r_attn,
        small[2],
        small[3],
        small[4],
        r_up,
        small[8 : 8 + wide].reshape(wide * part),
        r_down,
        small[5],
        small[6],
        small[7],
    )


def solution(mesh):
    rows, vector = P("shard", None), P("shard")
    tokens = P(None, ("rep", "shard"), None)
    weights = (rows, vector, rows, rows, vector, rows, vector, vector, vector)
    weights += (rows, vector, rows, vector, vector, vector)
    return jax.shard_map(
        body,
        mesh=mesh,
        in_specs=(tokens, tokens, P(None, "rep", None)) + weights,
        out_specs=(tokens, tokens) + weights,
        check_vma=False,
    )
```

```python
import functools

import jax
import jax.numpy as jnp
from jax import lax
from jax.experimental import pallas as pl
from jax.experimental.pallas import tpu as pltpu
from jax.sharding import PartitionSpec as P

D = 768
H = 12
DH = 64
PAIR = 2 * DH
EPS = 1e-12
BIG = 1e30
SCALE = DH ** (-0.5)
ROWS = 256
f32 = jnp.float32
bf16 = jnp.bfloat16


def mm(left, right):
    return jnp.dot(left, right, preferred_element_type=f32)


def mm_nt(left, right):
    return lax.dot_general(left, right, (((1,), (1,)), ((), ())), preferred_element_type=f32)


def mm_tn(left, right):
    return lax.dot_general(left, right, (((0,), (0,)), ((), ())), preferred_element_type=f32)


def segment_ids(row, count):
    bounds = jnp.cumsum(row[:-1])
    places = jnp.arange(count, dtype=jnp.int32)
    return jnp.sum((places[:, None] >= bounds[None, :]).astype(jnp.int32), axis=1)


def mask_columns(ids):
    first = (ids == 0).astype(f32)[:, None]
    other = 1.0 - first
    lane = lax.broadcasted_iota(jnp.int32, (1, PAIR), 1) % DH
    on_query = jnp.where(lane == 0, -BIG * first, jnp.where(lane == 1, -BIG * other, 0.0))
    on_key = jnp.where(lane == 0, other, jnp.where(lane == 1, first, 0.0))
    return on_query.astype(bf16), on_key.astype(bf16)


def forward_heads(q_ref, k_ref, v_ref, mq_ref, mk_ref, attn_ref, lse_ref):
    lane = lax.broadcasted_iota(jnp.int32, (1, PAIR), 1)
    low = lane < DH
    keys, values, mk = k_ref[...], v_ref[...], mk_ref[...]
    one = jnp.ones_like(values)
    sides = []
    for own in (low, jnp.logical_not(low)):
        sides.append((own, jnp.where(own, keys, mk), jnp.where(own, values, one)))
    count = q_ref.shape[0]
    block = min(ROWS, count)
    for start in range(0, count, block):
        rows = pl.ds(start, block)
        query, mq = q_ref[rows, :] * SCALE, mq_ref[rows, :]
        outs = []
        for own, some_keys, some_values in sides:
            scores = mm_nt(jnp.where(own, query, mq), some_keys)
            top = jnp.max(scores, axis=1, keepdims=True)
            expo = jnp.exp(scores - top).astype(bf16)
            mixed = mm(expo, some_values)
            total = pltpu.roll(mixed, DH, 1)
            outs.append((mixed / total, top + jnp.log(total)))
        attn_ref[rows, :] = jnp.where(low, outs[0][0], outs[1][0]).astype(bf16)
        lse_ref[rows, :] = jnp.where(low, outs[0][1], outs[1][1])


def three_parts(value):
    first = value.astype(bf16).astype(f32)
    rest = value - first
    second = rest.astype(bf16).astype(f32)
    return first, second, rest - second


def backward_heads(
    q_ref, k_ref, v_ref, mq_ref, mk_ref, attn_ref, lse_ref, grad_ref, dq_ref, dk_ref, dv_ref
):
    lane = lax.broadcasted_iota(jnp.int32, (1, PAIR), 1)
    place = lane % DH
    low = lane < DH
    query, mq, grad = q_ref[...] * SCALE, mq_ref[...], grad_ref[...]
    product = grad.astype(f32) * attn_ref[...].astype(f32)
    lse = three_parts(-pltpu.roll(lse_ref[...], DH, 1))
    count_keys = k_ref.shape[0]
    block = min(ROWS, count_keys)
    sides = []
    for own in (low, jnp.logical_not(low)):
        delta = three_parts(-jnp.sum(jnp.where(own, product, 0.0), axis=1, keepdims=True))
        more = jnp.where(place == 2, lse[0], jnp.where(place == 3, lse[1], lse[2]))
        more = jnp.where(place < 2, mq, jnp.where(place < 5, more, 0.0).astype(bf16))
        some_query = jnp.where(own, query, more)
        more = jnp.where(place == 0, delta[0], jnp.where(place == 1, delta[1], delta[2]))
        some_grad = jnp.where(own, grad, jnp.where(place < 3, more, 0.0).astype(bf16))
        sides.append((own, some_query, some_grad, None))
    totals = [None, None]
    for start in range(0, count_keys, block):
        rows = pl.ds(start, block)
        keys, values, mk = k_ref[rows, :], v_ref[rows, :], mk_ref[rows, :]
        ones = jnp.ones_like(values)
        zeros = jnp.zeros_like(values)
        more_keys = jnp.where(place < 2, mk, jnp.where(place < 5, ones, zeros))
        more_values = jnp.where(place < 3, ones, zeros)
        parts = []
        for side in range(2):
            own, some_query, some_grad, _ = sides[side]
            some_keys = jnp.where(own, keys, more_keys)
            some_values = jnp.where(own, values, more_values)
            probs = jnp.exp(mm_nt(some_keys, some_query))
            slope = (probs * mm_nt(some_values, some_grad)).astype(bf16)
            dv = mm(probs.astype(bf16), some_grad)
            dk = mm(slope, some_query)
            dq = mm_tn(slope, some_keys)
            totals[side] = dq if totals[side] is None else totals[side] + dq
            parts.append((dk, dv))
        dk_ref[rows, :] = jnp.where(low, parts[0][0], parts[1][0]).astype(bf16)
        dv_ref[rows, :] = jnp.where(low, parts[0][1], parts[1][1]).astype(bf16)
    dq_ref[...] = (jnp.where(low, totals[0], totals[1]) * SCALE).astype(bf16)


def head_block(rows, offset):
    return pl.BlockSpec((rows, PAIR), lambda i: (0, i + offset))


def fixed_block(rows):
    return pl.BlockSpec((rows, PAIR), lambda i: (0, 0))


def attention_forward(query_array, key_array, offsets, mq, mk):
    count, keys = query_array.shape[0], key_array.shape[0]
    pairs = H * DH // PAIR
    return pl.pallas_call(
        forward_heads,
        grid=(pairs,),
        out_shape=(
            jax.ShapeDtypeStruct((count, D), bf16),
            jax.ShapeDtypeStruct((count, D), f32),
        ),
        in_specs=[
            head_block(count, 0),
            head_block(keys, offsets[0]),
            head_block(keys, offsets[1]),
            fixed_block(count),
            fixed_block(keys),
        ],
        out_specs=(head_block(count, 0), head_block(count, 0)),
        cost_estimate=pl.CostEstimate(
            flops=16 * count * keys * D, bytes_accessed=8 * (count + keys) * D, transcendentals=count * keys * H
        ),
        name="attention_forward",
    )(query_array, key_array, key_array, mq, mk)


def attention_backward(query_array, key_array, offsets, mq, mk, attn, lse, grad):
    count, keys = query_array.shape[0], key_array.shape[0]
    pairs = H * DH // PAIR
    return pl.pallas_call(
        backward_heads,
        grid=(pairs,),
        out_shape=(
            jax.ShapeDtypeStruct((count, D), bf16),
            jax.ShapeDtypeStruct((keys, D), bf16),
            jax.ShapeDtypeStruct((keys, D), bf16),
        ),
        in_specs=[
            head_block(count, 0),
            head_block(keys, offsets[0]),
            head_block(keys, offsets[1]),
            fixed_block(count),
            fixed_block(keys),
            head_block(count, 0),
            head_block(count, 0),
            head_block(count, 0),
        ],
        out_specs=(head_block(count, 0), head_block(keys, 0), head_block(keys, 0)),
        cost_estimate=pl.CostEstimate(
            flops=40 * count * keys * D, bytes_accessed=16 * (count + keys) * D, transcendentals=count * keys * H
        ),
        name="attention_backward",
    )(query_array, key_array, key_array, mq, mk, attn, lse, grad)


def normalize(rows):
    mean = jnp.mean(rows, axis=-1, keepdims=True)
    centered = rows - mean
    inverse = lax.rsqrt(jnp.mean(centered * centered, axis=-1, keepdims=True) + EPS)
    return centered * inverse, inverse


def norm_back(grad, normed, inverse, gain):
    scaled = grad * gain
    first = jnp.mean(scaled, axis=-1, keepdims=True)
    second = jnp.mean(scaled * normed, axis=-1, keepdims=True)
    return inverse * (scaled - first - normed * second)


def swap(value, axis, size, move):
    return lax.ppermute(value, axis, [(i, move(i)) for i in range(size)])


def put(buffer, value, index, axis=0):
    return lax.dynamic_update_slice_in_dim(buffer, value, index * value.shape[axis], axis)


def pick(value, index, parts, axis=0):
    size = value.shape[axis] // parts
    return lax.dynamic_slice_in_dim(value, index * size, size, axis)


class Places:
    def __init__(self):
        self.reps = lax.axis_size("rep")
        self.shards = lax.axis_size("shard")
        self.rep = lax.axis_index("rep")
        self.shard = lax.axis_index("shard")
        self.core = self.rep % 2


def gather_rows(at, own):
    half = own.shape[0] // 2
    out = jnp.zeros((at.shards * own.shape[0],) + own.shape[1:], own.dtype)
    out = put(out, own, at.shard)
    mine = pick(own, at.core, 2)
    for step in range(1, at.shards):
        there = swap(mine, "shard", at.shards, lambda i: (i + at.shards - step) % at.shards)
        other = swap(there, "rep", at.reps, lambda i: i ^ 1)
        block = (at.shard + step) % at.shards * 2
        out = put(out, there, block + at.core)
        out = put(out, other, block + 1 - at.core)
    return out


def reduce_rows(at, grad):
    shards, columns = at.shards, grad.shape[1]
    rows = grad.shape[0] // shards
    value = grad.reshape(shards * 2, rows // 2, columns)
    value = grad.reshape(shards, 2, rows // 2, columns)
    mine = lax.dynamic_index_in_dim(value, at.core, 1, False)
    away = lax.dynamic_index_in_dim(value, 1 - at.core, 1, False).astype(bf16)
    value = mine.astype(f32) + swap(away, "rep", at.reps, lambda i: i ^ 1).astype(f32)
    total = lax.dynamic_index_in_dim(value, at.shard, 0, False)
    for step in range(1, shards):
        away = lax.dynamic_index_in_dim(value, (at.shard + step) % shards, 0, False).astype(bf16)
        total = total + swap(away, "shard", shards, lambda i: (i + step) % shards).astype(f32)
    stages = []
    bit = 2
    while bit < at.reps:
        axis = 0 if total.shape[0] % 32 == 0 else 1
        stages.append((bit, axis))
        up = (at.rep // bit) % 2
        mine, away = pick(total, up, 2, axis), pick(total, 1 - up, 2, axis).astype(bf16)
        move = functools.partial(lambda b, i: i ^ b, bit)
        total = mine + swap(away, "rep", at.reps, move).astype(f32)
        bit *= 2
    total = total.astype(bf16)
    for bit, axis in reversed(stages):
        up = (at.rep // bit) % 2
        move = functools.partial(lambda b, i: i ^ b, bit)
        other = swap(total, "rep", at.reps, move)
        shape = list(total.shape)
        shape[axis] *= 2
        both = jnp.zeros(shape, bf16)
        total = put(put(both, total, up, axis), other, 1 - up, axis)
    other = swap(total, "rep", at.reps, lambda i: i ^ 1)
    first = jnp.where(at.core == 0, total, other)
    second = jnp.where(at.core == 0, other, total)
    return jnp.concatenate([first, second], axis=0).astype(f32)


def spread(at, value):
    micro, shards = value.shape[0], at.shards
    parts = []
    for step in range(micro):
        moves = [(i, (i + step) % micro * (shards // micro) + i // micro) for i in range(shards)]
        part = lax.dynamic_index_in_dim(value, (at.shard + step) % micro, 0, False)
        if any(a != b for a, b in moves):
            part = lax.ppermute(part, "shard", moves)
        parts.append(part)
    return jnp.concatenate(parts, axis=0)


def collect(at, value, micro):
    shards = at.shards
    slots = value.shape[0] // micro
    out = jnp.zeros((micro, slots) + value.shape[1:], value.dtype)
    for step in range(micro):
        moves = [((i + step) % micro * (shards // micro) + i // micro, i) for i in range(shards)]
        part = value[step * slots : (step + 1) * slots]
        if any(a != b for a, b in moves):
            part = lax.ppermute(part, "shard", moves)
        out = lax.dynamic_update_index_in_dim(out, part, (at.shard + step) % micro, 0)
    return out


def rows_at(start, size):
    return pl.ds(pl.multiple_of(start, 16), size)


def cols_at(start, size):
    return pl.ds(pl.multiple_of(start, PAIR), size)


class Here:
    def __init__(self):
        self.rep = lax.axis_index("rep")
        self.y = lax.axis_index("shard")
        self.core = lax.rem(self.rep, 2)
        self.x = lax.rem(lax.div(self.rep, 2), 2)

    def across(self, bit):
        up = lax.rem(lax.div(self.rep, bit), 2)
        return {"rep": self.rep + bit * (1 - 2 * up)}

    def over(self):
        return {"shard": 1 - self.y}


class Copies:
    def __init__(self, send, recv):
        self.send, self.recv, self.used, self.open = send, recv, 0, []

    def away(self, source, target, peer):
        k = self.used
        self.used += 1
        copy = pltpu.make_async_remote_copy(
            src_ref=source,
            dst_ref=target,
            send_sem=self.send.at[k],
            recv_sem=self.recv.at[k],
            device_id=peer,
            device_id_type=pl.DeviceIdType.MESH,
        )
        return copy

    def near(self, source, target):
        k = self.used
        self.used += 1
        return pltpu.make_async_copy(source, target, self.recv.at[k])


def greet(peers):
    barrier = pltpu.get_barrier_semaphore()
    for peer in peers:
        pl.semaphore_signal(barrier, inc=1, device_id=peer, device_id_type=pl.DeviceIdType.MESH)
    pl.semaphore_wait(barrier, len(peers))


class Gathered:
    def __init__(self, here, copies, own, full, cols):
        n = own.shape[0]
        h = n // 4
        q = 2 * here.x + here.core
        across = 2 * (1 - here.x) + here.core
        mine, other = here.y * n, (1 - here.y) * n

        def at(start, size):
            return full.at[rows_at(start, size), cols]

        self.local = copies.near(own, at(mine, n))
        self.over = copies.away(own.at[rows_at(q * h, h), :], at(mine + q * h, h), here.over())
        first, second = at(other + q * h, h), at(other + across * h, h)
        self.side = copies.away(first, first, here.across(2))
        self.core_one = copies.away(first, first, here.across(1))
        self.core_two = copies.away(second, second, here.across(1))

    def start(self):
        self.over.start()
        self.local.start()

    def forward_one(self):
        self.over.wait_recv()
        self.side.start()
        self.core_one.start()

    def forward_two(self):
        self.side.wait_recv()
        self.core_two.start()

    def ready(self):
        self.local.wait()
        self.core_one.wait_recv()
        self.core_two.wait_recv()

    def finish(self):
        for copy in (self.over, self.side, self.core_one, self.core_two):
            copy.wait_send()


def gelu_parts(pre):
    lower = 0.5 * (1.0 + lax.erf(pre * 0.7071067811865476))
    density = jnp.exp(-0.5 * pre * pre) * 0.3989422804014327
    return pre * lower, lower + pre * density


def forward_kernel(
    tokens,
    cotangent,
    seq,
    vectors,
    w_query,
    w_key,
    w_value,
    w_attn,
    w_up,
    w_down,
    o_x,
    o_three,
    o_attn,
    o_up,
    o_qkv,
    o_heads,
    o_lse,
    o_normed,
    o_inverse,
    o_hidden,
    o_active,
    o_branch,
    o_pre,
    o_second,
    o_layer,
    o_sums,
    o_sums_up,
    x,
    slope,
    three,
    proj,
    up,
    down,
    raw_vectors,
    vecs,
    vec_up,
    qkv,
    heads,
    lse,
    mq,
    mk,
    normed,
    inverse,
    hidden,
    active,
    bend,
    branch,
    second,
    layer,
    sums,
    sums_up,
    send,
    recv,
):
    here = Here()
    copies = Copies(send, recv)
    n = w_query.shape[0]
    y = here.y
    greet([here.over(), here.across(1), here.across(2)])

    g_query = Gathered(here, copies, w_query, three, pl.ds(0, D))
    g_key = Gathered(here, copies, w_key, three, pl.ds(D, D))
    g_value = Gathered(here, copies, w_value, three, pl.ds(2 * D, D))
    g_attn = Gathered(here, copies, w_attn, proj, pl.ds(0, D))
    g_up = Gathered(here, copies, w_up, up, pl.ds(0, up.shape[1]))
    g_down = Gathered(here, copies, w_down, down, pl.ds(0, D))
    vec_away = copies.away(vectors, raw_vectors.at[y], here.over())
    vec_near = copies.near(vectors, raw_vectors.at[y])
    low, high = pl.ds(0, n), pl.ds(n, n)
    x_away = copies.away(tokens.at[1 - y], x.at[high, :], here.over())
    x_near = copies.near(tokens.at[y], x.at[low, :])
    s_away = copies.away(cotangent.at[1 - y], slope.at[high, :], here.over())
    s_near = copies.near(cotangent.at[y], slope.at[low, :])
    for part in (g_query, g_key, g_value):
        part.start()
    vec_away.start()
    vec_near.start()
    x_away.start()
    x_near.start()
    for part in (g_attn, g_up, g_down):
        part.start()
    s_away.start()
    s_near.start()

    length = seq[y, 0]

    def inside(start, size):
        row = start + lax.broadcasted_iota(jnp.int32, (size, 1), 0)
        place = row + jnp.where(row < n, y * n, -y * n)
        return (place < length).astype(f32)

    first = inside(0, 2 * n)
    lane = lax.rem(lax.broadcasted_iota(jnp.int32, (1, PAIR), 1), DH)
    mq[...] = jnp.where(
        lane == 0, -BIG * first, jnp.where(lane == 1, -BIG * (1.0 - first), 0.0)
    ).astype(bf16)
    mk[...] = jnp.where(lane == 0, 1.0 - first, jnp.where(lane == 1, first, 0.0)).astype(bf16)

    for part in (g_query, g_key, g_value):
        part.forward_one()
    for part in (g_query, g_key, g_value):
        part.forward_two()
    vec_away.wait_recv()
    vec_near.wait()
    for half in range(2):
        table = raw_vectors[half].astype(f32)
        vecs[:, half * n : (half + 1) * n] = table
        wide = up.shape[1] // (2 * n)
        for i in range(wide):
            start = half * wide * n + i * n
            vec_up[:, start : start + n] = table[8 + i : 9 + i, :]
    for part in (g_query, g_key, g_value):
        part.ready()
    x_away.wait_recv()
    x_near.wait()

    tile = 256

    @pl.loop(0, 3 * D // tile)
    def _(i):
        cols = cols_at(i * tile, tile)
        which = lax.div(i, D // tile)
        inner = cols_at(lax.rem(i, D // tile) * tile, tile)
        bias = jnp.where(
            which == 0, vecs[0:1, inner], jnp.where(which == 2, vecs[1:2, inner], 0.0)
        )
        qkv[:, cols] = (mm(x[...], three[:, cols]) + bias).astype(bf16)

    lanes = lax.broadcasted_iota(jnp.int32, (1, PAIR), 1)
    left = lanes < DH
    lse[...] = jnp.zeros_like(lse)

    @pl.loop(0, H * DH // PAIR)
    def _(i):
        keys, values = qkv[:, cols_at(D + i * PAIR, PAIR)], qkv[:, cols_at(2 * D + i * PAIR, PAIR)]
        one = jnp.ones_like(values)
        sides = []
        for own in (left, jnp.logical_not(left)):
            sides.append((own, jnp.where(own, keys, mk[...]), jnp.where(own, values, one)))
        for start in range(0, 2 * n, ROWS):
            rows = pl.ds(start, ROWS)
            query = qkv[rows, cols_at(i * PAIR, PAIR)] * SCALE
            outs = []
            total_lse = lse[rows, :]
            for side, (own, some_keys, some_values) in enumerate(sides):
                scores = mm_nt(jnp.where(own, query, mq[rows, :]), some_keys)
                top = jnp.max(scores, axis=1, keepdims=True)
                expo = jnp.exp(scores - top).astype(bf16)
                mixed = mm(expo, some_values)
                total = pltpu.roll(mixed, DH, 1)
                outs.append(mixed / total)
                sum_all = jnp.where(own, total, mixed)
                total_lse = jnp.where(lanes == 2 * i + side, top + jnp.log(sum_all), total_lse)
            lse[rows, :] = total_lse
            heads[rows, cols_at(i * PAIR, PAIR)] = jnp.where(left, outs[0], outs[1]).astype(bf16)

        @pl.when(i == 0)
        def _():
            g_attn.forward_one()

        @pl.when(i == 1)
        def _():
            g_attn.forward_two()

        @pl.when(i == 3)
        def _():
            g_up.forward_one()

        @pl.when(i == 5)
        def _():
            g_up.forward_two()

    g_attn.ready()

    @pl.loop(0, 2 * n // ROWS)
    def _(i):
        rows = rows_at(i * ROWS, ROWS)
        resid = x[rows, :].astype(f32) + mm(heads[rows, :], proj[...]) + vecs[2:3, :]
        some, scale = normalize(resid)
        normed[rows, :] = some
        inverse[rows, :] = jnp.broadcast_to(scale, (ROWS, PAIR))
        hidden[rows, :] = (some * vecs[3:4, :] + vecs[4:5, :]).astype(bf16)

    g_up.ready()
    g_down.forward_one()

    @pl.loop(0, up.shape[1] // tile)
    def _(i):
        cols = cols_at(i * tile, tile)
        pre = mm(hidden[...], up[:, cols]) + vec_up[:, cols]
        value, rate = gelu_parts(pre)
        active[:, cols] = value.astype(bf16)
        bend[:, cols] = rate.astype(bf16)

        @pl.when(i == 6)
        def _():
            g_down.forward_two()

    g_down.ready()
    s_away.wait_recv()
    s_near.wait()
    sums[...] = jnp.zeros_like(sums)

    @pl.loop(0, 2 * n // ROWS)
    def _(i):
        rows = rows_at(i * ROWS, ROWS)
        resid = mm(active[rows, :], down[...]) + vecs[5:6, :]
        resid = resid + (normed[rows, :] * vecs[3:4, :] + vecs[4:5, :])
        some, scale = normalize(resid)
        layer[rows, :] = (some * vecs[6:7, :] + vecs[7:8, :]).astype(bf16)
        grad = slope[rows, :].astype(f32) * inside(i * ROWS, ROWS)
        back = norm_back(grad, some, scale, vecs[6:7, :])
        low_back = back.astype(bf16)
        second[rows, :] = back
        branch[rows, :] = low_back
        sums[5:6, :] += jnp.sum(low_back.astype(f32), axis=0, keepdims=True)
        sums[6:7, :] += jnp.sum(grad * some, axis=0, keepdims=True)
        sums[7:8, :] += jnp.sum(grad, axis=0, keepdims=True)

    @pl.loop(0, up.shape[1] // tile)
    def _(i):
        cols = cols_at(i * tile, tile)
        rate = bend[:, cols].astype(f32)
        low_pre = (mm_nt(branch[...], down[rows_at(i * tile, tile), :]) * rate).astype(bf16)
        bend[:, cols] = low_pre
        sums_up[:, cols] = jnp.sum(low_pre.astype(f32), axis=0, keepdims=True)

    outs = [
        copies.near(a, b)
        for a, b in (
            (x, o_x),
            (three, o_three),
            (proj, o_attn),
            (up, o_up),
            (qkv, o_qkv),
            (heads, o_heads),
            (lse, o_lse),
            (normed, o_normed),
            (inverse, o_inverse),
            (hidden, o_hidden),
            (active, o_active),
            (branch, o_branch),
            (bend, o_pre),
            (second, o_second),
            (layer, o_layer),
            (sums, o_sums),
            (sums_up, o_sums_up),
        )
    ]
    for copy in outs:
        copy.start()
    for copy in outs:
        copy.wait()
    for part in (g_query, g_key, g_value, g_attn, g_up, g_down):
        part.finish()
    for copy in (vec_away, x_away, s_away):
        copy.wait_send()


def run_forward(tokens, cotangent, seq, vectors, weights):
    n = weights[0].shape[0]
    count, wide = 2 * n, weights[4].shape[1]
    kinds = [
        ((count, D), bf16),
        ((D, 3 * D), bf16),
        ((D, D), bf16),
        ((D, wide), bf16),
        ((count, 3 * D), bf16),
        ((count, D), bf16),
        ((count, PAIR), f32),
        ((count, D), f32),
        ((count, PAIR), f32),
        ((count, D), bf16),
        ((count, wide), bf16),
        ((count, D), bf16),
        ((count, wide), bf16),
        ((count, D), f32),
        ((count, D), bf16),
        ((16, D), f32),
        ((1, wide), f32),
    ]
    scratch = [
        ((count, D), bf16),
        ((count, D), bf16),
        ((D, 3 * D), bf16),
        ((D, D), bf16),
        ((D, wide), bf16),
        ((wide, D), bf16),
        ((2, 16, n), bf16),
        ((16, D), f32),
        ((1, wide), f32),
        ((count, 3 * D), bf16),
        ((count, D), bf16),
        ((count, PAIR), f32),
        ((count, PAIR), bf16),
        ((count, PAIR), bf16),
        ((count, D), f32),
        ((count, PAIR), f32),
        ((count, D), bf16),
        ((count, wide), bf16),
        ((count, wide), bf16),
        ((count, D), bf16),
        ((count, D), f32),
        ((count, D), bf16),
        ((16, D), f32),
        ((1, wide), f32),
    ]
    anywhere = pl.BlockSpec(memory_space=pl.ANY)
    return pl.pallas_call(
        forward_kernel,
        out_shape=[jax.ShapeDtypeStruct(*kind) for kind in kinds],
        in_specs=[anywhere, anywhere, pl.BlockSpec(memory_space=pltpu.SMEM)] + [anywhere] * 7,
        out_specs=[anywhere] * len(kinds),
        scratch_shapes=[pltpu.VMEM(*kind) for kind in scratch]
        + [pltpu.SemaphoreType.DMA((64,)), pltpu.SemaphoreType.DMA((64,))],
        compiler_params=pltpu.CompilerParams(
            collective_id=0, has_side_effects=True, vmem_limit_bytes=66 * 1024 * 1024 - 3 * 1024 * 1024
        ),
        name="encoder_forward",
    )(tokens, cotangent, seq, vectors, *weights)

def general_body(
    tokens,
    cotangent,
    seq_lengths,
    w_query,
    b_query,
    w_key,
    w_value,
    b_value,
    w_attn,
    b_attn,
    norm_gain,
    norm_bias,
    w_up,
    b_up,
    w_down,
    b_down,
    out_gain,
    out_bias,
):
    at = Places()
    shards = at.shards
    micro, slots = tokens.shape[0], tokens.shape[1]
    span = shards // micro
    count = micro * slots
    x = spread(at, tokens)
    w_three = gather_rows(at, jnp.concatenate([w_query, w_key, w_value], axis=1))
    part = w_query.shape[0]
    wide = b_up.shape[0] // part
    vectors = jnp.concatenate(
        [
            jnp.stack(
                [b_query, b_value, b_attn, norm_gain, norm_bias, b_down, out_gain, out_bias]
            ),
            b_up.reshape(wide, part),
            jnp.zeros((16 - 8 - wide, part), bf16),
        ],
        axis=0,
    )
    table = put(jnp.zeros((shards,) + vectors.shape, bf16), vectors[None], at.shard)
    for step in range(1, shards):
        there = swap(vectors, "shard", shards, lambda i: (i + shards - step) % shards)
        table = put(table, there[None], (at.shard + step) % shards)
    table = table.astype(f32)
    (c_query, c_value, c_attn, c_gain, c_bias, c_down, c_out_gain, c_out_bias) = [
        table[:, i].reshape(1, D) for i in range(8)
    ]
    c_up = table[:, 8 : 8 + wide].reshape(1, D * wide)
    w_proj = gather_rows(at, w_attn)
    full_up = gather_rows(at, w_up)
    full_down = gather_rows(at, w_down)
    slope_in = spread(at, cotangent)

    group = slots * shards
    which, inner = at.shard // span, at.shard % span
    row = lax.dynamic_index_in_dim(seq_lengths[:, 0], which, 0, False)
    ids = segment_ids(row, group)

    def ids_of(device):
        parts = []
        for step in range(micro):
            source = micro * device + (which + micro - step) % micro
            parts.append(lax.dynamic_slice_in_dim(ids, source * slots, slots))
        return jnp.concatenate(parts)

    query_ids = ids_of(inner)
    nseq = seq_lengths.shape[-1] - 1
    valid = (query_ids < nseq).astype(f32)[:, None]
    three = mm(x, w_three) + jnp.concatenate([c_query, jnp.zeros_like(c_query), c_value], axis=1)
    three = three.astype(bf16)
    base = D // PAIR
    offsets = (base, 2 * base)
    key_array = three
    key_ids = [query_ids]
    if span > 1:
        offsets = (0, base)
        own = three[:, D:]
        parts = [own]
        for step in range(1, span):
            moves = [(i, i // span * span + (i + span - step) % span) for i in range(shards)]
            parts.append(lax.ppermute(own, "shard", moves))
            key_ids.append(ids_of((inner + step) % span))
        key_array = jnp.concatenate(parts, axis=0)
    mq, _ = mask_columns(query_ids)
    _, mk = mask_columns(jnp.concatenate(key_ids))
    attn, lse = attention_forward(three, key_array, offsets, mq, mk)

    normed_one, inverse_one = normalize(x.astype(f32) + mm(attn, w_proj) + c_attn)
    hidden = normed_one * c_gain + c_bias
    hidden_low = hidden.astype(bf16)
    pre = mm(hidden_low, full_up) + c_up
    lower = 0.5 * (1.0 + lax.erf(pre * 0.7071067811865476))
    active = (pre * lower).astype(bf16)
    density = jnp.exp(-0.5 * pre * pre) * 0.3989422804014327
    gelu_slope = lower + pre * density
    normed_two, inverse_two = normalize(hidden + mm(active, full_down) + c_down)
    layer = (normed_two * c_out_gain + c_out_bias).astype(bf16)
    grad_out = slope_in.astype(f32) * valid
    d_out_gain = jnp.sum(grad_out * normed_two, axis=0)
    d_out_bias = jnp.sum(grad_out, axis=0)
    grad_second = norm_back(grad_out, normed_two, inverse_two, c_out_gain)
    grad_branch = grad_second.astype(bf16)
    d_down = jnp.sum(grad_branch.astype(f32), axis=0)
    g_down = mm_tn(active, grad_branch)
    grad_pre = (mm_nt(grad_branch, full_down) * gelu_slope).astype(bf16)
    d_up = jnp.sum(grad_pre.astype(f32), axis=0)
    g_up = mm_tn(hidden_low, grad_pre)
    grad_hidden = mm_nt(grad_pre, full_up) + grad_second
    d_gain = jnp.sum(grad_hidden * normed_one, axis=0)
    d_bias = jnp.sum(grad_hidden, axis=0)
    grad_first = norm_back(grad_hidden, normed_one, inverse_one, c_gain)
    grad_proj = grad_first.astype(bf16)
    d_attn = jnp.sum(grad_proj.astype(f32), axis=0)
    g_attn = mm_tn(attn, grad_proj)
    grad_attn = mm_nt(grad_proj, w_proj).astype(bf16)
    dq, dk, dv = attention_backward(three, key_array, offsets, mq, mk, attn, lse, grad_attn)
    if span > 1:
        both = jnp.concatenate([dk, dv], axis=1)
        total = both[:count].astype(f32)
        for step in range(1, span):
            moves = [(i, i // span * span + (i + step) % span) for i in range(shards)]
            away = both[step * count : (step + 1) * count]
            total = total + lax.ppermute(away, "shard", moves).astype(f32)
        dk, dv = total[:, :D].astype(bf16), total[:, D:].astype(bf16)
    d_three = jnp.concatenate([dq, dk, dv], axis=1)
    d_query = jnp.sum(dq.astype(f32), axis=0)
    d_value = jnp.sum(dv.astype(f32), axis=0)
    g_three = mm_tn(x, d_three)
    back = (grad_first + mm_nt(d_three, w_three)).astype(bf16)

    sums = jnp.concatenate(
        [
            jnp.stack([d_query, d_value, d_attn, d_gain, d_bias, d_down, d_out_gain, d_out_bias]).reshape(
                8, shards, part
            ),
            d_up.reshape(shards, wide, part).transpose(1, 0, 2),
            jnp.zeros((PAIR - 8 - wide, shards, part), f32),
        ],
        axis=0,
    )
    sums = sums.reshape(PAIR, D).T
    r_down = reduce_rows(at, g_down)
    r_up = reduce_rows(at, g_up)
    r_attn = reduce_rows(at, g_attn)
    r_three = reduce_rows(at, jnp.concatenate([g_three, sums], axis=1))
    small = r_three[:, 3 * D :].T
    return (
        collect(at, layer, micro),
        collect(at, back, micro),
        r_three[:, :D],
        small[0],
        r_three[:, D : 2 * D],
        r_three[:, 2 * D : 3 * D],
        small[1],
        r_attn,
        small[2],
        small[3],
        small[4],
        r_up,
        small[8 : 8 + wide].reshape(wide * part),
        r_down,
        small[5],
        small[6],
        small[7],
    )


def body(tokens, cotangent, seq_lengths, *weights):
    shards, micro = lax.axis_size("shard"), tokens.shape[0]
    reps = lax.axis_size("rep")
    if shards != 2 or micro != 2 or reps % 4:
        return general_body(tokens, cotangent, seq_lengths, *weights)
    (
        w_query,
        b_query,
        w_key,
        w_value,
        b_value,
        w_attn,
        b_attn,
        norm_gain,
        norm_bias,
        w_up,
        b_up,
        w_down,
        b_down,
        out_gain,
        out_bias,
    ) = weights
    at = Places()
    part = w_query.shape[0]
    wide = b_up.shape[0] // part
    vectors = jnp.concatenate(
        [b_query, b_value, b_attn, norm_gain, norm_bias, b_down, out_gain, out_bias, b_up]
        + [jnp.zeros(((8 - wide) * part,), bf16)]
    ).reshape(16, part)
    (
        x,
        w_three,
        w_proj,
        full_up,
        three,
        attn,
        lse,
        normed_one,
        inverse_one,
        hidden_low,
        active,
        grad_branch,
        grad_pre,
        grad_second,
        layer,
        sums,
        d_up,
    ) = run_forward(
        tokens, cotangent, seq_lengths[:, 0], vectors, (w_query, w_key, w_value, w_attn, w_up, w_down)
    )
    slots = tokens.shape[1]
    ids = segment_ids(lax.dynamic_index_in_dim(seq_lengths[:, 0], at.shard, 0, False), 2 * slots)
    ids = jnp.roll(ids, -at.shard * slots)
    mq, mk = mask_columns(ids)
    base = D // PAIR
    offsets = (base, 2 * base)
    c_gain = None
    table = put(jnp.zeros((2, part), bf16), norm_gain[None], at.shard)
    there = swap(norm_gain[None], "shard", 2, lambda i: 1 - i)
    c_gain = put(table, there, 1 - at.shard).reshape(1, D).astype(f32)
    inverse_one = inverse_one[:, :1]
    lse = jnp.repeat(lse[:, :H], DH, axis=1)
    g_down = mm_tn(active, grad_branch)
    g_up = mm_tn(hidden_low, grad_pre)
    grad_hidden = mm_nt(grad_pre, full_up) + grad_second
    d_gain = jnp.sum(grad_hidden * normed_one, axis=0)
    d_bias = jnp.sum(grad_hidden, axis=0)
    grad_first = norm_back(grad_hidden, normed_one, inverse_one, c_gain)
    grad_proj = grad_first.astype(bf16)
    d_attn = jnp.sum(grad_proj.astype(f32), axis=0)
    g_attn = mm_tn(attn, grad_proj)
    grad_attn = mm_nt(grad_proj, w_proj).astype(bf16)
    dq, dk, dv = attention_backward(three, three, offsets, mq, mk, attn, lse, grad_attn)
    d_three = jnp.concatenate([dq, dk, dv], axis=1)
    d_query = jnp.sum(dq.astype(f32), axis=0)
    d_value = jnp.sum(dv.astype(f32), axis=0)
    g_three = mm_tn(x, d_three)
    back = (grad_first + mm_nt(d_three, w_three)).astype(bf16)
    sums = jnp.concatenate(
        [
            jnp.stack([d_query, d_value, d_attn, d_gain, d_bias, sums[5], sums[6], sums[7]]).reshape(
                8, shards, part
            ),
            d_up.reshape(shards, wide, part).transpose(1, 0, 2),
            jnp.zeros((PAIR - 8 - wide, shards, part), f32),
        ],
        axis=0,
    )
    sums = sums.reshape(PAIR, D).T
    r_down = reduce_rows(at, g_down)
    r_up = reduce_rows(at, g_up)
    r_attn = reduce_rows(at, g_attn)
    r_three = reduce_rows(at, jnp.concatenate([g_three, sums], axis=1))
    small = r_three[:, 3 * D :].T
    return (
        collect(at, layer, micro),
        collect(at, back, micro),
        r_three[:, :D],
        small[0],
        r_three[:, D : 2 * D],
        r_three[:, 2 * D : 3 * D],
        small[1],
        r_attn,
        small[2],
        small[3],
        small[4],
        r_up,
        small[8 : 8 + wide].reshape(wide * part),
        r_down,
        small[5],
        small[6],
        small[7],
    )


def solution(mesh):
    rows, vector = P("shard", None), P("shard")
    tokens = P(None, ("rep", "shard"), None)
    weights = (rows, vector, rows, rows, vector, rows, vector, vector, vector)
    weights += (rows, vector, rows, vector, vector, vector)
    return jax.shard_map(
        body,
        mesh=mesh,
        in_specs=(tokens, tokens, P(None, "rep", None)) + weights,
        out_specs=(tokens, tokens) + weights,
        check_vma=False,
    )
```

```python
import functools

import jax
import jax.numpy as jnp
from jax import lax
from jax.experimental import pallas as pl
from jax.experimental.pallas import tpu as pltpu
from jax.sharding import PartitionSpec as P

D = 768
H = 12
DH = 64
PAIR = 2 * DH
EPS = 1e-12
BIG = 1e30
SCALE = DH ** (-0.5)
ROWS = 256
f32 = jnp.float32
bf16 = jnp.bfloat16


def mm(left, right):
    return jnp.dot(left, right, preferred_element_type=f32)


def mm_nt(left, right):
    return lax.dot_general(left, right, (((1,), (1,)), ((), ())), preferred_element_type=f32)


def mm_tn(left, right):
    return lax.dot_general(left, right, (((0,), (0,)), ((), ())), preferred_element_type=f32)


def segment_ids(row, count):
    bounds = jnp.cumsum(row[:-1])
    places = jnp.arange(count, dtype=jnp.int32)
    return jnp.sum((places[:, None] >= bounds[None, :]).astype(jnp.int32), axis=1)


def mask_columns(ids):
    first = (ids == 0).astype(f32)[:, None]
    other = 1.0 - first
    lane = lax.broadcasted_iota(jnp.int32, (1, PAIR), 1) % DH
    on_query = jnp.where(lane == 0, -BIG * first, jnp.where(lane == 1, -BIG * other, 0.0))
    on_key = jnp.where(lane == 0, other, jnp.where(lane == 1, first, 0.0))
    return on_query.astype(bf16), on_key.astype(bf16)


def forward_heads(q_ref, k_ref, v_ref, mq_ref, mk_ref, attn_ref, lse_ref):
    lane = lax.broadcasted_iota(jnp.int32, (1, PAIR), 1)
    low = lane < DH
    keys, values, mk = k_ref[...], v_ref[...], mk_ref[...]
    one = jnp.ones_like(values)
    sides = []
    for own in (low, jnp.logical_not(low)):
        sides.append((own, jnp.where(own, keys, mk), jnp.where(own, values, one)))
    count = q_ref.shape[0]
    block = min(ROWS, count)
    for start in range(0, count, block):
        rows = pl.ds(start, block)
        query, mq = q_ref[rows, :] * SCALE, mq_ref[rows, :]
        outs = []
        for own, some_keys, some_values in sides:
            scores = mm_nt(jnp.where(own, query, mq), some_keys)
            top = jnp.max(scores, axis=1, keepdims=True)
            expo = jnp.exp(scores - top).astype(bf16)
            mixed = mm(expo, some_values)
            total = pltpu.roll(mixed, DH, 1)
            outs.append((mixed / total, top + jnp.log(total)))
        attn_ref[rows, :] = jnp.where(low, outs[0][0], outs[1][0]).astype(bf16)
        lse_ref[rows, :] = jnp.where(low, outs[0][1], outs[1][1])


def three_parts(value):
    first = value.astype(bf16).astype(f32)
    rest = value - first
    second = rest.astype(bf16).astype(f32)
    return first, second, rest - second


def backward_heads(
    q_ref, k_ref, v_ref, mq_ref, mk_ref, attn_ref, lse_ref, grad_ref, dq_ref, dk_ref, dv_ref
):
    lane = lax.broadcasted_iota(jnp.int32, (1, PAIR), 1)
    place = lane % DH
    low = lane < DH
    query, mq, grad = q_ref[...] * SCALE, mq_ref[...], grad_ref[...]
    product = grad.astype(f32) * attn_ref[...].astype(f32)
    lse = three_parts(-pltpu.roll(lse_ref[...], DH, 1))
    count_keys = k_ref.shape[0]
    block = min(ROWS, count_keys)
    sides = []
    for own in (low, jnp.logical_not(low)):
        delta = three_parts(-jnp.sum(jnp.where(own, product, 0.0), axis=1, keepdims=True))
        more = jnp.where(place == 2, lse[0], jnp.where(place == 3, lse[1], lse[2]))
        more = jnp.where(place < 2, mq, jnp.where(place < 5, more, 0.0).astype(bf16))
        some_query = jnp.where(own, query, more)
        more = jnp.where(place == 0, delta[0], jnp.where(place == 1, delta[1], delta[2]))
        some_grad = jnp.where(own, grad, jnp.where(place < 3, more, 0.0).astype(bf16))
        sides.append((own, some_query, some_grad, None))
    totals = [None, None]
    for start in range(0, count_keys, block):
        rows = pl.ds(start, block)
        keys, values, mk = k_ref[rows, :], v_ref[rows, :], mk_ref[rows, :]
        ones = jnp.ones_like(values)
        zeros = jnp.zeros_like(values)
        more_keys = jnp.where(place < 2, mk, jnp.where(place < 5, ones, zeros))
        more_values = jnp.where(place < 3, ones, zeros)
        parts = []
        for side in range(2):
            own, some_query, some_grad, _ = sides[side]
            some_keys = jnp.where(own, keys, more_keys)
            some_values = jnp.where(own, values, more_values)
            probs = jnp.exp(mm_nt(some_keys, some_query))
            slope = (probs * mm_nt(some_values, some_grad)).astype(bf16)
            dv = mm(probs.astype(bf16), some_grad)
            dk = mm(slope, some_query)
            dq = mm_tn(slope, some_keys)
            totals[side] = dq if totals[side] is None else totals[side] + dq
            parts.append((dk, dv))
        dk_ref[rows, :] = jnp.where(low, parts[0][0], parts[1][0]).astype(bf16)
        dv_ref[rows, :] = jnp.where(low, parts[0][1], parts[1][1]).astype(bf16)
    dq_ref[...] = (jnp.where(low, totals[0], totals[1]) * SCALE).astype(bf16)


def head_block(rows, offset):
    return pl.BlockSpec((rows, PAIR), lambda i: (0, i + offset))


def fixed_block(rows):
    return pl.BlockSpec((rows, PAIR), lambda i: (0, 0))


def attention_forward(query_array, key_array, offsets, mq, mk):
    count, keys = query_array.shape[0], key_array.shape[0]
    pairs = H * DH // PAIR
    return pl.pallas_call(
        forward_heads,
        grid=(pairs,),
        out_shape=(
            jax.ShapeDtypeStruct((count, D), bf16),
            jax.ShapeDtypeStruct((count, D), f32),
        ),
        in_specs=[
            head_block(count, 0),
            head_block(keys, offsets[0]),
            head_block(keys, offsets[1]),
            fixed_block(count),
            fixed_block(keys),
        ],
        out_specs=(head_block(count, 0), head_block(count, 0)),
        cost_estimate=pl.CostEstimate(
            flops=16 * count * keys * D, bytes_accessed=8 * (count + keys) * D, transcendentals=count * keys * H
        ),
        name="attention_forward",
    )(query_array, key_array, key_array, mq, mk)


def attention_backward(query_array, key_array, offsets, mq, mk, attn, lse, grad):
    count, keys = query_array.shape[0], key_array.shape[0]
    pairs = H * DH // PAIR
    return pl.pallas_call(
        backward_heads,
        grid=(pairs,),
        out_shape=(
            jax.ShapeDtypeStruct((count, D), bf16),
            jax.ShapeDtypeStruct((keys, D), bf16),
            jax.ShapeDtypeStruct((keys, D), bf16),
        ),
        in_specs=[
            head_block(count, 0),
            head_block(keys, offsets[0]),
            head_block(keys, offsets[1]),
            fixed_block(count),
            fixed_block(keys),
            head_block(count, 0),
            head_block(count, 0),
            head_block(count, 0),
        ],
        out_specs=(head_block(count, 0), head_block(keys, 0), head_block(keys, 0)),
        cost_estimate=pl.CostEstimate(
            flops=40 * count * keys * D, bytes_accessed=16 * (count + keys) * D, transcendentals=count * keys * H
        ),
        name="attention_backward",
    )(query_array, key_array, key_array, mq, mk, attn, lse, grad)


def normalize(rows):
    mean = jnp.mean(rows, axis=-1, keepdims=True)
    centered = rows - mean
    inverse = lax.rsqrt(jnp.mean(centered * centered, axis=-1, keepdims=True) + EPS)
    return centered * inverse, inverse


def norm_back(grad, normed, inverse, gain):
    scaled = grad * gain
    first = jnp.mean(scaled, axis=-1, keepdims=True)
    second = jnp.mean(scaled * normed, axis=-1, keepdims=True)
    return inverse * (scaled - first - normed * second)


def swap(value, axis, size, move):
    return lax.ppermute(value, axis, [(i, move(i)) for i in range(size)])


def put(buffer, value, index, axis=0):
    return lax.dynamic_update_slice_in_dim(buffer, value, index * value.shape[axis], axis)


def pick(value, index, parts, axis=0):
    size = value.shape[axis] // parts
    return lax.dynamic_slice_in_dim(value, index * size, size, axis)


class Places:
    def __init__(self):
        self.reps = lax.axis_size("rep")
        self.shards = lax.axis_size("shard")
        self.rep = lax.axis_index("rep")
        self.shard = lax.axis_index("shard")
        self.core = self.rep % 2


def gather_rows(at, own):
    half = own.shape[0] // 2
    out = jnp.zeros((at.shards * own.shape[0],) + own.shape[1:], own.dtype)
    out = put(out, own, at.shard)
    mine = pick(own, at.core, 2)
    for step in range(1, at.shards):
        there = swap(mine, "shard", at.shards, lambda i: (i + at.shards - step) % at.shards)
        other = swap(there, "rep", at.reps, lambda i: i ^ 1)
        block = (at.shard + step) % at.shards * 2
        out = put(out, there, block + at.core)
        out = put(out, other, block + 1 - at.core)
    return out


def reduce_rows(at, grad):
    shards, columns = at.shards, grad.shape[1]
    rows = grad.shape[0] // shards
    value = grad.reshape(shards * 2, rows // 2, columns)
    value = grad.reshape(shards, 2, rows // 2, columns)
    mine = lax.dynamic_index_in_dim(value, at.core, 1, False)
    away = lax.dynamic_index_in_dim(value, 1 - at.core, 1, False).astype(bf16)
    value = mine.astype(f32) + swap(away, "rep", at.reps, lambda i: i ^ 1).astype(f32)
    total = lax.dynamic_index_in_dim(value, at.shard, 0, False)
    for step in range(1, shards):
        away = lax.dynamic_index_in_dim(value, (at.shard + step) % shards, 0, False).astype(bf16)
        total = total + swap(away, "shard", shards, lambda i: (i + step) % shards).astype(f32)
    stages = []
    bit = 2
    while bit < at.reps:
        axis = 0 if total.shape[0] % 32 == 0 else 1
        stages.append((bit, axis))
        up = (at.rep // bit) % 2
        mine, away = pick(total, up, 2, axis), pick(total, 1 - up, 2, axis).astype(bf16)
        move = functools.partial(lambda b, i: i ^ b, bit)
        total = mine + swap(away, "rep", at.reps, move).astype(f32)
        bit *= 2
    total = total.astype(bf16)
    for bit, axis in reversed(stages):
        up = (at.rep // bit) % 2
        move = functools.partial(lambda b, i: i ^ b, bit)
        other = swap(total, "rep", at.reps, move)
        shape = list(total.shape)
        shape[axis] *= 2
        both = jnp.zeros(shape, bf16)
        total = put(put(both, total, up, axis), other, 1 - up, axis)
    other = swap(total, "rep", at.reps, lambda i: i ^ 1)
    first = jnp.where(at.core == 0, total, other)
    second = jnp.where(at.core == 0, other, total)
    return jnp.concatenate([first, second], axis=0).astype(f32)


def spread(at, value):
    micro, shards = value.shape[0], at.shards
    parts = []
    for step in range(micro):
        moves = [(i, (i + step) % micro * (shards // micro) + i // micro) for i in range(shards)]
        part = lax.dynamic_index_in_dim(value, (at.shard + step) % micro, 0, False)
        if any(a != b for a, b in moves):
            part = lax.ppermute(part, "shard", moves)
        parts.append(part)
    return jnp.concatenate(parts, axis=0)


def collect(at, value, micro):
    shards = at.shards
    slots = value.shape[0] // micro
    out = jnp.zeros((micro, slots) + value.shape[1:], value.dtype)
    for step in range(micro):
        moves = [((i + step) % micro * (shards // micro) + i // micro, i) for i in range(shards)]
        part = value[step * slots : (step + 1) * slots]
        if any(a != b for a, b in moves):
            part = lax.ppermute(part, "shard", moves)
        out = lax.dynamic_update_index_in_dim(out, part, (at.shard + step) % micro, 0)
    return out


def rows_at(start, size):
    return pl.ds(pl.multiple_of(start, 16), size)


def cols_at(start, size):
    return pl.ds(pl.multiple_of(start, PAIR), size)


class Here:
    def __init__(self):
        self.rep = lax.axis_index("rep")
        self.y = lax.axis_index("shard")
        self.core = lax.rem(self.rep, 2)
        self.x = lax.rem(lax.div(self.rep, 2), 2)

    def across(self, bit):
        up = lax.rem(lax.div(self.rep, bit), 2)
        return {"rep": self.rep + bit * (1 - 2 * up)}

    def over(self):
        return {"shard": 1 - self.y}


class Copies:
    def __init__(self, send, recv):
        self.send, self.recv, self.used, self.open = send, recv, 0, []

    def away(self, source, target, peer):
        k = self.used
        self.used += 1
        copy = pltpu.make_async_remote_copy(
            src_ref=source,
            dst_ref=target,
            send_sem=self.send.at[k],
            recv_sem=self.recv.at[k],
            device_id=peer,
            device_id_type=pl.DeviceIdType.MESH,
        )
        return copy

    def near(self, source, target):
        k = self.used
        self.used += 1
        return pltpu.make_async_copy(source, target, self.recv.at[k])


def greet(peers):
    barrier = pltpu.get_barrier_semaphore()
    for peer in peers:
        pl.semaphore_signal(barrier, inc=1, device_id=peer, device_id_type=pl.DeviceIdType.MESH)
    pl.semaphore_wait(barrier, len(peers))


class Gathered:
    def __init__(self, here, copies, own, full, cols):
        n = own.shape[0]
        h = n // 4
        q = 2 * here.x + here.core
        across = 2 * (1 - here.x) + here.core
        mine, other = here.y * n, (1 - here.y) * n

        def at(start, size):
            return full.at[rows_at(start, size), cols]

        self.local = copies.near(own, at(mine, n))
        self.over = copies.away(own.at[rows_at(q * h, h), :], at(mine + q * h, h), here.over())
        first, second = at(other + q * h, h), at(other + across * h, h)
        self.side = copies.away(first, first, here.across(2))
        self.core_one = copies.away(first, first, here.across(1))
        self.core_two = copies.away(second, second, here.across(1))

    def start(self):
        self.over.start()
        self.local.start()

    def forward_one(self):
        self.over.wait_recv()
        self.side.start()
        self.core_one.start()

    def forward_two(self):
        self.side.wait_recv()
        self.core_two.start()

    def ready(self):
        self.local.wait()
        self.core_one.wait_recv()
        self.core_two.wait_recv()

    def finish(self):
        for copy in (self.over, self.side, self.core_one, self.core_two):
            copy.wait_send()


def gelu_parts(pre):
    lower = 0.5 * (1.0 + lax.erf(pre * 0.7071067811865476))
    density = jnp.exp(-0.5 * pre * pre) * 0.3989422804014327
    return pre * lower, lower + pre * density


UNITS = 12


class Units:
    def __init__(self, here, reps, send, recv, swap_buffer, own, far, near, done, result):
        self.here, self.send, self.recv = here, send, recv
        self.swap_buffer, self.own, self.far, self.near, self.done = swap_buffer, own, far, near, done
        self.result = result
        self.n = own.shape[2]
        self.bits = []
        bit = 2
        while bit < reps:
            self.bits.append(bit)
            bit *= 2
        self.stages = 3 + 2 * len(self.bits)

    def copy(self, stage, u, source, target, peer):
        return pltpu.make_async_remote_copy(
            src_ref=source,
            dst_ref=target,
            send_sem=self.send.at[stage, u],
            recv_sem=self.recv.at[stage, u],
            device_id=peer,
            device_id_type=pl.DeviceIdType.MESH,
        )

    def slot(self, u, side):
        n = self.n
        return self.swap_buffer.at[rows_at(lax.rem(u, 4) * 2 * n, 2 * n), pl.ds(side * n, n)]

    def rows_of(self, level):
        size, start = self.n, 0
        for bit in self.bits[:level]:
            size //= 2
            start = start + lax.rem(lax.div(self.here.rep, bit), 2) * size
        return start, size

    def core_copy(self, u):
        return self.copy(0, u, self.slot(u, 0), self.slot(u, 1), self.here.across(1))

    def y_copy(self, u):
        return self.copy(1, u, self.own.at[u, 1 - self.here.y], self.far.at[u], self.here.over())

    def down_copy(self, k, u):
        start, size = self.rows_of(k)
        half = size // 2
        up = lax.rem(lax.div(self.here.rep, self.bits[k]), 2)
        rows = rows_at(start + (1 - up) * half, half)
        return self.copy(
            2 + k, u, self.own.at[u, self.here.y, rows, :], self.near[k].at[u], self.here.across(self.bits[k])
        )

    def up_copy(self, k, u):
        level = len(self.bits) - k
        start, size = self.rows_of(level)
        bit = self.bits[level - 1] if level else 1
        piece = self.done.at[u, self.here.core, rows_at(start, size), :]
        return self.copy(2 + len(self.bits) + k, u, piece, piece, self.here.across(bit))

    def out_copy(self, u):
        return pltpu.make_async_copy(self.done.at[u], self.result.at[u], self.send.at[self.stages, u])

    def first_sum(self, u):
        n, y = self.n, self.here.y
        self.core_copy(u).wait_recv()
        for shard in (1 - y, y):
            rows = rows_at((lax.rem(u, 4) * 2 + shard) * n, n)
            theirs = self.swap_buffer[rows, pl.ds(n, n)].astype(f32)
            self.own[u, shard] = (self.own[u, shard].astype(f32) + theirs).astype(bf16)
            if shard is not y:
                self.y_copy(u).start()

    def stage(self, k, u):
        bits = len(self.bits)
        y = self.here.y
        if k == 0:
            self.y_copy(u).wait_recv()
            start, size = self.rows_of(0)
            arrived = self.far
        elif k <= bits:
            self.down_copy(k - 1, u).wait_recv()
            arrived = self.near[k - 1]
            start, size = self.rows_of(k)
        if k < bits:
            half = size // 2
            up = lax.rem(lax.div(self.here.rep, self.bits[k]), 2)
            for part in (1 - up, up):
                rows = rows_at(start + part * half, half)
                theirs = arrived[u, rows_at(part * half, half), :].astype(f32)
                self.own[u, y, rows, :] = (self.own[u, y, rows, :].astype(f32) + theirs).astype(bf16)
                if part is not up:
                    self.down_copy(k, u).start()
        elif k == bits:
            rows = rows_at(start, size)
            total = self.own[u, y, rows, :].astype(f32) + arrived[u].astype(f32)
            self.done[u, self.here.core, rows, :] = total.astype(bf16)
            self.up_copy(0, u).start()
        else:
            self.up_copy(k - bits - 1, u).wait_recv()
            if k <= 2 * bits:
                self.up_copy(k - bits, u).start()
            else:
                self.out_copy(u).start()

    def tick(self, t):
        for k in reversed(range(2 * len(self.bits) + 2)):
            u = t - k
            if isinstance(u, int):
                if 0 <= u < UNITS:
                    self.stage(k, u)
            else:
                pl.when(jnp.logical_and(u >= 0, u < UNITS))(functools.partial(self.stage, k, u))

    def finish(self):
        @pl.loop(0, UNITS)
        def _(u):
            @pl.when(u >= UNITS - 4)
            def _():
                self.core_copy(u).wait_send()

            self.y_copy(u).wait_send()
            for k in range(len(self.bits)):
                self.down_copy(k, u).wait_send()
            for k in range(len(self.bits) + 1):
                self.up_copy(k, u).wait_send()
            self.out_copy(u).wait()


def layer_kernel(
    tokens,
    cotangent,
    seq,
    vectors,
    w_query,
    w_key,
    w_value,
    w_attn,
    w_up,
    w_down,
    o_layer,
    o_back,
    o_grads,
    o_small,
    x,
    slope,
    three,
    proj,
    up,
    down,
    raw_vectors,
    vecs,
    vec_up,
    qkv,
    heads,
    lse,
    mq,
    mk,
    normed,
    inverse,
    hidden,
    active,
    bend,
    branch,
    second,
    layer,
    sums,
    sums_up,
    others,
    own,
    far,
    near_x,
    near_z,
    near_w,
    done,
    small,
    send,
    recv,
    unit_send,
    unit_recv,
    free,
):
    reps = lax.axis_size("rep")
    here = Here()
    copies = Copies(send, recv)
    n = w_query.shape[0]
    y = here.y
    near = (near_x, near_z, near_w)
    units = Units(here, reps, unit_send, unit_recv, down, own, far, near, done, o_grads)
    peers = [here.over(), here.across(1)] + [here.across(bit) for bit in units.bits]
    greet(peers)

    g_query = Gathered(here, copies, w_query, three, pl.ds(0, D))
    g_key = Gathered(here, copies, w_key, three, pl.ds(D, D))
    g_value = Gathered(here, copies, w_value, three, pl.ds(2 * D, D))
    g_attn = Gathered(here, copies, w_attn, proj, pl.ds(0, D))
    g_up = Gathered(here, copies, w_up, up, pl.ds(0, up.shape[1]))
    g_down = Gathered(here, copies, w_down, down, pl.ds(0, D))
    vec_away = copies.away(vectors, raw_vectors.at[y], here.over())
    vec_near = copies.near(vectors, raw_vectors.at[y])
    low, high = pl.ds(0, n), pl.ds(n, n)
    x_away = copies.away(tokens.at[1 - y], x.at[high, :], here.over())
    x_near = copies.near(tokens.at[y], x.at[low, :])
    s_away = copies.away(cotangent.at[1 - y], slope.at[high, :], here.over())
    s_near = copies.near(cotangent.at[y], slope.at[low, :])
    layer_away = copies.away(layer.at[high, :], o_layer.at[y], here.over())
    layer_near = copies.near(layer.at[low, :], o_layer.at[y])
    back_away = copies.away(hidden.at[high, :], o_back.at[y], here.over())
    back_near = copies.near(hidden.at[low, :], o_back.at[y])
    for part in (g_query, g_key, g_value):
        part.start()
    vec_away.start()
    vec_near.start()
    x_away.start()
    x_near.start()
    for part in (g_attn, g_up, g_down):
        part.start()
    s_away.start()
    s_near.start()

    length = seq[y, 0, 0]

    def inside(start, size):
        row = start + lax.broadcasted_iota(jnp.int32, (size, 1), 0)
        place = row + jnp.where(row < n, y * n, -y * n)
        return (place < length).astype(f32)

    first = inside(0, 2 * n)
    lane = lax.rem(lax.broadcasted_iota(jnp.int32, (1, PAIR), 1), DH)
    mq[...] = jnp.where(
        lane == 0, -BIG * first, jnp.where(lane == 1, -BIG * (1.0 - first), 0.0)
    ).astype(bf16)
    mk[...] = jnp.where(lane == 0, 1.0 - first, jnp.where(lane == 1, first, 0.0)).astype(bf16)
    sums[...] = jnp.zeros_like(sums)
    lse[...] = jnp.zeros_like(lse)

    for part in (g_query, g_key, g_value):
        part.forward_one()
    for part in (g_query, g_key, g_value):
        part.forward_two()
    vec_away.wait_recv()
    vec_near.wait()
    wide = up.shape[1] // (2 * n)
    for half in range(2):
        table = raw_vectors[half]
        vecs[:, half * n : (half + 1) * n] = table
        for i in range(wide):
            start = half * wide * n + i * n
            vec_up[:, start : start + n] = table[8 + i : 9 + i, :]
    for part in (g_query, g_key, g_value):
        part.ready()
    x_away.wait_recv()
    x_near.wait()

    tile = 256

    @pl.loop(0, 3 * D // tile)
    def _(i):
        cols = cols_at(i * tile, tile)
        which = lax.div(i, D // tile)
        inner = cols_at(lax.rem(i, D // tile) * tile, tile)
        bias = jnp.where(
            which == 0, vecs[0:1, inner], jnp.where(which == 2, vecs[1:2, inner], 0.0)
        )
        qkv[:, cols] = (mm(x[...], three[:, cols]) + bias).astype(bf16)

    lanes = lax.broadcasted_iota(jnp.int32, (1, PAIR), 1)
    left = lanes < DH
    pairs = H * DH // PAIR

    @pl.loop(0, pairs)
    def _(i):
        keys, values = qkv[:, cols_at(D + i * PAIR, PAIR)], qkv[:, cols_at(2 * D + i * PAIR, PAIR)]
        one = jnp.ones_like(values)
        sides = []
        for side in (left, jnp.logical_not(left)):
            sides.append((side, jnp.where(side, keys, mk[...]), jnp.where(side, values, one)))
        for start in range(0, 2 * n, ROWS):
            rows = pl.ds(start, ROWS)
            query = qkv[rows, cols_at(i * PAIR, PAIR)] * SCALE
            outs = []
            total_lse = lse[rows, :]
            for number, (side, some_keys, some_values) in enumerate(sides):
                scores = mm_nt(jnp.where(side, query, mq[rows, :]), some_keys)
                top = jnp.max(scores, axis=1, keepdims=True)
                expo = jnp.exp(scores - top).astype(bf16)
                mixed = mm(expo, some_values)
                total = pltpu.roll(mixed, DH, 1)
                outs.append(mixed / total)
                sum_all = jnp.where(side, total, mixed)
                total_lse = jnp.where(lanes == 2 * i + number, top + jnp.log(sum_all), total_lse)
            lse[rows, :] = total_lse
            heads[rows, cols_at(i * PAIR, PAIR)] = jnp.where(left, outs[0], outs[1]).astype(bf16)

        @pl.when(i == 0)
        def _():
            g_attn.forward_one()

        @pl.when(i == 1)
        def _():
            g_attn.forward_two()

        @pl.when(i == 3)
        def _():
            g_up.forward_one()

        @pl.when(i == 5)
        def _():
            g_up.forward_two()

    g_attn.ready()

    @pl.loop(0, 2 * n // ROWS)
    def _(i):
        rows = rows_at(i * ROWS, ROWS)
        resid = x[rows, :].astype(f32) + mm(heads[rows, :], proj[...]) + vecs[2:3, :]
        some, scale = normalize(resid)
        normed[rows, :] = some
        inverse[rows, :] = jnp.broadcast_to(scale, (ROWS, PAIR))
        hidden[rows, :] = (some * vecs[3:4, :] + vecs[4:5, :]).astype(bf16)

    g_up.ready()
    g_down.forward_one()

    @pl.loop(0, up.shape[1] // tile)
    def _(i):
        cols = cols_at(i * tile, tile)
        pre = mm(hidden[...], up[:, cols]) + vec_up[:, cols]
        value, rate = gelu_parts(pre)
        active[:, cols] = value.astype(bf16)
        bend[:, cols] = rate.astype(bf16)

        @pl.when(i == 6)
        def _():
            g_down.forward_two()

    g_down.ready()
    s_away.wait_recv()
    s_near.wait()

    @pl.loop(0, 2 * n // ROWS)
    def _(i):
        rows = rows_at(i * ROWS, ROWS)
        resid = mm(active[rows, :], down[...]) + vecs[5:6, :]
        resid = resid + (normed[rows, :] * vecs[3:4, :] + vecs[4:5, :])
        some, scale = normalize(resid)
        layer[rows, :] = (some * vecs[6:7, :] + vecs[7:8, :]).astype(bf16)
        grad = slope[rows, :].astype(f32) * inside(i * ROWS, ROWS)
        back = norm_back(grad, some, scale, vecs[6:7, :])
        low_back = back.astype(bf16)
        second[rows, :] = back
        branch[rows, :] = low_back
        sums[5:6, :] += jnp.sum(low_back.astype(f32), axis=0, keepdims=True)
        sums[6:7, :] += jnp.sum(grad * some, axis=0, keepdims=True)
        sums[7:8, :] += jnp.sum(grad, axis=0, keepdims=True)

    layer_away.start()
    layer_near.start()

    @pl.loop(0, up.shape[1] // tile)
    def _(i):
        cols = cols_at(i * tile, tile)
        rate = bend[:, cols].astype(f32)
        low_pre = (mm_nt(branch[...], down[rows_at(i * tile, tile), :]) * rate).astype(bf16)
        bend[:, cols] = low_pre
        sums_up[:, cols] = jnp.sum(low_pre.astype(f32), axis=0, keepdims=True)

    for copy in (g_down.over, g_down.side, g_down.core_one, g_down.core_two):
        copy.wait_send()
    pl.semaphore_signal(
        free, inc=1, device_id=here.across(1), device_id_type=pl.DeviceIdType.MESH
    )
    c = here.core
    waited = False

    def make_pair(u, block):
        for one in (u, u + 1):
            if one >= 4:
                units.core_copy(one - 4).wait_send()
        for shard in range(2):
            value = block(shard, 1 - c)
            for k in range(2):
                rows = rows_at((u + k) % 4 * 2 * n + shard * n, n)
                down[rows, pl.ds(0, n)] = value[:, k * n : (k + 1) * n].astype(bf16)
        for one in (u - 2, u - 1):
            if one >= 0:
                units.first_sum(one)
        if u == 0:
            pl.semaphore_wait(free, 1)
        units.core_copy(u).start()
        units.core_copy(u + 1).start()
        for shard in range(2):
            value = block(shard, c)
            for k in range(2):
                own[u + k, shard] = value[:, k * n : (k + 1) * n].astype(bf16)

    def make_one(u, left_side, right_side, before):
        units.core_copy(u - 4).wait_send()
        for shard in range(2):
            value = mm_tn(left_side[:, shard * n : (shard + 1) * n], right_side)
            one, two = value[:, :n], value[:, n:]
            rows = pl.ds(u % 4 * 2 * n + shard * n, n)
            down[rows, pl.ds(0, n)] = jnp.where(c == 0, two, one).astype(bf16)
            own[u, shard] = jnp.where(c == 0, one, two).astype(bf16)
        for one in before:
            units.first_sum(one)
        units.core_copy(u).start()

    for r in range(2):
        make_pair(
            2 * r,
            lambda shard, h: mm_tn(
                active[:, cols_at(shard * 4 * n + h * 2 * n + r * n, n)], branch[...]
            ),
        )
    for p in range(2):
        make_pair(
            4 + 2 * p,
            lambda shard, h: mm_tn(
                hidden[:, shard * n : (shard + 1) * n], bend[:, cols_at(h * 4 * n + p * 2 * n, 2 * n)]
            ),
        )
        units.tick(p)

    @pl.loop(0, 2 * n // ROWS)
    def _(i):
        rows = rows_at(i * ROWS, ROWS)
        grad = mm_nt(bend[rows, :], up[...]) + second[rows, :]
        some = normed[rows, :]
        sums[3:4, :] += jnp.sum(grad * some, axis=0, keepdims=True)
        sums[4:5, :] += jnp.sum(grad, axis=0, keepdims=True)
        back = norm_back(grad, some, inverse[rows, 0:1], vecs[3:4, :])
        low_back = back.astype(bf16)
        second[rows, :] = back
        branch[rows, :] = low_back
        sums[2:3, :] += jnp.sum(low_back.astype(f32), axis=0, keepdims=True)
        slope[rows, :] = mm_nt(low_back, proj[...]).astype(bf16)

        @pl.when(i == 0)
        def _():
            units.first_sum(6)
            units.first_sum(7)

    units.tick(2)
    make_one(8, heads, branch[...], ())
    units.tick(3)
    place = lax.rem(lanes, DH)

    @pl.loop(0, pairs)
    def _(i):
        cols, key_cols, value_cols = [cols_at(part * D + i * PAIR, PAIR) for part in range(3)]
        query = qkv[:, cols] * SCALE
        grad = slope[:, cols]
        product = grad.astype(f32) * heads[:, cols].astype(f32)
        sides = []
        for number, side in enumerate((left, jnp.logical_not(left))):
            delta = three_parts(-jnp.sum(jnp.where(side, product, 0.0), axis=1, keepdims=True))
            logs = jnp.where(lanes == 2 * i + number, lse[...], 0.0)
            logs = three_parts(-jnp.sum(logs, axis=1, keepdims=True))
            more = jnp.where(place == 2, logs[0], jnp.where(place == 3, logs[1], logs[2]))
            more = jnp.where(place < 2, mq[...], jnp.where(place < 5, more, 0.0).astype(bf16))
            some_query = jnp.where(side, query, more)
            more = jnp.where(place == 0, delta[0], jnp.where(place == 1, delta[1], delta[2]))
            some_grad = jnp.where(side, grad, jnp.where(place < 3, more, 0.0).astype(bf16))
            sides.append((side, some_query, some_grad))
        totals = [None, None]
        for start in range(0, 2 * n, ROWS):
            rows = pl.ds(start, ROWS)
            keys, values = qkv[rows, key_cols], qkv[rows, value_cols]
            ones, zeros = jnp.ones_like(values), jnp.zeros_like(values)
            more_keys = jnp.where(place < 2, mk[rows, :], jnp.where(place < 5, ones, zeros))
            more_values = jnp.where(place < 3, ones, zeros)
            parts = []
            for number, (side, some_query, some_grad) in enumerate(sides):
                some_keys = jnp.where(side, keys, more_keys)
                some_values = jnp.where(side, values, more_values)
                probs = jnp.exp(mm_nt(some_keys, some_query))
                rate = (probs * mm_nt(some_values, some_grad)).astype(bf16)
                dv = mm(probs.astype(bf16), some_grad)
                dk = mm(rate, some_query)
                dq = mm_tn(rate, some_keys)
                totals[number] = dq if totals[number] is None else totals[number] + dq
                parts.append((dk, dv))
            active[rows, key_cols] = jnp.where(left, parts[0][0], parts[1][0]).astype(bf16)
            active[rows, value_cols] = jnp.where(left, parts[0][1], parts[1][1]).astype(bf16)
        active[:, cols] = (jnp.where(left, totals[0], totals[1]) * SCALE).astype(bf16)

        @pl.when(i == 0)
        def _():
            units.first_sum(8)

        @pl.when(i > 0)
        def _():
            units.tick(3 + i)

    for k in range(3):
        make_one(9 + k, x, active[:, k * D : (k + 1) * D], (8 + k,) if k else ())
        if k == 1:
            units.tick(9)
    units.first_sum(11)
    sums[0:1, :] = jnp.sum(active[:, 0:D].astype(f32), axis=0, keepdims=True)
    sums[1:2, :] = jnp.sum(active[:, 2 * D : 3 * D].astype(f32), axis=0, keepdims=True)
    for i in range(wide):
        sums[8 + i : 9 + i, :] = sums_up[:, i * D : (i + 1) * D]

    rounds = []
    ways = [here.across(1), here.over()] + [here.across(bit) for bit in units.bits]
    for k, way in enumerate(ways):
        rounds.append(copies.away(sums, others.at[k], way))
    rounds[0].start()

    @pl.loop(0, 2 * n // ROWS)
    def _(i):
        rows = rows_at(i * ROWS, ROWS)
        back = second[rows, :] + mm_nt(active[rows, 0 : 3 * D], three[...])
        hidden[rows, :] = back.astype(bf16)

    back_away.start()
    back_near.start()
    units.tick(10)
    last = UNITS + 2 * len(units.bits) + 1
    step = 0
    for t in range(11, last):
        units.tick(t)
        if step < len(rounds):
            rounds[step].wait()
            sums[...] += others[step]
            step += 1
            if step < len(rounds):
                rounds[step].start()
    while step < len(rounds):
        rounds[step].wait()
        sums[...] += others[step]
        step += 1
        if step < len(rounds):
            rounds[step].start()
    small[0:8, :] = sums[0:8, cols_at(y * n, n)]
    for i in range(wide):
        k = i * n // D
        from_row = 8 + wide // 2 * y + k
        small[8 + i : 9 + i, :] = sums[pl.ds(from_row, 1), i * n % D : i * n % D + n]
    small_out = copies.near(small, o_small)
    small_out.start()
    units.finish()
    small_out.wait()
    for copy in (layer_away, back_away):
        copy.wait()
    for copy in (layer_near, back_near):
        copy.wait()
    for part in (g_query, g_key, g_value, g_attn, g_up):
        part.finish()
    for copy in (vec_away, x_away, s_away):
        copy.wait_send()


def run_layer(tokens, cotangent, seq, vectors, weights, reps):
    n = weights[0].shape[0]
    count, wide = 2 * n, weights[4].shape[1]
    bits = reps.bit_length() - 2
    kinds = [
        ((2, n, D), bf16),
        ((2, n, D), bf16),
        ((UNITS, 2, n, n), bf16),
        ((16, n), f32),
    ]
    near = [((UNITS, max(16, n >> (k + 1)), n), bf16) for k in range(3)]
    scratch = [
        ((count, D), bf16),
        ((count, D), bf16),
        ((D, 3 * D), bf16),
        ((D, D), bf16),
        ((D, wide), bf16),
        ((wide, D), bf16),
        ((2, 16, n), f32),
        ((16, D), f32),
        ((1, wide), f32),
        ((count, 3 * D), bf16),
        ((count, D), bf16),
        ((count, PAIR), f32),
        ((count, PAIR), bf16),
        ((count, PAIR), bf16),
        ((count, D), f32),
        ((count, PAIR), f32),
        ((count, D), bf16),
        ((count, wide), bf16),
        ((count, wide), bf16),
        ((count, D), bf16),
        ((count, D), f32),
        ((count, D), bf16),
        ((16, D), f32),
        ((1, wide), f32),
        ((bits + 2, 16, D), f32),
        ((UNITS, 2, n, n), bf16),
        ((UNITS, n, n), bf16),
        *near,
        ((UNITS, 2, n, n), bf16),
        ((16, n), f32),
    ]
    anywhere = pl.BlockSpec(memory_space=pl.ANY)
    stages = 4 + 2 * bits
    return pl.pallas_call(
        layer_kernel,
        out_shape=[jax.ShapeDtypeStruct(*kind) for kind in kinds],
        in_specs=[anywhere, anywhere, pl.BlockSpec(memory_space=pltpu.SMEM)] + [anywhere] * 7,
        out_specs=[anywhere] * len(kinds),
        scratch_shapes=[pltpu.VMEM(*kind) for kind in scratch]
        + [
            pltpu.SemaphoreType.DMA((64,)),
            pltpu.SemaphoreType.DMA((64,)),
            pltpu.SemaphoreType.DMA((stages, UNITS)),
            pltpu.SemaphoreType.DMA((stages, UNITS)),
            pltpu.SemaphoreType.REGULAR,
        ],
        compiler_params=pltpu.CompilerParams(
            collective_id=0, has_side_effects=True, vmem_limit_bytes=67043328
        ),
        name="encoder_layer",
    )(tokens, cotangent, seq, vectors, *weights)


def general_body(
    tokens,
    cotangent,
    seq_lengths,
    w_query,
    b_query,
    w_key,
    w_value,
    b_value,
    w_attn,
    b_attn,
    norm_gain,
    norm_bias,
    w_up,
    b_up,
    w_down,
    b_down,
    out_gain,
    out_bias,
):
    at = Places()
    shards = at.shards
    micro, slots = tokens.shape[0], tokens.shape[1]
    span = shards // micro
    count = micro * slots
    x = spread(at, tokens)
    w_three = gather_rows(at, jnp.concatenate([w_query, w_key, w_value], axis=1))
    part = w_query.shape[0]
    wide = b_up.shape[0] // part
    vectors = jnp.concatenate(
        [
            jnp.stack(
                [b_query, b_value, b_attn, norm_gain, norm_bias, b_down, out_gain, out_bias]
            ),
            b_up.reshape(wide, part),
            jnp.zeros((16 - 8 - wide, part), bf16),
        ],
        axis=0,
    )
    table = put(jnp.zeros((shards,) + vectors.shape, bf16), vectors[None], at.shard)
    for step in range(1, shards):
        there = swap(vectors, "shard", shards, lambda i: (i + shards - step) % shards)
        table = put(table, there[None], (at.shard + step) % shards)
    table = table.astype(f32)
    (c_query, c_value, c_attn, c_gain, c_bias, c_down, c_out_gain, c_out_bias) = [
        table[:, i].reshape(1, D) for i in range(8)
    ]
    c_up = table[:, 8 : 8 + wide].reshape(1, D * wide)
    w_proj = gather_rows(at, w_attn)
    full_up = gather_rows(at, w_up)
    full_down = gather_rows(at, w_down)
    slope_in = spread(at, cotangent)

    group = slots * shards
    which, inner = at.shard // span, at.shard % span
    row = lax.dynamic_index_in_dim(seq_lengths[:, 0], which, 0, False)
    ids = segment_ids(row, group)

    def ids_of(device):
        parts = []
        for step in range(micro):
            source = micro * device + (which + micro - step) % micro
            parts.append(lax.dynamic_slice_in_dim(ids, source * slots, slots))
        return jnp.concatenate(parts)

    query_ids = ids_of(inner)
    nseq = seq_lengths.shape[-1] - 1
    valid = (query_ids < nseq).astype(f32)[:, None]
    three = mm(x, w_three) + jnp.concatenate([c_query, jnp.zeros_like(c_query), c_value], axis=1)
    three = three.astype(bf16)
    base = D // PAIR
    offsets = (base, 2 * base)
    key_array = three
    key_ids = [query_ids]
    if span > 1:
        offsets = (0, base)
        own = three[:, D:]
        parts = [own]
        for step in range(1, span):
            moves = [(i, i // span * span + (i + span - step) % span) for i in range(shards)]
            parts.append(lax.ppermute(own, "shard", moves))
            key_ids.append(ids_of((inner + step) % span))
        key_array = jnp.concatenate(parts, axis=0)
    mq, _ = mask_columns(query_ids)
    _, mk = mask_columns(jnp.concatenate(key_ids))
    attn, lse = attention_forward(three, key_array, offsets, mq, mk)

    normed_one, inverse_one = normalize(x.astype(f32) + mm(attn, w_proj) + c_attn)
    hidden = normed_one * c_gain + c_bias
    hidden_low = hidden.astype(bf16)
    pre = mm(hidden_low, full_up) + c_up
    lower = 0.5 * (1.0 + lax.erf(pre * 0.7071067811865476))
    active = (pre * lower).astype(bf16)
    density = jnp.exp(-0.5 * pre * pre) * 0.3989422804014327
    gelu_slope = lower + pre * density
    normed_two, inverse_two = normalize(hidden + mm(active, full_down) + c_down)
    layer = (normed_two * c_out_gain + c_out_bias).astype(bf16)
    grad_out = slope_in.astype(f32) * valid
    d_out_gain = jnp.sum(grad_out * normed_two, axis=0)
    d_out_bias = jnp.sum(grad_out, axis=0)
    grad_second = norm_back(grad_out, normed_two, inverse_two, c_out_gain)
    grad_branch = grad_second.astype(bf16)
    d_down = jnp.sum(grad_branch.astype(f32), axis=0)
    g_down = mm_tn(active, grad_branch)
    grad_pre = (mm_nt(grad_branch, full_down) * gelu_slope).astype(bf16)
    d_up = jnp.sum(grad_pre.astype(f32), axis=0)
    g_up = mm_tn(hidden_low, grad_pre)
    grad_hidden = mm_nt(grad_pre, full_up) + grad_second
    d_gain = jnp.sum(grad_hidden * normed_one, axis=0)
    d_bias = jnp.sum(grad_hidden, axis=0)
    grad_first = norm_back(grad_hidden, normed_one, inverse_one, c_gain)
    grad_proj = grad_first.astype(bf16)
    d_attn = jnp.sum(grad_proj.astype(f32), axis=0)
    g_attn = mm_tn(attn, grad_proj)
    grad_attn = mm_nt(grad_proj, w_proj).astype(bf16)
    dq, dk, dv = attention_backward(three, key_array, offsets, mq, mk, attn, lse, grad_attn)
    if span > 1:
        both = jnp.concatenate([dk, dv], axis=1)
        total = both[:count].astype(f32)
        for step in range(1, span):
            moves = [(i, i // span * span + (i + step) % span) for i in range(shards)]
            away = both[step * count : (step + 1) * count]
            total = total + lax.ppermute(away, "shard", moves).astype(f32)
        dk, dv = total[:, :D].astype(bf16), total[:, D:].astype(bf16)
    d_three = jnp.concatenate([dq, dk, dv], axis=1)
    d_query = jnp.sum(dq.astype(f32), axis=0)
    d_value = jnp.sum(dv.astype(f32), axis=0)
    g_three = mm_tn(x, d_three)
    back = (grad_first + mm_nt(d_three, w_three)).astype(bf16)

    sums = jnp.concatenate(
        [
            jnp.stack([d_query, d_value, d_attn, d_gain, d_bias, d_down, d_out_gain, d_out_bias]).reshape(
                8, shards, part
            ),
            d_up.reshape(shards, wide, part).transpose(1, 0, 2),
            jnp.zeros((PAIR - 8 - wide, shards, part), f32),
        ],
        axis=0,
    )
    sums = sums.reshape(PAIR, D).T
    r_down = reduce_rows(at, g_down)
    r_up = reduce_rows(at, g_up)
    r_attn = reduce_rows(at, g_attn)
    r_three = reduce_rows(at, jnp.concatenate([g_three, sums], axis=1))
    small = r_three[:, 3 * D :].T
    return (
        collect(at, layer, micro),
        collect(at, back, micro),
        r_three[:, :D],
        small[0],
        r_three[:, D : 2 * D],
        r_three[:, 2 * D : 3 * D],
        small[1],
        r_attn,
        small[2],
        small[3],
        small[4],
        r_up,
        small[8 : 8 + wide].reshape(wide * part),
        r_down,
        small[5],
        small[6],
        small[7],
    )


def body(tokens, cotangent, seq_lengths, *weights):
    shards, micro = lax.axis_size("shard"), tokens.shape[0]
    reps = lax.axis_size("rep")
    if shards != 2 or micro != 2 or reps not in (4, 8, 16):
        return general_body(tokens, cotangent, seq_lengths, *weights)
    (
        w_query,
        b_query,
        w_key,
        w_value,
        b_value,
        w_attn,
        b_attn,
        norm_gain,
        norm_bias,
        w_up,
        b_up,
        w_down,
        b_down,
        out_gain,
        out_bias,
    ) = weights
    part = w_query.shape[0]
    wide = b_up.shape[0] // part
    lines = [b_query, b_value, b_attn, norm_gain, norm_bias, b_down, out_gain, out_bias]
    lines += [b_up[i * part : (i + 1) * part] for i in range(wide)]
    number = lax.broadcasted_iota(jnp.int32, (16, part), 0)
    vectors = jnp.zeros((16, part), f32)
    for i, line in enumerate(lines):
        vectors = jnp.where(number == i, line.astype(f32)[None], vectors)
    layer, back, grads, small = run_layer(
        tokens,
        cotangent,
        seq_lengths,
        vectors,
        (w_query, w_key, w_value, w_attn, w_up, w_down),
        reps,
    )
    g_down = grads[:4].reshape(2, 2, 2, part, part).transpose(2, 0, 3, 1, 4).reshape(4 * part, D)
    g_up = grads[4:8].reshape(2, 2, 2, part, part).transpose(3, 2, 0, 1, 4).reshape(part, 8 * part)
    g_attn, g_query, g_key, g_value = [
        grads[8 + k].transpose(1, 0, 2).reshape(part, D).astype(f32) for k in range(4)
    ]
    return (
        layer,
        back,
        g_query,
        small[0],
        g_key,
        g_value,
        small[1],
        g_attn,
        small[2],
        small[3],
        small[4],
        g_up.astype(f32),
        small[8 : 8 + wide].reshape(wide * part),
        g_down.astype(f32),
        small[5],
        small[6],
        small[7],
    )


def solution(mesh):
    rows, vector = P("shard", None), P("shard")
    tokens = P(None, ("rep", "shard"), None)
    weights = (rows, vector, rows, rows, vector, rows, vector, vector, vector)
    weights += (rows, vector, rows, vector, vector, vector)
    return jax.shard_map(
        body,
        mesh=mesh,
        in_specs=(tokens, tokens, P(None, "rep", None)) + weights,
        out_specs=(tokens, tokens) + weights,
        check_vma=False,
    )
```

```python
import functools

import jax
import jax.numpy as jnp
from jax import lax
from jax.experimental import pallas as pl
from jax.experimental.pallas import tpu as pltpu
from jax.sharding import PartitionSpec as P

D = 768
H = 12
DH = 64
PAIR = 2 * DH
EPS = 1e-12
BIG = 1e30
SCALE = DH ** (-0.5)
ROWS = 256
f32 = jnp.float32
bf16 = jnp.bfloat16


def mm(left, right):
    return jnp.dot(left, right, preferred_element_type=f32)


def mm_nt(left, right):
    return lax.dot_general(left, right, (((1,), (1,)), ((), ())), preferred_element_type=f32)


def mm_tn(left, right):
    return lax.dot_general(left, right, (((0,), (0,)), ((), ())), preferred_element_type=f32)


def segment_ids(row, count):
    bounds = jnp.cumsum(row[:-1])
    places = jnp.arange(count, dtype=jnp.int32)
    return jnp.sum((places[:, None] >= bounds[None, :]).astype(jnp.int32), axis=1)


def mask_columns(ids):
    first = (ids == 0).astype(f32)[:, None]
    other = 1.0 - first
    lane = lax.broadcasted_iota(jnp.int32, (1, PAIR), 1) % DH
    on_query = jnp.where(lane == 0, -BIG * first, jnp.where(lane == 1, -BIG * other, 0.0))
    on_key = jnp.where(lane == 0, other, jnp.where(lane == 1, first, 0.0))
    return on_query.astype(bf16), on_key.astype(bf16)


def forward_heads(q_ref, k_ref, v_ref, mq_ref, mk_ref, attn_ref, lse_ref):
    lane = lax.broadcasted_iota(jnp.int32, (1, PAIR), 1)
    low = lane < DH
    keys, values, mk = k_ref[...], v_ref[...], mk_ref[...]
    one = jnp.ones_like(values)
    sides = []
    for own in (low, jnp.logical_not(low)):
        sides.append((own, jnp.where(own, keys, mk), jnp.where(own, values, one)))
    count = q_ref.shape[0]
    block = min(ROWS, count)
    for start in range(0, count, block):
        rows = pl.ds(start, block)
        query, mq = q_ref[rows, :] * SCALE, mq_ref[rows, :]
        outs = []
        for own, some_keys, some_values in sides:
            scores = mm_nt(jnp.where(own, query, mq), some_keys)
            top = jnp.max(scores, axis=1, keepdims=True)
            expo = jnp.exp(scores - top).astype(bf16)
            mixed = mm(expo, some_values)
            total = pltpu.roll(mixed, DH, 1)
            outs.append((mixed / total, top + jnp.log(total)))
        attn_ref[rows, :] = jnp.where(low, outs[0][0], outs[1][0]).astype(bf16)
        lse_ref[rows, :] = jnp.where(low, outs[0][1], outs[1][1])


def three_parts(value):
    first = value.astype(bf16).astype(f32)
    rest = value - first
    second = rest.astype(bf16).astype(f32)
    return first, second, rest - second


def backward_heads(
    q_ref, k_ref, v_ref, mq_ref, mk_ref, attn_ref, lse_ref, grad_ref, dq_ref, dk_ref, dv_ref
):
    lane = lax.broadcasted_iota(jnp.int32, (1, PAIR), 1)
    place = lane % DH
    low = lane < DH
    query, mq, grad = q_ref[...] * SCALE, mq_ref[...], grad_ref[...]
    product = grad.astype(f32) * attn_ref[...].astype(f32)
    lse = three_parts(-pltpu.roll(lse_ref[...], DH, 1))
    count_keys = k_ref.shape[0]
    block = min(ROWS, count_keys)
    sides = []
    for own in (low, jnp.logical_not(low)):
        delta = three_parts(-jnp.sum(jnp.where(own, product, 0.0), axis=1, keepdims=True))
        more = jnp.where(place == 2, lse[0], jnp.where(place == 3, lse[1], lse[2]))
        more = jnp.where(place < 2, mq, jnp.where(place < 5, more, 0.0).astype(bf16))
        some_query = jnp.where(own, query, more)
        more = jnp.where(place == 0, delta[0], jnp.where(place == 1, delta[1], delta[2]))
        some_grad = jnp.where(own, grad, jnp.where(place < 3, more, 0.0).astype(bf16))
        sides.append((own, some_query, some_grad, None))
    totals = [None, None]
    for start in range(0, count_keys, block):
        rows = pl.ds(start, block)
        keys, values, mk = k_ref[rows, :], v_ref[rows, :], mk_ref[rows, :]
        ones = jnp.ones_like(values)
        zeros = jnp.zeros_like(values)
        more_keys = jnp.where(place < 2, mk, jnp.where(place < 5, ones, zeros))
        more_values = jnp.where(place < 3, ones, zeros)
        parts = []
        for side in range(2):
            own, some_query, some_grad, _ = sides[side]
            some_keys = jnp.where(own, keys, more_keys)
            some_values = jnp.where(own, values, more_values)
            probs = jnp.exp(mm_nt(some_keys, some_query))
            slope = (probs * mm_nt(some_values, some_grad)).astype(bf16)
            dv = mm(probs.astype(bf16), some_grad)
            dk = mm(slope, some_query)
            dq = mm_tn(slope, some_keys)
            totals[side] = dq if totals[side] is None else totals[side] + dq
            parts.append((dk, dv))
        dk_ref[rows, :] = jnp.where(low, parts[0][0], parts[1][0]).astype(bf16)
        dv_ref[rows, :] = jnp.where(low, parts[0][1], parts[1][1]).astype(bf16)
    dq_ref[...] = (jnp.where(low, totals[0], totals[1]) * SCALE).astype(bf16)


def head_block(rows, offset):
    return pl.BlockSpec((rows, PAIR), lambda i: (0, i + offset))


def fixed_block(rows):
    return pl.BlockSpec((rows, PAIR), lambda i: (0, 0))


def attention_forward(query_array, key_array, offsets, mq, mk):
    count, keys = query_array.shape[0], key_array.shape[0]
    pairs = H * DH // PAIR
    return pl.pallas_call(
        forward_heads,
        grid=(pairs,),
        out_shape=(
            jax.ShapeDtypeStruct((count, D), bf16),
            jax.ShapeDtypeStruct((count, D), f32),
        ),
        in_specs=[
            head_block(count, 0),
            head_block(keys, offsets[0]),
            head_block(keys, offsets[1]),
            fixed_block(count),
            fixed_block(keys),
        ],
        out_specs=(head_block(count, 0), head_block(count, 0)),
        cost_estimate=pl.CostEstimate(
            flops=16 * count * keys * D, bytes_accessed=8 * (count + keys) * D, transcendentals=count * keys * H
        ),
        name="attention_forward",
    )(query_array, key_array, key_array, mq, mk)


def attention_backward(query_array, key_array, offsets, mq, mk, attn, lse, grad):
    count, keys = query_array.shape[0], key_array.shape[0]
    pairs = H * DH // PAIR
    return pl.pallas_call(
        backward_heads,
        grid=(pairs,),
        out_shape=(
            jax.ShapeDtypeStruct((count, D), bf16),
            jax.ShapeDtypeStruct((keys, D), bf16),
            jax.ShapeDtypeStruct((keys, D), bf16),
        ),
        in_specs=[
            head_block(count, 0),
            head_block(keys, offsets[0]),
            head_block(keys, offsets[1]),
            fixed_block(count),
            fixed_block(keys),
            head_block(count, 0),
            head_block(count, 0),
            head_block(count, 0),
        ],
        out_specs=(head_block(count, 0), head_block(keys, 0), head_block(keys, 0)),
        cost_estimate=pl.CostEstimate(
            flops=40 * count * keys * D, bytes_accessed=16 * (count + keys) * D, transcendentals=count * keys * H
        ),
        name="attention_backward",
    )(query_array, key_array, key_array, mq, mk, attn, lse, grad)


def normalize(rows):
    mean = jnp.mean(rows, axis=-1, keepdims=True)
    centered = rows - mean
    inverse = lax.rsqrt(jnp.mean(centered * centered, axis=-1, keepdims=True) + EPS)
    return centered * inverse, inverse


def norm_back(grad, normed, inverse, gain):
    scaled = grad * gain
    first = jnp.mean(scaled, axis=-1, keepdims=True)
    second = jnp.mean(scaled * normed, axis=-1, keepdims=True)
    return inverse * (scaled - first - normed * second)


def swap(value, axis, size, move):
    return lax.ppermute(value, axis, [(i, move(i)) for i in range(size)])


def put(buffer, value, index, axis=0):
    return lax.dynamic_update_slice_in_dim(buffer, value, index * value.shape[axis], axis)


def pick(value, index, parts, axis=0):
    size = value.shape[axis] // parts
    return lax.dynamic_slice_in_dim(value, index * size, size, axis)


class Places:
    def __init__(self):
        self.reps = lax.axis_size("rep")
        self.shards = lax.axis_size("shard")
        self.rep = lax.axis_index("rep")
        self.shard = lax.axis_index("shard")
        self.core = self.rep % 2


def gather_rows(at, own):
    half = own.shape[0] // 2
    out = jnp.zeros((at.shards * own.shape[0],) + own.shape[1:], own.dtype)
    out = put(out, own, at.shard)
    mine = pick(own, at.core, 2)
    for step in range(1, at.shards):
        there = swap(mine, "shard", at.shards, lambda i: (i + at.shards - step) % at.shards)
        other = swap(there, "rep", at.reps, lambda i: i ^ 1)
        block = (at.shard + step) % at.shards * 2
        out = put(out, there, block + at.core)
        out = put(out, other, block + 1 - at.core)
    return out


def reduce_rows(at, grad):
    shards, columns = at.shards, grad.shape[1]
    rows = grad.shape[0] // shards
    value = grad.reshape(shards * 2, rows // 2, columns)
    value = grad.reshape(shards, 2, rows // 2, columns)
    mine = lax.dynamic_index_in_dim(value, at.core, 1, False)
    away = lax.dynamic_index_in_dim(value, 1 - at.core, 1, False).astype(bf16)
    value = mine.astype(f32) + swap(away, "rep", at.reps, lambda i: i ^ 1).astype(f32)
    total = lax.dynamic_index_in_dim(value, at.shard, 0, False)
    for step in range(1, shards):
        away = lax.dynamic_index_in_dim(value, (at.shard + step) % shards, 0, False).astype(bf16)
        total = total + swap(away, "shard", shards, lambda i: (i + step) % shards).astype(f32)
    stages = []
    bit = 2
    while bit < at.reps:
        axis = 0 if total.shape[0] % 32 == 0 else 1
        stages.append((bit, axis))
        up = (at.rep // bit) % 2
        mine, away = pick(total, up, 2, axis), pick(total, 1 - up, 2, axis).astype(bf16)
        move = functools.partial(lambda b, i: i ^ b, bit)
        total = mine + swap(away, "rep", at.reps, move).astype(f32)
        bit *= 2
    total = total.astype(bf16)
    for bit, axis in reversed(stages):
        up = (at.rep // bit) % 2
        move = functools.partial(lambda b, i: i ^ b, bit)
        other = swap(total, "rep", at.reps, move)
        shape = list(total.shape)
        shape[axis] *= 2
        both = jnp.zeros(shape, bf16)
        total = put(put(both, total, up, axis), other, 1 - up, axis)
    other = swap(total, "rep", at.reps, lambda i: i ^ 1)
    first = jnp.where(at.core == 0, total, other)
    second = jnp.where(at.core == 0, other, total)
    return jnp.concatenate([first, second], axis=0).astype(f32)


def spread(at, value):
    micro, shards = value.shape[0], at.shards
    parts = []
    for step in range(micro):
        moves = [(i, (i + step) % micro * (shards // micro) + i // micro) for i in range(shards)]
        part = lax.dynamic_index_in_dim(value, (at.shard + step) % micro, 0, False)
        if any(a != b for a, b in moves):
            part = lax.ppermute(part, "shard", moves)
        parts.append(part)
    return jnp.concatenate(parts, axis=0)


def collect(at, value, micro):
    shards = at.shards
    slots = value.shape[0] // micro
    out = jnp.zeros((micro, slots) + value.shape[1:], value.dtype)
    for step in range(micro):
        moves = [((i + step) % micro * (shards // micro) + i // micro, i) for i in range(shards)]
        part = value[step * slots : (step + 1) * slots]
        if any(a != b for a, b in moves):
            part = lax.ppermute(part, "shard", moves)
        out = lax.dynamic_update_index_in_dim(out, part, (at.shard + step) % micro, 0)
    return out


def rows_at(start, size):
    return pl.ds(pl.multiple_of(start, 16), size)


def cols_at(start, size):
    return pl.ds(pl.multiple_of(start, PAIR), size)


class Here:
    def __init__(self):
        self.rep = lax.axis_index("rep")
        self.y = lax.axis_index("shard")
        self.core = lax.rem(self.rep, 2)
        self.x = lax.rem(lax.div(self.rep, 2), 2)

    def across(self, bit):
        up = lax.rem(lax.div(self.rep, bit), 2)
        return {"rep": self.rep + bit * (1 - 2 * up)}

    def over(self):
        return {"shard": 1 - self.y}


class Copies:
    def __init__(self, send, recv):
        self.send, self.recv, self.used, self.open = send, recv, 0, []

    def away(self, source, target, peer):
        k = self.used
        self.used += 1
        copy = pltpu.make_async_remote_copy(
            src_ref=source,
            dst_ref=target,
            send_sem=self.send.at[k],
            recv_sem=self.recv.at[k],
            device_id=peer,
            device_id_type=pl.DeviceIdType.MESH,
        )
        return copy

    def near(self, source, target):
        k = self.used
        self.used += 1
        return pltpu.make_async_copy(source, target, self.recv.at[k])


def greet(peers):
    barrier = pltpu.get_barrier_semaphore()
    for peer in peers:
        pl.semaphore_signal(barrier, inc=1, device_id=peer, device_id_type=pl.DeviceIdType.MESH)
    pl.semaphore_wait(barrier, len(peers))


class Gathered:
    def __init__(self, here, copies, own, full, shard_rows, first_row, n, cols):
        h = n // 4
        q = 2 * here.x + here.core
        across = 2 * (1 - here.x) + here.core
        mine = here.y * shard_rows + first_row
        other = (1 - here.y) * shard_rows + first_row

        def at(start, size):
            return full.at[rows_at(start, size), cols]

        self.local = copies.near(own(0, n), at(mine, n))
        self.over = copies.away(own(q * h, h), at(mine + q * h, h), here.over())
        first, second = at(other + q * h, h), at(other + across * h, h)
        self.side = copies.away(first, first, here.across(2))
        self.core_one = copies.away(first, first, here.across(1))
        self.core_two = copies.away(second, second, here.across(1))

    def start(self):
        self.over.start()
        self.local.start()

    def forward_one(self):
        self.over.wait_recv()
        self.side.start()
        self.core_one.start()

    def forward_two(self):
        self.side.wait_recv()
        self.core_two.start()

    def ready(self):
        self.local.wait()
        self.core_one.wait_recv()
        self.core_two.wait_recv()

    def finish(self):
        for copy in (self.over, self.side, self.core_one, self.core_two):
            copy.wait_send()


def gelu_parts(pre):
    lower = 0.5 * (1.0 + lax.erf(pre * 0.7071067811865476))
    density = jnp.exp(-0.5 * pre * pre) * 0.3989422804014327
    return pre * lower, lower + pre * density


UNITS = 12


class Units:
    def __init__(self, here, reps, send, recv, swap_buffer, own, far, near, done, result):
        self.here, self.send, self.recv = here, send, recv
        self.swap_buffer, self.own, self.far, self.near, self.done = swap_buffer, own, far, near, done
        self.result = result
        self.n = own.shape[2]
        self.bits = []
        bit = 2
        while bit < reps:
            self.bits.append(bit)
            bit *= 2
        self.stages = 3 + 2 * len(self.bits)

    def copy(self, stage, u, source, target, peer):
        return pltpu.make_async_remote_copy(
            src_ref=source,
            dst_ref=target,
            send_sem=self.send.at[stage, u],
            recv_sem=self.recv.at[stage, u],
            device_id=peer,
            device_id_type=pl.DeviceIdType.MESH,
        )

    def slot(self, u, side):
        n = self.n
        return self.swap_buffer.at[rows_at(lax.rem(u, 4) * 2 * n, 2 * n), pl.ds(side * n, n)]

    def rows_of(self, level):
        size, start = self.n, 0
        for bit in self.bits[:level]:
            size //= 2
            start = start + lax.rem(lax.div(self.here.rep, bit), 2) * size
        return start, size

    def core_copy(self, u):
        return self.copy(0, u, self.slot(u, 0), self.slot(u, 1), self.here.across(1))

    def y_copy(self, u):
        return self.copy(1, u, self.own.at[u, 1 - self.here.y], self.far.at[u], self.here.over())

    def down_copy(self, k, u):
        start, size = self.rows_of(k)
        half = size // 2
        up = lax.rem(lax.div(self.here.rep, self.bits[k]), 2)
        rows = rows_at(start + (1 - up) * half, half)
        return self.copy(
            2 + k, u, self.own.at[u, self.here.y, rows, :], self.near[k].at[u], self.here.across(self.bits[k])
        )

    def up_copy(self, k, u):
        level = len(self.bits) - k
        start, size = self.rows_of(level)
        bit = self.bits[level - 1] if level else 1
        piece = self.done.at[u, self.here.core, rows_at(start, size), :]
        return self.copy(2 + len(self.bits) + k, u, piece, piece, self.here.across(bit))

    def out_copies(self, u):
        n = self.n
        down, up, *square = self.result
        for h in range(2):
            if u < 4:
                place = down.at[pl.ds(h * 2 * n + u // 2 * n, n), pl.ds(u % 2 * n, n)]
            elif u < 8:
                place = up.at[:, pl.ds(h * 4 * n + (u - 4) * n, n)]
            else:
                place = square[u - 8].at[:, pl.ds(h * n, n)]
            yield pltpu.make_async_copy(
                self.done.at[u, h], place, (self.send, self.recv)[h].at[self.stages, u]
            )

    def put_out(self, u):
        for copy in self.out_copies(u):
            copy.start()

    def first_sum(self, u):
        n, y = self.n, self.here.y
        self.core_copy(u).wait_recv()
        for shard in (1 - y, y):
            rows = rows_at((lax.rem(u, 4) * 2 + shard) * n, n)
            theirs = self.swap_buffer[rows, pl.ds(n, n)].astype(f32)
            self.own[u, shard] = (self.own[u, shard].astype(f32) + theirs).astype(bf16)
            if shard is not y:
                self.y_copy(u).start()

    def stage(self, k, u):
        bits = len(self.bits)
        y = self.here.y
        if k == 0:
            self.y_copy(u).wait_recv()
            start, size = self.rows_of(0)
            arrived = self.far
        elif k <= bits:
            self.down_copy(k - 1, u).wait_recv()
            arrived = self.near[k - 1]
            start, size = self.rows_of(k)
        if k < bits:
            half = size // 2
            up = lax.rem(lax.div(self.here.rep, self.bits[k]), 2)
            for part in (1 - up, up):
                rows = rows_at(start + part * half, half)
                theirs = arrived[u, rows_at(part * half, half), :].astype(f32)
                self.own[u, y, rows, :] = (self.own[u, y, rows, :].astype(f32) + theirs).astype(bf16)
                if part is not up:
                    self.down_copy(k, u).start()
        elif k == bits:
            rows = rows_at(start, size)
            total = self.own[u, y, rows, :].astype(f32) + arrived[u].astype(f32)
            self.done[u, self.here.core, rows, :] = total.astype(bf16)
            self.up_copy(0, u).start()
        else:
            self.up_copy(k - bits - 1, u).wait_recv()
            if k <= 2 * bits:
                self.up_copy(k - bits, u).start()
            elif isinstance(u, int):
                self.put_out(u)

    def tick(self, t):
        for k in reversed(range(2 * len(self.bits) + 2)):
            u = t - k
            if isinstance(u, int):
                if 0 <= u < UNITS:
                    self.stage(k, u)
            else:
                pl.when(jnp.logical_and(u >= 0, u < UNITS))(functools.partial(self.stage, k, u))

    def finish(self):
        @pl.loop(0, UNITS)
        def _(u):
            @pl.when(u >= UNITS - 4)
            def _():
                self.core_copy(u).wait_send()

            self.y_copy(u).wait_send()
            for k in range(len(self.bits)):
                self.down_copy(k, u).wait_send()
            for k in range(len(self.bits) + 1):
                self.up_copy(k, u).wait_send()

        for u in range(UNITS):
            for copy in self.out_copies(u):
                copy.wait()


def layer_kernel(
    tokens,
    cotangent,
    seq,
    *rest,
):
    lines, b_up, weights = rest[:8], rest[8], rest[9:15]
    layer_steps(tokens, cotangent, seq, lines, b_up, *weights, rest[15:24], *rest[24:])


def layer_steps(
    tokens,
    cotangent,
    seq,
    lines,
    b_up,
    w_query,
    w_key,
    w_value,
    w_attn,
    w_up,
    w_down,
    outs,
    x,
    slope,
    three,
    proj,
    up,
    down,
    raw_vectors,
    vecs,
    vec_up,
    qkv,
    heads,
    lse,
    mq,
    mk,
    normed,
    inverse,
    hidden,
    active,
    bend,
    branch,
    second,
    layer,
    sums,
    sums_up,
    others,
    own,
    far,
    near_x,
    near_z,
    near_w,
    done,
    small,
    send,
    recv,
    unit_send,
    unit_recv,
    free,
):
    reps = lax.axis_size("rep")
    here = Here()
    copies = Copies(send, recv)
    n = w_query.shape[0]
    y = here.y
    near = (near_x, near_z, near_w)
    o_layer, o_back, *o_grads, o_small = outs
    units = Units(here, reps, unit_send, unit_recv, down, own, far, near, done, o_grads)
    peers = [here.over(), here.across(1)] + [here.across(bit) for bit in units.bits]
    greet(peers)

    wide = up.shape[1] // (2 * n)

    def piece(weight, full, row, col, into):
        def own(start, size):
            return weight.at[rows_at(row + start, size), pl.ds(col, D)]

        return Gathered(here, copies, own, full, weight.shape[0], row, n, pl.ds(into + col, D))

    g_three = [piece(w, three, 0, 0, k * D) for k, w in enumerate((w_query, w_key, w_value))]
    g_attn = piece(w_attn, proj, 0, 0, 0)
    g_up = [piece(w_up, up, 0, k * D, 0) for k in range(up.shape[1] // D)]
    g_down = [piece(w_down, down, k * n, 0, 0) for k in range(w_down.shape[0] // n)]
    vec_away = copies.away(raw_vectors.at[y], raw_vectors.at[y], here.over())
    low, high = pl.ds(0, n), pl.ds(n, n)
    x_away = copies.away(tokens.at[1 - y], x.at[high, :], here.over())
    x_near = copies.near(tokens.at[y], x.at[low, :])
    s_away = copies.away(cotangent.at[1 - y], slope.at[high, :], here.over())
    s_near = copies.near(cotangent.at[y], slope.at[low, :])
    layer_away = copies.away(layer.at[high, :], o_layer.at[y], here.over())
    layer_near = copies.near(layer.at[low, :], o_layer.at[y])
    back_away = copies.away(hidden.at[high, :], o_back.at[y], here.over())
    back_near = copies.near(hidden.at[low, :], o_back.at[y])
    x_near.start()
    for part in g_three:
        part.start()
    for i, line in enumerate(lines):
        raw_vectors[y, i : i + 1, :] = line[...].astype(f32).reshape(1, n)
    for i in range(wide):
        raw_vectors[y, 8 + i : 9 + i, :] = b_up[i * n : (i + 1) * n].astype(f32).reshape(1, n)
    vec_away.start()
    x_away.start()
    for part in [g_attn] + g_up + g_down:
        part.start()
    s_away.start()
    s_near.start()

    length = seq[y, 0, 0]

    def inside(start, size):
        row = start + lax.broadcasted_iota(jnp.int32, (size, 1), 0)
        place = row + jnp.where(row < n, y * n, -y * n)
        return (place < length).astype(f32)

    first = inside(0, 2 * n)
    lane = lax.rem(lax.broadcasted_iota(jnp.int32, (1, PAIR), 1), DH)
    mq[...] = jnp.where(
        lane == 0, -BIG * first, jnp.where(lane == 1, -BIG * (1.0 - first), 0.0)
    ).astype(bf16)
    mk[...] = jnp.where(lane == 0, 1.0 - first, jnp.where(lane == 1, first, 0.0)).astype(bf16)
    sums[...] = jnp.zeros_like(sums)
    lse[...] = jnp.zeros_like(lse)

    for part in g_three:
        part.forward_one()
    for part in g_three:
        part.forward_two()
    vec_away.wait_recv()
    for half in range(2):
        table = raw_vectors[half]
        vecs[:, half * n : (half + 1) * n] = table
        for i in range(wide):
            start = half * wide * n + i * n
            vec_up[:, start : start + n] = table[8 + i : 9 + i, :]
    for part in g_three:
        part.ready()
    x_near.wait()
    tile = 256

    @pl.loop(0, 2)
    def _(half):
        pl.when(half == 1)(x_away.wait_recv)
        rows = rows_at(half * n, n)

        @pl.loop(0, 3 * D // tile)
        def _(i):
            cols = cols_at(i * tile, tile)
            which = lax.div(i, D // tile)
            inner = cols_at(lax.rem(i, D // tile) * tile, tile)
            bias = jnp.where(
                which == 0, vecs[0:1, inner], jnp.where(which == 2, vecs[1:2, inner], 0.0)
            )
            qkv[rows, cols] = (mm(x[rows, :], three[:, cols]) + bias).astype(bf16)

    lanes = lax.broadcasted_iota(jnp.int32, (1, PAIR), 1)
    left = lanes < DH
    pairs = H * DH // PAIR

    @pl.loop(0, pairs)
    def _(i):
        keys, values = qkv[:, cols_at(D + i * PAIR, PAIR)], qkv[:, cols_at(2 * D + i * PAIR, PAIR)]
        one = jnp.ones_like(values)
        sides = []
        for side in (left, jnp.logical_not(left)):
            sides.append((side, jnp.where(side, keys, mk[...]), jnp.where(side, values, one)))
        for start in range(0, 2 * n, ROWS):
            rows = pl.ds(start, ROWS)
            query = qkv[rows, cols_at(i * PAIR, PAIR)] * SCALE
            outs = []
            total_lse = lse[rows, :]
            for number, (side, some_keys, some_values) in enumerate(sides):
                scores = mm_nt(jnp.where(side, query, mq[rows, :]), some_keys)
                top = jnp.max(scores, axis=1, keepdims=True)
                expo = jnp.exp(scores - top).astype(bf16)
                mixed = mm(expo, some_values)
                total = pltpu.roll(mixed, DH, 1)
                outs.append(mixed / total)
                sum_all = jnp.where(side, total, mixed)
                total_lse = jnp.where(lanes == 2 * i + number, top + jnp.log(sum_all), total_lse)
            lse[rows, :] = total_lse
            heads[rows, cols_at(i * PAIR, PAIR)] = jnp.where(left, outs[0], outs[1]).astype(bf16)

        plan = [
            [g_attn.forward_one, g_up[0].forward_one, g_up[1].forward_one],
            [g_attn.forward_two, g_up[0].forward_two, g_up[2].forward_one],
            [g_up[1].forward_two, g_up[3].forward_one],
            [g_up[2].forward_two, g_down[0].forward_one],
            [g_up[3].forward_two, g_down[1].forward_one],
            [g_down[0].forward_two, g_down[2].forward_one],
        ]
        for number, steps in enumerate(plan):

            @pl.when(i == number)
            def _():
                for one in steps:
                    one()

    g_attn.ready()

    @pl.loop(0, 2 * n // ROWS)
    def _(i):
        rows = rows_at(i * ROWS, ROWS)
        resid = x[rows, :].astype(f32) + mm(heads[rows, :], proj[...]) + vecs[2:3, :]
        some, scale = normalize(resid)
        normed[rows, :] = some
        inverse[rows, :] = jnp.broadcast_to(scale, (ROWS, PAIR))
        hidden[rows, :] = (some * vecs[3:4, :] + vecs[4:5, :]).astype(bf16)

    g_down[1].forward_two()
    g_down[3].forward_one()
    for part in g_up:
        part.ready()

    @pl.loop(0, up.shape[1] // tile)
    def _(i):
        cols = cols_at(i * tile, tile)
        pre = mm(hidden[...], up[:, cols]) + vec_up[:, cols]
        value, rate = gelu_parts(pre)
        active[:, cols] = value.astype(bf16)
        bend[:, cols] = rate.astype(bf16)

        pl.when(i == 3)(g_down[2].forward_two)
        pl.when(i == 8)(g_down[3].forward_two)

    for part in g_down:
        part.ready()
    s_away.wait_recv()
    s_near.wait()

    @pl.loop(0, 2 * n // ROWS)
    def _(i):
        rows = rows_at(i * ROWS, ROWS)
        resid = mm(active[rows, :], down[...]) + vecs[5:6, :]
        resid = resid + (normed[rows, :] * vecs[3:4, :] + vecs[4:5, :])
        some, scale = normalize(resid)
        layer[rows, :] = (some * vecs[6:7, :] + vecs[7:8, :]).astype(bf16)
        grad = slope[rows, :].astype(f32) * inside(i * ROWS, ROWS)
        back = norm_back(grad, some, scale, vecs[6:7, :])
        low_back = back.astype(bf16)
        second[rows, :] = back
        branch[rows, :] = low_back
        sums[5:6, :] += jnp.sum(low_back.astype(f32), axis=0, keepdims=True)
        sums[6:7, :] += jnp.sum(grad * some, axis=0, keepdims=True)
        sums[7:8, :] += jnp.sum(grad, axis=0, keepdims=True)

    layer_away.start()
    layer_near.start()

    @pl.loop(0, up.shape[1] // tile)
    def _(i):
        cols = cols_at(i * tile, tile)
        rate = bend[:, cols].astype(f32)
        low_pre = (mm_nt(branch[...], down[rows_at(i * tile, tile), :]) * rate).astype(bf16)
        bend[:, cols] = low_pre
        sums_up[:, cols] = jnp.sum(low_pre.astype(f32), axis=0, keepdims=True)

    for part in g_down:
        part.finish()
    pl.semaphore_signal(
        free, inc=1, device_id=here.across(1), device_id_type=pl.DeviceIdType.MESH
    )
    c = here.core
    waited = False

    def make_pair(u, block):
        for one in (u, u + 1):
            if one >= 4:
                units.core_copy(one - 4).wait_send()
        for shard in range(2):
            value = block(shard, 1 - c)
            for k in range(2):
                rows = rows_at((u + k) % 4 * 2 * n + shard * n, n)
                down[rows, pl.ds(0, n)] = value[:, k * n : (k + 1) * n].astype(bf16)
        for one in (u - 2, u - 1):
            if one >= 0:
                units.first_sum(one)
        if u == 0:
            pl.semaphore_wait(free, 1)
        units.core_copy(u).start()
        units.core_copy(u + 1).start()
        for shard in range(2):
            value = block(shard, c)
            for k in range(2):
                own[u + k, shard] = value[:, k * n : (k + 1) * n].astype(bf16)

    def make_one(u, left_side, right_side, before):
        units.core_copy(u - 4).wait_send()
        for shard in range(2):
            value = mm_tn(left_side[:, shard * n : (shard + 1) * n], right_side)
            one, two = value[:, :n], value[:, n:]
            rows = pl.ds(u % 4 * 2 * n + shard * n, n)
            down[rows, pl.ds(0, n)] = jnp.where(c == 0, two, one).astype(bf16)
            own[u, shard] = jnp.where(c == 0, one, two).astype(bf16)
        for one in before:
            units.first_sum(one)
        units.core_copy(u).start()

    for r in range(2):
        make_pair(
            2 * r,
            lambda shard, h: mm_tn(
                active[:, cols_at(shard * 4 * n + h * 2 * n + r * n, n)], branch[...]
            ),
        )
    for p in range(2):
        make_pair(
            4 + 2 * p,
            lambda shard, h: mm_tn(
                hidden[:, shard * n : (shard + 1) * n], bend[:, cols_at(h * 4 * n + p * 2 * n, 2 * n)]
            ),
        )
        units.tick(p)

    @pl.loop(0, 2 * n // ROWS)
    def _(i):
        rows = rows_at(i * ROWS, ROWS)
        grad = mm_nt(bend[rows, :], up[...]) + second[rows, :]
        some = normed[rows, :]
        sums[3:4, :] += jnp.sum(grad * some, axis=0, keepdims=True)
        sums[4:5, :] += jnp.sum(grad, axis=0, keepdims=True)
        back = norm_back(grad, some, inverse[rows, 0:1], vecs[3:4, :])
        low_back = back.astype(bf16)
        second[rows, :] = back
        branch[rows, :] = low_back
        sums[2:3, :] += jnp.sum(low_back.astype(f32), axis=0, keepdims=True)
        slope[rows, :] = mm_nt(low_back, proj[...]).astype(bf16)

        @pl.when(i == 0)
        def _():
            units.first_sum(6)
            units.first_sum(7)

    units.tick(2)
    make_one(8, heads, branch[...], ())
    units.tick(3)
    place = lax.rem(lanes, DH)

    @pl.loop(0, pairs)
    def _(i):
        cols, key_cols, value_cols = [cols_at(part * D + i * PAIR, PAIR) for part in range(3)]
        query = qkv[:, cols] * SCALE
        grad = slope[:, cols]
        product = grad.astype(f32) * heads[:, cols].astype(f32)
        sides = []
        for number, side in enumerate((left, jnp.logical_not(left))):
            delta = three_parts(-jnp.sum(jnp.where(side, product, 0.0), axis=1, keepdims=True))
            logs = jnp.where(lanes == 2 * i + number, lse[...], 0.0)
            logs = three_parts(-jnp.sum(logs, axis=1, keepdims=True))
            more = jnp.where(place == 2, logs[0], jnp.where(place == 3, logs[1], logs[2]))
            more = jnp.where(place < 2, mq[...], jnp.where(place < 5, more, 0.0).astype(bf16))
            some_query = jnp.where(side, query, more)
            more = jnp.where(place == 0, delta[0], jnp.where(place == 1, delta[1], delta[2]))
            some_grad = jnp.where(side, grad, jnp.where(place < 3, more, 0.0).astype(bf16))
            sides.append((side, some_query, some_grad))
        totals = [None, None]
        for start in range(0, 2 * n, ROWS):
            rows = pl.ds(start, ROWS)
            keys, values = qkv[rows, key_cols], qkv[rows, value_cols]
            ones, zeros = jnp.ones_like(values), jnp.zeros_like(values)
            more_keys = jnp.where(place < 2, mk[rows, :], jnp.where(place < 5, ones, zeros))
            more_values = jnp.where(place < 3, ones, zeros)
            parts = []
            for number, (side, some_query, some_grad) in enumerate(sides):
                some_keys = jnp.where(side, keys, more_keys)
                some_values = jnp.where(side, values, more_values)
                probs = jnp.exp(mm_nt(some_keys, some_query))
                rate = (probs * mm_nt(some_values, some_grad)).astype(bf16)
                dv = mm(probs.astype(bf16), some_grad)
                dk = mm(rate, some_query)
                dq = mm_tn(rate, some_keys)
                totals[number] = dq if totals[number] is None else totals[number] + dq
                parts.append((dk, dv))
            active[rows, key_cols] = jnp.where(left, parts[0][0], parts[1][0]).astype(bf16)
            active[rows, value_cols] = jnp.where(left, parts[0][1], parts[1][1]).astype(bf16)
        active[:, cols] = (jnp.where(left, totals[0], totals[1]) * SCALE).astype(bf16)

        @pl.when(i == 0)
        def _():
            units.first_sum(8)

        @pl.when(i > 0)
        def _():
            units.tick(3 + i)

    for k in range(3):
        make_one(9 + k, x, active[:, k * D : (k + 1) * D], (8 + k,) if k else ())
        if k == 1:
            for u in range(2 * len(units.bits) + 1, 9):
                units.put_out(u - 2 * len(units.bits) - 1)
            units.tick(9)
    units.first_sum(11)
    sums[0:1, :] = jnp.sum(active[:, 0:D].astype(f32), axis=0, keepdims=True)
    sums[1:2, :] = jnp.sum(active[:, 2 * D : 3 * D].astype(f32), axis=0, keepdims=True)
    for i in range(up.shape[1] // D):
        sums[8 + i : 9 + i, :] = sums_up[:, i * D : (i + 1) * D]

    rounds = []
    ways = [here.across(1), here.over()] + [here.across(bit) for bit in units.bits]
    for k, way in enumerate(ways):
        rounds.append(copies.away(sums, others.at[k], way))
    rounds[0].start()

    @pl.loop(0, 2 * n // ROWS)
    def _(i):
        rows = rows_at(i * ROWS, ROWS)
        back = second[rows, :] + mm_nt(active[rows, 0 : 3 * D], three[...])
        hidden[rows, :] = back.astype(bf16)

    back_away.start()
    back_near.start()
    units.tick(10)
    last = UNITS + 2 * len(units.bits) + 1
    step = 0
    for t in range(11, last):
        units.tick(t)
        if step < len(rounds):
            rounds[step].wait()
            sums[...] += others[step]
            step += 1
            if step < len(rounds):
                rounds[step].start()
    while step < len(rounds):
        rounds[step].wait()
        sums[...] += others[step]
        step += 1
        if step < len(rounds):
            rounds[step].start()
    small[0:8, :] = sums[0:8, cols_at(y * n, n)]
    for i in range(wide):
        k = i * n // D
        from_row = 8 + wide // 2 * y + k
        small[8 + i : 9 + i, :] = sums[pl.ds(from_row, 1), i * n % D : i * n % D + n]
    small_out = copies.near(small, o_small)
    small_out.start()
    units.finish()
    small_out.wait()
    for copy in (layer_away, back_away):
        copy.wait()
    for copy in (layer_near, back_near):
        copy.wait()
    for part in g_three + [g_attn] + g_up:
        part.finish()
    for copy in (vec_away, x_away, s_away):
        copy.wait_send()


def run_layer(tokens, cotangent, seq, lines, b_up, weights, reps):
    n = weights[0].shape[0]
    count, wide = 2 * n, weights[4].shape[1]
    bits = reps.bit_length() - 2
    kinds = [
        ((2, n, D), bf16),
        ((2, n, D), bf16),
        ((4 * n, D), bf16),
        ((n, wide), bf16),
        ((n, D), bf16),
        ((n, D), bf16),
        ((n, D), bf16),
        ((n, D), bf16),
        ((16, n), f32),
    ]
    near = [((UNITS, max(16, n >> (k + 1)), n), bf16) for k in range(3)]
    scratch = [
        ((count, D), bf16),
        ((count, D), bf16),
        ((D, 3 * D), bf16),
        ((D, D), bf16),
        ((D, wide), bf16),
        ((wide, D), bf16),
        ((2, 16, n), f32),
        ((16, D), f32),
        ((1, wide), f32),
        ((count, 3 * D), bf16),
        ((count, D), bf16),
        ((count, PAIR), f32),
        ((count, PAIR), bf16),
        ((count, PAIR), bf16),
        ((count, D), f32),
        ((count, PAIR), f32),
        ((count, D), bf16),
        ((count, wide), bf16),
        ((count, wide), bf16),
        ((count, D), bf16),
        ((count, D), f32),
        ((count, D), bf16),
        ((16, D), f32),
        ((1, wide), f32),
        ((bits + 2, 16, D), f32),
        ((UNITS, 2, n, n), bf16),
        ((UNITS, n, n), bf16),
        *near,
        ((UNITS, 2, n, n), bf16),
        ((16, n), f32),
    ]
    anywhere = pl.BlockSpec(memory_space=pl.ANY)
    stages = 4 + 2 * bits
    return pl.pallas_call(
        layer_kernel,
        out_shape=[jax.ShapeDtypeStruct(*kind) for kind in kinds],
        in_specs=[anywhere, anywhere, pl.BlockSpec(memory_space=pltpu.SMEM)]
        + [pl.BlockSpec(memory_space=pltpu.VMEM)] * 9
        + [anywhere] * 6,
        out_specs=[anywhere] * len(kinds),
        scratch_shapes=[pltpu.VMEM(*kind) for kind in scratch]
        + [
            pltpu.SemaphoreType.DMA((80,)),
            pltpu.SemaphoreType.DMA((80,)),
            pltpu.SemaphoreType.DMA((stages, UNITS)),
            pltpu.SemaphoreType.DMA((stages, UNITS)),
            pltpu.SemaphoreType.REGULAR,
        ],
        compiler_params=pltpu.CompilerParams(
            collective_id=0, has_side_effects=True, vmem_limit_bytes=67043328
        ),
        name="encoder_layer",
    )(tokens, cotangent, seq, *lines, b_up, *weights)


def split_vectors(table, *outs):
    *lines, b_up = outs
    n = table.shape[1]
    for i, line in enumerate(lines):
        line[...] = table[i : i + 1, :].reshape(n)
    for i in range(b_up.shape[0] // n):
        b_up[pl.ds(i * n, n)] = table[8 + i : 9 + i, :].reshape(n)


def run_split(table, wide):
    n = table.shape[1]
    inside = pl.BlockSpec(memory_space=pltpu.VMEM)
    return pl.pallas_call(
        split_vectors,
        out_shape=[jax.ShapeDtypeStruct((n,), f32)] * 8 + [jax.ShapeDtypeStruct((wide * n,), f32)],
        in_specs=[inside],
        out_specs=[inside] * 9,
        name="split_vectors",
    )(table)


def general_body(
    tokens,
    cotangent,
    seq_lengths,
    w_query,
    b_query,
    w_key,
    w_value,
    b_value,
    w_attn,
    b_attn,
    norm_gain,
    norm_bias,
    w_up,
    b_up,
    w_down,
    b_down,
    out_gain,
    out_bias,
):
    at = Places()
    shards = at.shards
    micro, slots = tokens.shape[0], tokens.shape[1]
    span = shards // micro
    count = micro * slots
    x = spread(at, tokens)
    w_three = gather_rows(at, jnp.concatenate([w_query, w_key, w_value], axis=1))
    part = w_query.shape[0]
    wide = b_up.shape[0] // part
    vectors = jnp.concatenate(
        [
            jnp.stack(
                [b_query, b_value, b_attn, norm_gain, norm_bias, b_down, out_gain, out_bias]
            ),
            b_up.reshape(wide, part),
            jnp.zeros((16 - 8 - wide, part), bf16),
        ],
        axis=0,
    )
    table = put(jnp.zeros((shards,) + vectors.shape, bf16), vectors[None], at.shard)
    for step in range(1, shards):
        there = swap(vectors, "shard", shards, lambda i: (i + shards - step) % shards)
        table = put(table, there[None], (at.shard + step) % shards)
    table = table.astype(f32)
    (c_query, c_value, c_attn, c_gain, c_bias, c_down, c_out_gain, c_out_bias) = [
        table[:, i].reshape(1, D) for i in range(8)
    ]
    c_up = table[:, 8 : 8 + wide].reshape(1, D * wide)
    w_proj = gather_rows(at, w_attn)
    full_up = gather_rows(at, w_up)
    full_down = gather_rows(at, w_down)
    slope_in = spread(at, cotangent)

    group = slots * shards
    which, inner = at.shard // span, at.shard % span
    row = lax.dynamic_index_in_dim(seq_lengths[:, 0], which, 0, False)
    ids = segment_ids(row, group)

    def ids_of(device):
        parts = []
        for step in range(micro):
            source = micro * device + (which + micro - step) % micro
            parts.append(lax.dynamic_slice_in_dim(ids, source * slots, slots))
        return jnp.concatenate(parts)

    query_ids = ids_of(inner)
    nseq = seq_lengths.shape[-1] - 1
    valid = (query_ids < nseq).astype(f32)[:, None]
    three = mm(x, w_three) + jnp.concatenate([c_query, jnp.zeros_like(c_query), c_value], axis=1)
    three = three.astype(bf16)
    base = D // PAIR
    offsets = (base, 2 * base)
    key_array = three
    key_ids = [query_ids]
    if span > 1:
        offsets = (0, base)
        own = three[:, D:]
        parts = [own]
        for step in range(1, span):
            moves = [(i, i // span * span + (i + span - step) % span) for i in range(shards)]
            parts.append(lax.ppermute(own, "shard", moves))
            key_ids.append(ids_of((inner + step) % span))
        key_array = jnp.concatenate(parts, axis=0)
    mq, _ = mask_columns(query_ids)
    _, mk = mask_columns(jnp.concatenate(key_ids))
    attn, lse = attention_forward(three, key_array, offsets, mq, mk)

    normed_one, inverse_one = normalize(x.astype(f32) + mm(attn, w_proj) + c_attn)
    hidden = normed_one * c_gain + c_bias
    hidden_low = hidden.astype(bf16)
    pre = mm(hidden_low, full_up) + c_up
    lower = 0.5 * (1.0 + lax.erf(pre * 0.7071067811865476))
    active = (pre * lower).astype(bf16)
    density = jnp.exp(-0.5 * pre * pre) * 0.3989422804014327
    gelu_slope = lower + pre * density
    normed_two, inverse_two = normalize(hidden + mm(active, full_down) + c_down)
    layer = (normed_two * c_out_gain + c_out_bias).astype(bf16)
    grad_out = slope_in.astype(f32) * valid
    d_out_gain = jnp.sum(grad_out * normed_two, axis=0)
    d_out_bias = jnp.sum(grad_out, axis=0)
    grad_second = norm_back(grad_out, normed_two, inverse_two, c_out_gain)
    grad_branch = grad_second.astype(bf16)
    d_down = jnp.sum(grad_branch.astype(f32), axis=0)
    g_down = mm_tn(active, grad_branch)
    grad_pre = (mm_nt(grad_branch, full_down) * gelu_slope).astype(bf16)
    d_up = jnp.sum(grad_pre.astype(f32), axis=0)
    g_up = mm_tn(hidden_low, grad_pre)
    grad_hidden = mm_nt(grad_pre, full_up) + grad_second
    d_gain = jnp.sum(grad_hidden * normed_one, axis=0)
    d_bias = jnp.sum(grad_hidden, axis=0)
    grad_first = norm_back(grad_hidden, normed_one, inverse_one, c_gain)
    grad_proj = grad_first.astype(bf16)
    d_attn = jnp.sum(grad_proj.astype(f32), axis=0)
    g_attn = mm_tn(attn, grad_proj)
    grad_attn = mm_nt(grad_proj, w_proj).astype(bf16)
    dq, dk, dv = attention_backward(three, key_array, offsets, mq, mk, attn, lse, grad_attn)
    if span > 1:
        both = jnp.concatenate([dk, dv], axis=1)
        total = both[:count].astype(f32)
        for step in range(1, span):
            moves = [(i, i // span * span + (i + step) % span) for i in range(shards)]
            away = both[step * count : (step + 1) * count]
            total = total + lax.ppermute(away, "shard", moves).astype(f32)
        dk, dv = total[:, :D].astype(bf16), total[:, D:].astype(bf16)
    d_three = jnp.concatenate([dq, dk, dv], axis=1)
    d_query = jnp.sum(dq.astype(f32), axis=0)
    d_value = jnp.sum(dv.astype(f32), axis=0)
    g_three = mm_tn(x, d_three)
    back = (grad_first + mm_nt(d_three, w_three)).astype(bf16)

    sums = jnp.concatenate(
        [
            jnp.stack([d_query, d_value, d_attn, d_gain, d_bias, d_down, d_out_gain, d_out_bias]).reshape(
                8, shards, part
            ),
            d_up.reshape(shards, wide, part).transpose(1, 0, 2),
            jnp.zeros((PAIR - 8 - wide, shards, part), f32),
        ],
        axis=0,
    )
    sums = sums.reshape(PAIR, D).T
    r_down = reduce_rows(at, g_down)
    r_up = reduce_rows(at, g_up)
    r_attn = reduce_rows(at, g_attn)
    r_three = reduce_rows(at, jnp.concatenate([g_three, sums], axis=1))
    small = r_three[:, 3 * D :].T
    return (
        collect(at, layer, micro),
        collect(at, back, micro),
        r_three[:, :D],
        small[0],
        r_three[:, D : 2 * D],
        r_three[:, 2 * D : 3 * D],
        small[1],
        r_attn,
        small[2],
        small[3],
        small[4],
        r_up,
        small[8 : 8 + wide].reshape(wide * part),
        r_down,
        small[5],
        small[6],
        small[7],
    )


def body(tokens, cotangent, seq_lengths, *weights):
    shards, micro = lax.axis_size("shard"), tokens.shape[0]
    reps = lax.axis_size("rep")
    if shards != 2 or micro != 2 or reps not in (4, 8, 16):
        return general_body(tokens, cotangent, seq_lengths, *weights)
    (
        w_query,
        b_query,
        w_key,
        w_value,
        b_value,
        w_attn,
        b_attn,
        norm_gain,
        norm_bias,
        w_up,
        b_up,
        w_down,
        b_down,
        out_gain,
        out_bias,
    ) = weights
    part = w_query.shape[0]
    wide = b_up.shape[0] // part
    lines = [b_query, b_value, b_attn, norm_gain, norm_bias, b_down, out_gain, out_bias]
    layer, back, *grads, small = run_layer(
        tokens,
        cotangent,
        seq_lengths,
        lines,
        b_up,
        (w_query, w_key, w_value, w_attn, w_up, w_down),
        reps,
    )
    g_down, g_up, g_attn, g_query, g_key, g_value = [grad.astype(f32) for grad in grads]
    d_query, d_value, d_attn, d_gain, d_bias, d_down, d_out_gain, d_out_bias, d_up = run_split(small, wide)
    return (
        layer,
        back,
        g_query,
        d_query,
        g_key,
        g_value,
        d_value,
        g_attn,
        d_attn,
        d_gain,
        d_bias,
        g_up,
        d_up,
        g_down,
        d_down,
        d_out_gain,
        d_out_bias,
    )


def solution(mesh):
    rows, vector = P("shard", None), P("shard")
    tokens = P(None, ("rep", "shard"), None)
    weights = (rows, vector, rows, rows, vector, rows, vector, vector, vector)
    weights += (rows, vector, rows, vector, vector, vector)
    return jax.shard_map(
        body,
        mesh=mesh,
        in_specs=(tokens, tokens, P(None, "rep", None)) + weights,
        out_specs=(tokens, tokens) + weights,
        check_vma=False,
    )
```

```python
import functools

import jax
import jax.numpy as jnp
from jax import lax
from jax.experimental import pallas as pl
from jax.experimental.pallas import tpu as pltpu
from jax.sharding import PartitionSpec as P

D = 768
H = 12
DH = 64
PAIR = 2 * DH
EPS = 1e-12
BIG = 1e30
SCALE = DH ** (-0.5)
ROWS = 256
f32 = jnp.float32
bf16 = jnp.bfloat16


def mm(left, right):
    return jnp.dot(left, right, preferred_element_type=f32)


def mm_nt(left, right):
    return lax.dot_general(left, right, (((1,), (1,)), ((), ())), preferred_element_type=f32)


def mm_tn(left, right):
    return lax.dot_general(left, right, (((0,), (0,)), ((), ())), preferred_element_type=f32)


def segment_ids(row, count):
    bounds = jnp.cumsum(row[:-1])
    places = jnp.arange(count, dtype=jnp.int32)
    return jnp.sum((places[:, None] >= bounds[None, :]).astype(jnp.int32), axis=1)


def mask_columns(ids):
    first = (ids == 0).astype(f32)[:, None]
    other = 1.0 - first
    lane = lax.broadcasted_iota(jnp.int32, (1, PAIR), 1) % DH
    on_query = jnp.where(lane == 0, -BIG * first, jnp.where(lane == 1, -BIG * other, 0.0))
    on_key = jnp.where(lane == 0, other, jnp.where(lane == 1, first, 0.0))
    return on_query.astype(bf16), on_key.astype(bf16)


def forward_heads(q_ref, k_ref, v_ref, mq_ref, mk_ref, attn_ref, lse_ref):
    lane = lax.broadcasted_iota(jnp.int32, (1, PAIR), 1)
    low = lane < DH
    keys, values, mk = k_ref[...], v_ref[...], mk_ref[...]
    one = jnp.ones_like(values)
    sides = []
    for own in (low, jnp.logical_not(low)):
        sides.append((own, jnp.where(own, keys, mk), jnp.where(own, values, one)))
    count = q_ref.shape[0]
    block = min(ROWS, count)
    for start in range(0, count, block):
        rows = pl.ds(start, block)
        query, mq = q_ref[rows, :] * SCALE, mq_ref[rows, :]
        outs = []
        for own, some_keys, some_values in sides:
            scores = mm_nt(jnp.where(own, query, mq), some_keys)
            top = jnp.max(scores, axis=1, keepdims=True)
            expo = jnp.exp(scores - top).astype(bf16)
            mixed = mm(expo, some_values)
            total = pltpu.roll(mixed, DH, 1)
            outs.append((mixed / total, top + jnp.log(total)))
        attn_ref[rows, :] = jnp.where(low, outs[0][0], outs[1][0]).astype(bf16)
        lse_ref[rows, :] = jnp.where(low, outs[0][1], outs[1][1])


def three_parts(value):
    first = value.astype(bf16).astype(f32)
    rest = value - first
    second = rest.astype(bf16).astype(f32)
    return first, second, rest - second


def backward_heads(
    q_ref, k_ref, v_ref, mq_ref, mk_ref, attn_ref, lse_ref, grad_ref, dq_ref, dk_ref, dv_ref
):
    lane = lax.broadcasted_iota(jnp.int32, (1, PAIR), 1)
    place = lane % DH
    low = lane < DH
    query, mq, grad = q_ref[...] * SCALE, mq_ref[...], grad_ref[...]
    product = grad.astype(f32) * attn_ref[...].astype(f32)
    lse = three_parts(-pltpu.roll(lse_ref[...], DH, 1))
    count_keys = k_ref.shape[0]
    block = min(ROWS, count_keys)
    sides = []
    for own in (low, jnp.logical_not(low)):
        delta = three_parts(-jnp.sum(jnp.where(own, product, 0.0), axis=1, keepdims=True))
        more = jnp.where(place == 2, lse[0], jnp.where(place == 3, lse[1], lse[2]))
        more = jnp.where(place < 2, mq, jnp.where(place < 5, more, 0.0).astype(bf16))
        some_query = jnp.where(own, query, more)
        more = jnp.where(place == 0, delta[0], jnp.where(place == 1, delta[1], delta[2]))
        some_grad = jnp.where(own, grad, jnp.where(place < 3, more, 0.0).astype(bf16))
        sides.append((own, some_query, some_grad, None))
    totals = [None, None]
    for start in range(0, count_keys, block):
        rows = pl.ds(start, block)
        keys, values, mk = k_ref[rows, :], v_ref[rows, :], mk_ref[rows, :]
        ones = jnp.ones_like(values)
        zeros = jnp.zeros_like(values)
        more_keys = jnp.where(place < 2, mk, jnp.where(place < 5, ones, zeros))
        more_values = jnp.where(place < 3, ones, zeros)
        parts = []
        for side in range(2):
            own, some_query, some_grad, _ = sides[side]
            some_keys = jnp.where(own, keys, more_keys)
            some_values = jnp.where(own, values, more_values)
            probs = jnp.exp(mm_nt(some_keys, some_query))
            slope = (probs * mm_nt(some_values, some_grad)).astype(bf16)
            dv = mm(probs.astype(bf16), some_grad)
            dk = mm(slope, some_query)
            dq = mm_tn(slope, some_keys)
            totals[side] = dq if totals[side] is None else totals[side] + dq
            parts.append((dk, dv))
        dk_ref[rows, :] = jnp.where(low, parts[0][0], parts[1][0]).astype(bf16)
        dv_ref[rows, :] = jnp.where(low, parts[0][1], parts[1][1]).astype(bf16)
    dq_ref[...] = (jnp.where(low, totals[0], totals[1]) * SCALE).astype(bf16)


def head_block(rows, offset):
    return pl.BlockSpec((rows, PAIR), lambda i: (0, i + offset))


def fixed_block(rows):
    return pl.BlockSpec((rows, PAIR), lambda i: (0, 0))


def attention_forward(query_array, key_array, offsets, mq, mk):
    count, keys = query_array.shape[0], key_array.shape[0]
    pairs = H * DH // PAIR
    return pl.pallas_call(
        forward_heads,
        grid=(pairs,),
        out_shape=(
            jax.ShapeDtypeStruct((count, D), bf16),
            jax.ShapeDtypeStruct((count, D), f32),
        ),
        in_specs=[
            head_block(count, 0),
            head_block(keys, offsets[0]),
            head_block(keys, offsets[1]),
            fixed_block(count),
            fixed_block(keys),
        ],
        out_specs=(head_block(count, 0), head_block(count, 0)),
        cost_estimate=pl.CostEstimate(
            flops=16 * count * keys * D, bytes_accessed=8 * (count + keys) * D, transcendentals=count * keys * H
        ),
        name="attention_forward",
    )(query_array, key_array, key_array, mq, mk)


def attention_backward(query_array, key_array, offsets, mq, mk, attn, lse, grad):
    count, keys = query_array.shape[0], key_array.shape[0]
    pairs = H * DH // PAIR
    return pl.pallas_call(
        backward_heads,
        grid=(pairs,),
        out_shape=(
            jax.ShapeDtypeStruct((count, D), bf16),
            jax.ShapeDtypeStruct((keys, D), bf16),
            jax.ShapeDtypeStruct((keys, D), bf16),
        ),
        in_specs=[
            head_block(count, 0),
            head_block(keys, offsets[0]),
            head_block(keys, offsets[1]),
            fixed_block(count),
            fixed_block(keys),
            head_block(count, 0),
            head_block(count, 0),
            head_block(count, 0),
        ],
        out_specs=(head_block(count, 0), head_block(keys, 0), head_block(keys, 0)),
        cost_estimate=pl.CostEstimate(
            flops=40 * count * keys * D, bytes_accessed=16 * (count + keys) * D, transcendentals=count * keys * H
        ),
        name="attention_backward",
    )(query_array, key_array, key_array, mq, mk, attn, lse, grad)


def normalize(rows):
    mean = jnp.mean(rows, axis=-1, keepdims=True)
    centered = rows - mean
    inverse = lax.rsqrt(jnp.mean(centered * centered, axis=-1, keepdims=True) + EPS)
    return centered * inverse, inverse


def norm_back(grad, normed, inverse, gain):
    scaled = grad * gain
    first = jnp.mean(scaled, axis=-1, keepdims=True)
    second = jnp.mean(scaled * normed, axis=-1, keepdims=True)
    return inverse * (scaled - first - normed * second)


def swap(value, axis, size, move):
    return lax.ppermute(value, axis, [(i, move(i)) for i in range(size)])


def put(buffer, value, index, axis=0):
    return lax.dynamic_update_slice_in_dim(buffer, value, index * value.shape[axis], axis)


def pick(value, index, parts, axis=0):
    size = value.shape[axis] // parts
    return lax.dynamic_slice_in_dim(value, index * size, size, axis)


class Places:
    def __init__(self):
        self.reps = lax.axis_size("rep")
        self.shards = lax.axis_size("shard")
        self.rep = lax.axis_index("rep")
        self.shard = lax.axis_index("shard")
        self.core = self.rep % 2


def gather_rows(at, own):
    half = own.shape[0] // 2
    out = jnp.zeros((at.shards * own.shape[0],) + own.shape[1:], own.dtype)
    out = put(out, own, at.shard)
    mine = pick(own, at.core, 2)
    for step in range(1, at.shards):
        there = swap(mine, "shard", at.shards, lambda i: (i + at.shards - step) % at.shards)
        other = swap(there, "rep", at.reps, lambda i: i ^ 1)
        block = (at.shard + step) % at.shards * 2
        out = put(out, there, block + at.core)
        out = put(out, other, block + 1 - at.core)
    return out


def reduce_rows(at, grad):
    shards, columns = at.shards, grad.shape[1]
    rows = grad.shape[0] // shards
    value = grad.reshape(shards * 2, rows // 2, columns)
    value = grad.reshape(shards, 2, rows // 2, columns)
    mine = lax.dynamic_index_in_dim(value, at.core, 1, False)
    away = lax.dynamic_index_in_dim(value, 1 - at.core, 1, False).astype(bf16)
    value = mine.astype(f32) + swap(away, "rep", at.reps, lambda i: i ^ 1).astype(f32)
    total = lax.dynamic_index_in_dim(value, at.shard, 0, False)
    for step in range(1, shards):
        away = lax.dynamic_index_in_dim(value, (at.shard + step) % shards, 0, False).astype(bf16)
        total = total + swap(away, "shard", shards, lambda i: (i + step) % shards).astype(f32)
    stages = []
    bit = 2
    while bit < at.reps:
        axis = 0 if total.shape[0] % 32 == 0 else 1
        stages.append((bit, axis))
        up = (at.rep // bit) % 2
        mine, away = pick(total, up, 2, axis), pick(total, 1 - up, 2, axis).astype(bf16)
        move = functools.partial(lambda b, i: i ^ b, bit)
        total = mine + swap(away, "rep", at.reps, move).astype(f32)
        bit *= 2
    total = total.astype(bf16)
    for bit, axis in reversed(stages):
        up = (at.rep // bit) % 2
        move = functools.partial(lambda b, i: i ^ b, bit)
        other = swap(total, "rep", at.reps, move)
        shape = list(total.shape)
        shape[axis] *= 2
        both = jnp.zeros(shape, bf16)
        total = put(put(both, total, up, axis), other, 1 - up, axis)
    other = swap(total, "rep", at.reps, lambda i: i ^ 1)
    first = jnp.where(at.core == 0, total, other)
    second = jnp.where(at.core == 0, other, total)
    return jnp.concatenate([first, second], axis=0).astype(f32)


def spread(at, value):
    micro, shards = value.shape[0], at.shards
    parts = []
    for step in range(micro):
        moves = [(i, (i + step) % micro * (shards // micro) + i // micro) for i in range(shards)]
        part = lax.dynamic_index_in_dim(value, (at.shard + step) % micro, 0, False)
        if any(a != b for a, b in moves):
            part = lax.ppermute(part, "shard", moves)
        parts.append(part)
    return jnp.concatenate(parts, axis=0)


def collect(at, value, micro):
    shards = at.shards
    slots = value.shape[0] // micro
    out = jnp.zeros((micro, slots) + value.shape[1:], value.dtype)
    for step in range(micro):
        moves = [((i + step) % micro * (shards // micro) + i // micro, i) for i in range(shards)]
        part = value[step * slots : (step + 1) * slots]
        if any(a != b for a, b in moves):
            part = lax.ppermute(part, "shard", moves)
        out = lax.dynamic_update_index_in_dim(out, part, (at.shard + step) % micro, 0)
    return out


def rows_at(start, size):
    return pl.ds(pl.multiple_of(start, 16), size)


def cols_at(start, size):
    return pl.ds(pl.multiple_of(start, PAIR), size)


class Here:
    def __init__(self):
        self.rep = lax.axis_index("rep")
        self.y = lax.axis_index("shard")
        self.core = lax.rem(self.rep, 2)
        self.x = lax.rem(lax.div(self.rep, 2), 2)

    def up(self, bit):
        return lax.rem(lax.div(self.rep, bit), 2)

    def across(self, bit):
        return {"rep": self.rep + bit * (1 - 2 * self.up(bit))}

    def over(self):
        return {"shard": 1 - self.y}


class Copies:
    def __init__(self, send, recv):
        self.send, self.recv, self.used, self.open = send, recv, 0, []

    def away(self, source, target, peer):
        k = self.used
        self.used += 1
        copy = pltpu.make_async_remote_copy(
            src_ref=source,
            dst_ref=target,
            send_sem=self.send.at[k],
            recv_sem=self.recv.at[k],
            device_id=peer,
            device_id_type=pl.DeviceIdType.MESH,
        )
        return copy

    def near(self, source, target):
        k = self.used
        self.used += 1
        return pltpu.make_async_copy(source, target, self.recv.at[k])


def greet(peers):
    barrier = pltpu.get_barrier_semaphore()
    for peer in peers:
        pl.semaphore_signal(barrier, inc=1, device_id=peer, device_id_type=pl.DeviceIdType.MESH)
    pl.semaphore_wait(barrier, len(peers))


class Gathered:
    def __init__(self, here, copies, own, full, mine, other, n, cols, bits):
        def at(start, size):
            return full.at[rows_at(start, size), cols]

        def held(level):
            start, size = here.core * (n // 2), n // 2
            for bit in reversed(bits[level:]):
                size //= 2
                start = start + here.up(bit) * size
            return start, size

        start, size = held(0)
        self.local = copies.near(own(0, n), at(mine, n))
        self.hops = [copies.away(own(start, size), at(mine + start, size), here.over())]
        for level, bit in enumerate(list(bits) + [1]):
            start, size = held(level)
            part = at(other + start, size)
            self.hops.append(copies.away(part, part, here.across(bit)))
        self.progress = 0

    def start(self):
        self.hops[0].start()
        self.local.start()

    def step(self):
        if self.progress + 1 < len(self.hops):
            self.hops[self.progress].wait_recv()
            self.progress += 1
            self.hops[self.progress].start()

    def ready(self):
        while self.progress + 1 < len(self.hops):
            self.step()
        self.local.wait()
        self.hops[-1].wait_recv()

    def finish(self):
        for copy in self.hops:
            copy.wait_send()


def gelu_parts(pre):
    lower = 0.5 * (1.0 + lax.erf(pre * 0.7071067811865476))
    density = jnp.exp(-0.5 * pre * pre) * 0.3989422804014327
    return pre * lower, lower + pre * density


UNITS = 12
WAYS = (1, 0, 1, 0, 1, 2, 1, 0, 0, 0, 0, 0)
PLAN = (
    (3, 4),
    (5, 3, 6, 4),
    (7, 5, 8),
    (9, 3, 4, 10, 6),
    (7, 11, 9, 5),
    (8, 6, 10),
    (11, 7),
    (8,),
    (9, 10),
    (11,),
    (),
    (),
    (),
    (),
    (22, 23),
    (21, 20),
    (22, 25),
    (21, 24, 20),
    (22, 23),
    (27, 21, 20, 25),
    (22, 23, 26, 24, 21, 27),
    (20, 25, 22, 28, 23),
    (24, 21, 26, 27, 28),
    (20, 25, 22, 21),
    (21, 23, 24, 20, 26),
    (20,),
    (27, 22, 28),
    (25, 23, 22),
    (24, 25, 40, 26),
    (29, 27),
    (23, 28),
    (24, 23, 29, 25, 30, 25, 26, 24, 27, 24, 28, 30, 29, 31, 26, 40, 27, 28, 27, 30, 31, 29, 26, 30, 31, 40, 26, 29, 28, 30, 28, 31, 40, 29, 30, 31, 29, 40, 29, 31, 30, 30, 31, 31),
    (),
    (),
    (20, 21),
)


class Units:
    def __init__(self, here, reps, send, recv, swap_buffer, own, far, near, done, result):
        self.here, self.send, self.recv = here, send, recv
        self.swap_buffer, self.own, self.far, self.near, self.done = swap_buffer, own, far, near, done
        self.result = result
        self.n = own.shape[4]
        self.all_bits = []
        bit = 2
        while bit < reps:
            self.all_bits.append(bit)
            bit *= 2
        self.progress = [0] * UNITS
        self.stages = 3 + 2 * len(self.all_bits)

    def bits(self, u):
        bits = list(self.all_bits)
        if WAYS[u] == 2 and len(bits) > 1:
            bits[0], bits[1] = bits[1], bits[0]
        return bits

    def copy(self, stage, u, source, target, peer):
        return pltpu.make_async_remote_copy(
            src_ref=source,
            dst_ref=target,
            send_sem=self.send.at[stage, u],
            recv_sem=self.recv.at[stage, u],
            device_id=peer,
            device_id_type=pl.DeviceIdType.MESH,
        )

    def slot(self, u, side):
        n = self.n
        if u < 4:
            return (self.done, self.own)[side].at[UNITS - 4 + u]
        return self.swap_buffer.at[pl.ds(u % 4 * 2 * n, 2 * n), pl.ds(side * n, n)]

    def lay(self, u, shard, value):
        n = self.n
        if u < 4:
            for part in range(2):
                rows = value[part * (n // 2) : (part + 1) * (n // 2), :]
                self.done[UNITS - 4 + u, shard, part] = rows.astype(bf16)
        else:
            rows = pl.ds(u % 4 * 2 * n + shard * n, n)
            self.swap_buffer[rows, pl.ds(0, n)] = value.astype(bf16)

    def theirs(self, u, shard, part):
        n = self.n
        if u < 4:
            return self.own[UNITS - 4 + u, shard, part]
        rows = rows_at(u % 4 * 2 * n + shard * n + part * (n // 2), n // 2)
        return self.swap_buffer[rows, pl.ds(n, n)]

    def core_copy(self, u):
        return self.copy(0, u, self.slot(u, 0), self.slot(u, 1), self.here.across(1))

    def away_copy(self, k, u):
        y, own, here = self.here.y, self.own, self.here
        bits = self.bits(u)
        up = here.up(bits[0])
        first_y = WAYS[u] == 0
        if k == 0 and first_y:
            return self.copy(1, u, own.at[u, 1 - y], self.far.at[u], here.over())
        if k == 0:
            return self.copy(1, u, own.at[u, :, 1 - up], self.far.at[u], here.across(bits[0]))
        if k == 1 and first_y:
            return self.copy(2, u, own.at[u, y, 1 - up], self.near[0].at[u], here.across(bits[0]))
        if k == 1:
            return self.copy(2, u, own.at[u, 1 - y, up], self.near[0].at[u], here.over())
        start, size = self.inner(u, k - 2)
        half = size // 2
        rows = rows_at(start + (1 - here.up(bits[k - 1])) * half, half)
        return self.copy(
            1 + k, u, own.at[u, y, up, rows, :], self.near[k - 1].at[u], here.across(bits[k - 1])
        )

    def inner(self, u, level):
        size, start = self.n // 2, 0
        for bit in self.bits(u)[1 : 1 + level]:
            size //= 2
            start = start + self.here.up(bit) * size
        return start, size

    def back_copy(self, k, u):
        bits = self.bits(u)
        level = len(bits) - k
        piece = self.done.at[u, self.here.core]
        bit = bits[level - 1] if level else 1
        if level:
            start, size = self.inner(u, level - 1)
            piece = self.done.at[u, self.here.core, self.here.up(bits[0]), rows_at(start, size), :]
        return self.copy(2 + len(bits) + k, u, piece, piece, self.here.across(bit))

    def out_copies(self, u):
        n = self.n
        down, up, *square = self.result
        for h in range(2):
            for part in range(2):
                rows = part * (n // 2)
                if u < 4:
                    place = down.at[pl.ds(h * 2 * n + u // 2 * n + rows, n // 2), pl.ds(u % 2 * n, n)]
                elif u < 8:
                    place = up.at[pl.ds(rows, n // 2), pl.ds(h * 4 * n + (u - 4) * n, n)]
                else:
                    place = square[u - 8].at[pl.ds(rows, n // 2), pl.ds(h * n, n)]
                yield pltpu.make_async_copy(
                    self.done.at[u, h, part], place, (self.send, self.recv)[h].at[self.stages + part, u]
                )

    def keep(self, u, shard, value):
        half = self.n // 2
        for part in range(2):
            self.own[u, shard, part] = value[part * half : (part + 1) * half, :].astype(bf16)

    def first_sum(self, u):
        y = self.here.y
        up = self.here.up(self.bits(u)[0])
        self.core_copy(u).wait_recv()
        if WAYS[u] == 0:
            order = [(1 - y, 0), (1 - y, 1), (y, 0), (y, 1)]
        else:
            order = [(0, 1 - up), (1, 1 - up), (0, up), (1, up)]
        for number, (shard, part) in enumerate(order):
            theirs = self.theirs(u, shard, part).astype(f32)
            self.own[u, shard, part] = (self.own[u, shard, part].astype(f32) + theirs).astype(bf16)
            if number == 1:
                self.away_copy(0, u).start()

    def step(self, u):
        bits = len(self.all_bits)
        k = self.progress[u]
        if k > 2 * bits + 1:
            return
        self.progress[u] = k + 1
        y, own = self.here.y, self.own
        up = self.here.up(self.bits(u)[0])
        if k <= bits:
            self.away_copy(k, u).wait_recv()
        if k == 0:
            if WAYS[u] == 0:
                order = [((y, 1 - up), 1 - up), ((y, up), up)]
            else:
                order = [((1 - y, up), 1 - y), ((y, up), y)]
            for number, ((shard, part), source) in enumerate(order):
                theirs = self.far[u, source].astype(f32)
                own[u, shard, part] = (own[u, shard, part].astype(f32) + theirs).astype(bf16)
                if number == 0:
                    self.away_copy(1, u).start()
        elif k < bits:
            start, size = self.inner(u, k - 1)
            half = size // 2
            side = self.here.up(self.bits(u)[k])
            for number, part in enumerate((1 - side, side)):
                rows = rows_at(start + part * half, half)
                theirs = self.near[k - 1][u, rows_at(part * half, half), :].astype(f32)
                own[u, y, up, rows, :] = (own[u, y, up, rows, :].astype(f32) + theirs).astype(bf16)
                if number == 0:
                    self.away_copy(k + 1, u).start()
        elif k == bits:
            start, size = self.inner(u, k - 1)
            total = own[u, y, up, rows_at(start, size), :].astype(f32)
            total = total + self.near[k - 1][u].astype(f32)
            self.done[u, self.here.core, up, rows_at(start, size), :] = total.astype(bf16)
            self.back_copy(0, u).start()
        else:
            self.back_copy(k - bits - 1, u).wait_recv()
            if k <= 2 * bits:
                self.back_copy(k - bits, u).start()
            else:
                for copy in self.out_copies(u):
                    copy.start()

    def finish(self):
        for u in range(UNITS):
            while self.progress[u] <= 2 * len(self.all_bits) + 1:
                self.step(u)
        for u in range(UNITS):
            if u >= UNITS - 4:
                self.core_copy(u).wait_send()
            for k in range(len(self.all_bits) + 1):
                self.away_copy(k, u).wait_send()
                self.back_copy(k, u).wait_send()
            for copy in self.out_copies(u):
                copy.wait()


def layer_kernel(
    tokens,
    cotangent,
    seq,
    *rest,
):
    lines, b_up, weights = rest[:8], rest[8], rest[9:15]
    layer_steps(tokens, cotangent, seq, lines, b_up, *weights, rest[15:24], *rest[24:])


def layer_steps(
    tokens,
    cotangent,
    seq,
    lines,
    b_up,
    w_query,
    w_key,
    w_value,
    w_attn,
    w_up,
    w_down,
    outs,
    x,
    slope,
    three,
    proj,
    up,
    down,
    raw_vectors,
    vecs,
    vec_up,
    qkv,
    heads,
    lse,
    mq,
    mk,
    normed,
    inverse,
    hidden,
    active,
    bend,
    branch,
    second,
    layer,
    sums,
    sums_up,
    others,
    own,
    far,
    near_x,
    near_z,
    near_w,
    done,
    small,
    send,
    recv,
    unit_send,
    unit_recv,
    free,
):
    reps = lax.axis_size("rep")
    here = Here()
    copies = Copies(send, recv)
    n = w_query.shape[0]
    y = here.y
    near = (near_x, near_z, near_w)
    o_layer, o_back, *o_grads, o_small = outs
    units = Units(here, reps, unit_send, unit_recv, down, own, far, near, done, o_grads)
    peers = [here.over(), here.across(1)] + [here.across(bit) for bit in units.all_bits]
    greet(peers)

    wide = up.shape[1] // (2 * n)

    pieces = []

    def piece(weight, full, row, col, into):
        def own(start, size):
            return weight.at[rows_at(row + start, size), pl.ds(col, D)]

        rows = weight.shape[0]
        bits = units.all_bits[:2]
        pieces.append(
            Gathered(
                here,
                copies,
                own,
                full,
                y * rows + row,
                (1 - y) * rows + row,
                n,
                pl.ds(into + col, D),
                bits if len(pieces) % 2 == 0 else bits[::-1],
            )
        )
        return pieces[-1]

    g_three = [piece(w, three, 0, 0, k * D) for k, w in enumerate((w_query, w_key, w_value))]
    g_attn = piece(w_attn, proj, 0, 0, 0)
    g_up = [piece(w_up, up, 0, k * D, 0) for k in range(up.shape[1] // D)]
    g_down = [piece(w_down, down, k * n, 0, 0) for k in range(w_down.shape[0] // n)]
    vec_away = copies.away(raw_vectors.at[y], raw_vectors.at[y], here.over())
    low, high = pl.ds(0, n), pl.ds(n, n)
    x_away = copies.away(tokens.at[1 - y], x.at[high, :], here.over())
    x_near = copies.near(tokens.at[y], x.at[low, :])
    s_away = copies.away(cotangent.at[1 - y], slope.at[high, :], here.over())
    s_near = copies.near(cotangent.at[y], slope.at[low, :])
    layer_away = copies.away(layer.at[high, :], o_layer.at[y], here.over())
    layer_near = copies.near(layer.at[low, :], o_layer.at[y])
    back_away = copies.away(hidden.at[high, :], o_back.at[y], here.over())
    back_near = copies.near(hidden.at[low, :], o_back.at[y])
    x_near.start()
    for part in g_three:
        part.start()
    for i, line in enumerate(lines):
        raw_vectors[y, i : i + 1, :] = line[...].astype(f32).reshape(1, n)
    for i in range(wide):
        raw_vectors[y, 8 + i : 9 + i, :] = b_up[i * n : (i + 1) * n].astype(f32).reshape(1, n)
    vec_away.start()
    x_away.start()
    for part in [g_attn] + g_up + g_down:
        part.start()
    s_away.start()
    s_near.start()

    length = seq[y, 0, 0]

    def inside(start, size):
        row = start + lax.broadcasted_iota(jnp.int32, (size, 1), 0)
        place = row + jnp.where(row < n, y * n, -y * n)
        return (place < length).astype(f32)

    first = inside(0, 2 * n)
    lane = lax.rem(lax.broadcasted_iota(jnp.int32, (1, PAIR), 1), DH)
    mq[...] = jnp.where(
        lane == 0, -BIG * first, jnp.where(lane == 1, -BIG * (1.0 - first), 0.0)
    ).astype(bf16)
    mk[...] = jnp.where(lane == 0, 1.0 - first, jnp.where(lane == 1, first, 0.0)).astype(bf16)
    sums[...] = jnp.zeros_like(sums)
    lse[...] = jnp.zeros_like(lse)

    for _ in range(3):
        for part in g_three:
            part.step()
    vec_away.wait_recv()
    for half in range(2):
        table = raw_vectors[half]
        vecs[:, half * n : (half + 1) * n] = table
        for i in range(wide):
            start = half * wide * n + i * n
            vec_up[:, start : start + n] = table[8 + i : 9 + i, :]
    for part in g_three:
        part.ready()
    x_near.wait()
    tile = 256

    @pl.loop(0, 2)
    def _(half):
        pl.when(half == 1)(x_away.wait_recv)
        rows = rows_at(half * n, n)

        @pl.loop(0, 3 * D // tile)
        def _(i):
            cols = cols_at(i * tile, tile)
            which = lax.div(i, D // tile)
            inner = cols_at(lax.rem(i, D // tile) * tile, tile)
            bias = jnp.where(
                which == 0, vecs[0:1, inner], jnp.where(which == 2, vecs[1:2, inner], 0.0)
            )
            qkv[rows, cols] = (mm(x[rows, :], three[:, cols]) + bias).astype(bf16)

    rounds = []
    ways = [here.across(1), here.over()] + [here.across(bit) for bit in units.all_bits]
    for k, way in enumerate(ways):
        rounds.append(copies.away(sums, others.at[k], way))
    round_done = [0]

    def next_round():
        k = round_done[0]
        if k < len(rounds):
            round_done[0] = k + 1
            rounds[k].wait()
            sums[...] += others[k]
            if k + 1 < len(rounds):
                rounds[k + 1].start()

    def visit(place):
        for one in PLAN[place]:
            if one == 40:
                next_round()
            elif one >= 20:
                units.step(one - 20)
            else:
                pieces[one].step()

    def visit_one_of(i, places):
        for number, place in enumerate(places):

            @pl.when(i == number)
            def _():
                visit(place)

    visit(0)
    lanes = lax.broadcasted_iota(jnp.int32, (1, PAIR), 1)
    left = lanes < DH
    pairs = H * DH // PAIR

    @pl.loop(0, pairs)
    def _(i):
        keys, values = qkv[:, cols_at(D + i * PAIR, PAIR)], qkv[:, cols_at(2 * D + i * PAIR, PAIR)]
        one = jnp.ones_like(values)
        sides = []
        for side in (left, jnp.logical_not(left)):
            sides.append((side, jnp.where(side, keys, mk[...]), jnp.where(side, values, one)))
        for start in range(0, 2 * n, ROWS):
            rows = pl.ds(start, ROWS)
            query = qkv[rows, cols_at(i * PAIR, PAIR)] * SCALE
            outs = []
            total_lse = lse[rows, :]
            for number, (side, some_keys, some_values) in enumerate(sides):
                scores = mm_nt(jnp.where(side, query, mq[rows, :]), some_keys)
                top = jnp.max(scores, axis=1, keepdims=True)
                expo = jnp.exp(scores - top).astype(bf16)
                mixed = mm(expo, some_values)
                total = pltpu.roll(mixed, DH, 1)
                outs.append(mixed / total)
                sum_all = jnp.where(side, total, mixed)
                total_lse = jnp.where(lanes == 2 * i + number, top + jnp.log(sum_all), total_lse)
            lse[rows, :] = total_lse
            heads[rows, cols_at(i * PAIR, PAIR)] = jnp.where(left, outs[0], outs[1]).astype(bf16)

        visit_one_of(i, range(1, 7))

    g_attn.ready()

    @pl.loop(0, 2 * n // ROWS)
    def _(i):
        rows = rows_at(i * ROWS, ROWS)
        resid = x[rows, :].astype(f32) + mm(heads[rows, :], proj[...]) + vecs[2:3, :]
        some, scale = normalize(resid)
        normed[rows, :] = some
        inverse[rows, :] = jnp.broadcast_to(scale, (ROWS, PAIR))
        hidden[rows, :] = (some * vecs[3:4, :] + vecs[4:5, :]).astype(bf16)

    visit(7)
    for number, part in enumerate(g_up):
        part.ready()

        @pl.loop(number * D // tile, (number + 1) * D // tile)
        def _(i):
            cols = cols_at(i * tile, tile)
            pre = mm(hidden[...], up[:, cols]) + vec_up[:, cols]
            value, rate = gelu_parts(pre)
            active[:, cols] = value.astype(bf16)
            bend[:, cols] = rate.astype(bf16)

        visit(8 + number)

    for part in g_down:
        part.ready()
    s_away.wait_recv()
    s_near.wait()

    @pl.loop(0, 2 * n // ROWS)
    def _(i):
        rows = rows_at(i * ROWS, ROWS)
        resid = mm(active[rows, :], down[...]) + vecs[5:6, :]
        resid = resid + (normed[rows, :] * vecs[3:4, :] + vecs[4:5, :])
        some, scale = normalize(resid)
        layer[rows, :] = (some * vecs[6:7, :] + vecs[7:8, :]).astype(bf16)
        grad = slope[rows, :].astype(f32) * inside(i * ROWS, ROWS)
        back = norm_back(grad, some, scale, vecs[6:7, :])
        low_back = back.astype(bf16)
        second[rows, :] = back
        branch[rows, :] = low_back
        sums[5:6, :] += jnp.sum(low_back.astype(f32), axis=0, keepdims=True)
        sums[6:7, :] += jnp.sum(grad * some, axis=0, keepdims=True)
        sums[7:8, :] += jnp.sum(grad, axis=0, keepdims=True)

    c = here.core

    def make_pair(u, block, before):
        for one in (u, u + 1):
            if one >= 4:
                units.core_copy(one - 4).wait_send()
        for shard in range(2):
            value = block(shard, 1 - c)
            for k in range(2):
                units.lay(u + k, shard, value[:, k * n : (k + 1) * n])
        for one in before:
            units.first_sum(one)
        if u == 4:
            pl.semaphore_wait(free, 1)
        units.core_copy(u).start()
        units.core_copy(u + 1).start()
        for shard in range(2):
            value = block(shard, c)
            for k in range(2):
                units.keep(u + k, shard, value[:, k * n : (k + 1) * n])

    def make_one(u, left_side, right_side, before):
        units.core_copy(u - 4).wait_send()
        for shard in range(2):
            value = mm_tn(left_side[:, shard * n : (shard + 1) * n], right_side)
            one, two = value[:, :n], value[:, n:]
            units.lay(u, shard, jnp.where(c == 0, two, one))
            units.keep(u, shard, jnp.where(c == 0, one, two))
        for one in before:
            units.first_sum(one)
        units.core_copy(u).start()

    for r in range(2):
        make_pair(
            2 * r,
            lambda shard, h: mm_tn(
                active[:, cols_at(shard * 4 * n + h * 2 * n + r * n, n)], branch[...]
            ),
            (0, 1) if r else (),
        )
    visit(12)
    for number in range(3):

        @pl.loop(number * 4, number * 4 + 4)
        def _(i):
            cols = cols_at(i * tile, tile)
            rate = bend[:, cols].astype(f32)
            low_pre = (mm_nt(branch[...], down[rows_at(i * tile, tile), :]) * rate).astype(bf16)
            bend[:, cols] = low_pre
            sums_up[:, cols] = jnp.sum(low_pre.astype(f32), axis=0, keepdims=True)

        if number == 0:
            units.first_sum(2)
            units.first_sum(3)
        visit(32 + number)

    for part in g_down:
        part.finish()
    pl.semaphore_signal(
        free, inc=1, device_id=here.across(1), device_id_type=pl.DeviceIdType.MESH
    )
    for p in range(2):
        make_pair(
            4 + 2 * p,
            lambda shard, h: mm_tn(
                hidden[:, shard * n : (shard + 1) * n], bend[:, cols_at(h * 4 * n + p * 2 * n, 2 * n)]
            ),
            (4, 5) if p else (),
        )
        visit(13 + p)

    @pl.loop(0, 2 * n // ROWS)
    def _(i):
        rows = rows_at(i * ROWS, ROWS)
        grad = mm_nt(bend[rows, :], up[...]) + second[rows, :]
        some = normed[rows, :]
        sums[3:4, :] += jnp.sum(grad * some, axis=0, keepdims=True)
        sums[4:5, :] += jnp.sum(grad, axis=0, keepdims=True)
        back = norm_back(grad, some, inverse[rows, 0:1], vecs[3:4, :])
        low_back = back.astype(bf16)
        second[rows, :] = back
        branch[rows, :] = low_back
        sums[2:3, :] += jnp.sum(low_back.astype(f32), axis=0, keepdims=True)
        slope[rows, :] = mm_nt(low_back, proj[...]).astype(bf16)

        @pl.when(i == 0)
        def _():
            units.first_sum(6)
            units.first_sum(7)

        visit_one_of(i, range(15, 18))

    make_one(8, heads, branch[...], ())
    visit(18)
    place = lax.rem(lanes, DH)

    @pl.loop(0, pairs)
    def _(i):
        cols, key_cols, value_cols = [cols_at(part * D + i * PAIR, PAIR) for part in range(3)]
        query = qkv[:, cols] * SCALE
        grad = slope[:, cols]
        product = grad.astype(f32) * heads[:, cols].astype(f32)
        sides = []
        for number, side in enumerate((left, jnp.logical_not(left))):
            delta = three_parts(-jnp.sum(jnp.where(side, product, 0.0), axis=1, keepdims=True))
            logs = jnp.where(lanes == 2 * i + number, lse[...], 0.0)
            logs = three_parts(-jnp.sum(logs, axis=1, keepdims=True))
            more = jnp.where(place == 2, logs[0], jnp.where(place == 3, logs[1], logs[2]))
            more = jnp.where(place < 2, mq[...], jnp.where(place < 5, more, 0.0).astype(bf16))
            some_query = jnp.where(side, query, more)
            more = jnp.where(place == 0, delta[0], jnp.where(place == 1, delta[1], delta[2]))
            some_grad = jnp.where(side, grad, jnp.where(place < 3, more, 0.0).astype(bf16))
            sides.append((side, some_query, some_grad))
        totals = [None, None]
        for start in range(0, 2 * n, ROWS):
            rows = pl.ds(start, ROWS)
            keys, values = qkv[rows, key_cols], qkv[rows, value_cols]
            ones, zeros = jnp.ones_like(values), jnp.zeros_like(values)
            more_keys = jnp.where(place < 2, mk[rows, :], jnp.where(place < 5, ones, zeros))
            more_values = jnp.where(place < 3, ones, zeros)
            parts = []
            for number, (side, some_query, some_grad) in enumerate(sides):
                some_keys = jnp.where(side, keys, more_keys)
                some_values = jnp.where(side, values, more_values)
                probs = jnp.exp(mm_nt(some_keys, some_query))
                rate = (probs * mm_nt(some_values, some_grad)).astype(bf16)
                dv = mm(probs.astype(bf16), some_grad)
                dk = mm(rate, some_query)
                dq = mm_tn(rate, some_keys)
                totals[number] = dq if totals[number] is None else totals[number] + dq
                parts.append((dk, dv))
            active[rows, key_cols] = jnp.where(left, parts[0][0], parts[1][0]).astype(bf16)
            active[rows, value_cols] = jnp.where(left, parts[0][1], parts[1][1]).astype(bf16)
        active[:, cols] = (jnp.where(left, totals[0], totals[1]) * SCALE).astype(bf16)

        @pl.when(i == 0)
        def _():
            units.first_sum(8)

        visit_one_of(i, range(19, 25))

    for k in range(3):
        make_one(9 + k, x, active[:, k * D : (k + 1) * D], (8 + k,) if k else ())
        visit(25 + k)
    units.first_sum(11)
    sums[0:1, :] = jnp.sum(active[:, 0:D].astype(f32), axis=0, keepdims=True)
    sums[1:2, :] = jnp.sum(active[:, 2 * D : 3 * D].astype(f32), axis=0, keepdims=True)
    for i in range(up.shape[1] // D):
        sums[8 + i : 9 + i, :] = sums_up[:, i * D : (i + 1) * D]

    rounds[0].start()

    @pl.loop(0, 2 * n // ROWS)
    def _(i):
        rows = rows_at(i * ROWS, ROWS)
        back = second[rows, :] + mm_nt(active[rows, 0 : 3 * D], three[...])
        hidden[rows, :] = back.astype(bf16)
        visit_one_of(i, range(28, 31))

    layer_away.start()
    layer_near.start()
    back_away.start()
    back_near.start()
    visit(31)
    for _ in rounds:
        next_round()
    small[0:8, :] = sums[0:8, cols_at(y * n, n)]
    for i in range(wide):
        k = i * n // D
        from_row = 8 + wide // 2 * y + k
        small[8 + i : 9 + i, :] = sums[pl.ds(from_row, 1), i * n % D : i * n % D + n]
    small_out = copies.near(small, o_small)
    small_out.start()
    units.finish()
    small_out.wait()
    for copy in (layer_away, back_away):
        copy.wait()
    for copy in (layer_near, back_near):
        copy.wait()
    for part in g_three + [g_attn] + g_up:
        part.finish()
    for copy in (vec_away, x_away, s_away):
        copy.wait_send()


def run_layer(tokens, cotangent, seq, lines, b_up, weights, reps):
    n = weights[0].shape[0]
    count, wide = 2 * n, weights[4].shape[1]
    bits = reps.bit_length() - 2
    kinds = [
        ((2, n, D), bf16),
        ((2, n, D), bf16),
        ((4 * n, D), bf16),
        ((n, wide), bf16),
        ((n, D), bf16),
        ((n, D), bf16),
        ((n, D), bf16),
        ((n, D), bf16),
        ((16, n), f32),
    ]
    near = [((UNITS, max(16, n >> (k + 1)), n), bf16) for k in range(3)]
    scratch = [
        ((count, D), bf16),
        ((count, D), bf16),
        ((D, 3 * D), bf16),
        ((D, D), bf16),
        ((D, wide), bf16),
        ((wide, D), bf16),
        ((2, 16, n), f32),
        ((16, D), f32),
        ((1, wide), f32),
        ((count, 3 * D), bf16),
        ((count, D), bf16),
        ((count, PAIR), f32),
        ((count, PAIR), bf16),
        ((count, PAIR), bf16),
        ((count, D), f32),
        ((count, PAIR), f32),
        ((count, D), bf16),
        ((count, wide), bf16),
        ((count, wide), bf16),
        ((count, D), bf16),
        ((count, D), f32),
        ((count, D), bf16),
        ((16, D), f32),
        ((1, wide), f32),
        ((bits + 2, 16, D), f32),
        ((UNITS, 2, 2, n // 2, n), bf16),
        ((UNITS, 2, n // 2, n), bf16),
        *near,
        ((UNITS, 2, 2, n // 2, n), bf16),
        ((16, n), f32),
    ]
    anywhere = pl.BlockSpec(memory_space=pl.ANY)
    stages = 5 + 2 * bits
    return pl.pallas_call(
        layer_kernel,
        out_shape=[jax.ShapeDtypeStruct(*kind) for kind in kinds],
        in_specs=[anywhere, anywhere, pl.BlockSpec(memory_space=pltpu.SMEM)]
        + [pl.BlockSpec(memory_space=pltpu.VMEM)] * 9
        + [anywhere] * 6,
        out_specs=[anywhere] * len(kinds),
        scratch_shapes=[pltpu.VMEM(*kind) for kind in scratch]
        + [
            pltpu.SemaphoreType.DMA((96,)),
            pltpu.SemaphoreType.DMA((96,)),
            pltpu.SemaphoreType.DMA((stages, UNITS)),
            pltpu.SemaphoreType.DMA((stages, UNITS)),
            pltpu.SemaphoreType.REGULAR,
        ],
        compiler_params=pltpu.CompilerParams(
            collective_id=0, has_side_effects=True, vmem_limit_bytes=67043328
        ),
        name="encoder_layer",
    )(tokens, cotangent, seq, *lines, b_up, *weights)


def split_vectors(table, *outs):
    *lines, b_up = outs
    n = table.shape[1]
    for i, line in enumerate(lines):
        line[...] = table[i : i + 1, :].reshape(n)
    for i in range(b_up.shape[0] // n):
        b_up[pl.ds(i * n, n)] = table[8 + i : 9 + i, :].reshape(n)


def run_split(table, wide):
    n = table.shape[1]
    inside = pl.BlockSpec(memory_space=pltpu.VMEM)
    return pl.pallas_call(
        split_vectors,
        out_shape=[jax.ShapeDtypeStruct((n,), f32)] * 8 + [jax.ShapeDtypeStruct((wide * n,), f32)],
        in_specs=[inside],
        out_specs=[inside] * 9,
        name="split_vectors",
    )(table)


def general_body(
    tokens,
    cotangent,
    seq_lengths,
    w_query,
    b_query,
    w_key,
    w_value,
    b_value,
    w_attn,
    b_attn,
    norm_gain,
    norm_bias,
    w_up,
    b_up,
    w_down,
    b_down,
    out_gain,
    out_bias,
):
    at = Places()
    shards = at.shards
    micro, slots = tokens.shape[0], tokens.shape[1]
    span = shards // micro
    count = micro * slots
    x = spread(at, tokens)
    w_three = gather_rows(at, jnp.concatenate([w_query, w_key, w_value], axis=1))
    part = w_query.shape[0]
    wide = b_up.shape[0] // part
    vectors = jnp.concatenate(
        [
            jnp.stack(
                [b_query, b_value, b_attn, norm_gain, norm_bias, b_down, out_gain, out_bias]
            ),
            b_up.reshape(wide, part),
            jnp.zeros((16 - 8 - wide, part), bf16),
        ],
        axis=0,
    )
    table = put(jnp.zeros((shards,) + vectors.shape, bf16), vectors[None], at.shard)
    for step in range(1, shards):
        there = swap(vectors, "shard", shards, lambda i: (i + shards - step) % shards)
        table = put(table, there[None], (at.shard + step) % shards)
    table = table.astype(f32)
    (c_query, c_value, c_attn, c_gain, c_bias, c_down, c_out_gain, c_out_bias) = [
        table[:, i].reshape(1, D) for i in range(8)
    ]
    c_up = table[:, 8 : 8 + wide].reshape(1, D * wide)
    w_proj = gather_rows(at, w_attn)
    full_up = gather_rows(at, w_up)
    full_down = gather_rows(at, w_down)
    slope_in = spread(at, cotangent)

    group = slots * shards
    which, inner = at.shard // span, at.shard % span
    row = lax.dynamic_index_in_dim(seq_lengths[:, 0], which, 0, False)
    ids = segment_ids(row, group)

    def ids_of(device):
        parts = []
        for step in range(micro):
            source = micro * device + (which + micro - step) % micro
            parts.append(lax.dynamic_slice_in_dim(ids, source * slots, slots))
        return jnp.concatenate(parts)

    query_ids = ids_of(inner)
    nseq = seq_lengths.shape[-1] - 1
    valid = (query_ids < nseq).astype(f32)[:, None]
    three = mm(x, w_three) + jnp.concatenate([c_query, jnp.zeros_like(c_query), c_value], axis=1)
    three = three.astype(bf16)
    base = D // PAIR
    offsets = (base, 2 * base)
    key_array = three
    key_ids = [query_ids]
    if span > 1:
        offsets = (0, base)
        own = three[:, D:]
        parts = [own]
        for step in range(1, span):
            moves = [(i, i // span * span + (i + span - step) % span) for i in range(shards)]
            parts.append(lax.ppermute(own, "shard", moves))
            key_ids.append(ids_of((inner + step) % span))
        key_array = jnp.concatenate(parts, axis=0)
    mq, _ = mask_columns(query_ids)
    _, mk = mask_columns(jnp.concatenate(key_ids))
    attn, lse = attention_forward(three, key_array, offsets, mq, mk)

    normed_one, inverse_one = normalize(x.astype(f32) + mm(attn, w_proj) + c_attn)
    hidden = normed_one * c_gain + c_bias
    hidden_low = hidden.astype(bf16)
    pre = mm(hidden_low, full_up) + c_up
    lower = 0.5 * (1.0 + lax.erf(pre * 0.7071067811865476))
    active = (pre * lower).astype(bf16)
    density = jnp.exp(-0.5 * pre * pre) * 0.3989422804014327
    gelu_slope = lower + pre * density
    normed_two, inverse_two = normalize(hidden + mm(active, full_down) + c_down)
    layer = (normed_two * c_out_gain + c_out_bias).astype(bf16)
    grad_out = slope_in.astype(f32) * valid
    d_out_gain = jnp.sum(grad_out * normed_two, axis=0)
    d_out_bias = jnp.sum(grad_out, axis=0)
    grad_second = norm_back(grad_out, normed_two, inverse_two, c_out_gain)
    grad_branch = grad_second.astype(bf16)
    d_down = jnp.sum(grad_branch.astype(f32), axis=0)
    g_down = mm_tn(active, grad_branch)
    grad_pre = (mm_nt(grad_branch, full_down) * gelu_slope).astype(bf16)
    d_up = jnp.sum(grad_pre.astype(f32), axis=0)
    g_up = mm_tn(hidden_low, grad_pre)
    grad_hidden = mm_nt(grad_pre, full_up) + grad_second
    d_gain = jnp.sum(grad_hidden * normed_one, axis=0)
    d_bias = jnp.sum(grad_hidden, axis=0)
    grad_first = norm_back(grad_hidden, normed_one, inverse_one, c_gain)
    grad_proj = grad_first.astype(bf16)
    d_attn = jnp.sum(grad_proj.astype(f32), axis=0)
    g_attn = mm_tn(attn, grad_proj)
    grad_attn = mm_nt(grad_proj, w_proj).astype(bf16)
    dq, dk, dv = attention_backward(three, key_array, offsets, mq, mk, attn, lse, grad_attn)
    if span > 1:
        both = jnp.concatenate([dk, dv], axis=1)
        total = both[:count].astype(f32)
        for step in range(1, span):
            moves = [(i, i // span * span + (i + step) % span) for i in range(shards)]
            away = both[step * count : (step + 1) * count]
            total = total + lax.ppermute(away, "shard", moves).astype(f32)
        dk, dv = total[:, :D].astype(bf16), total[:, D:].astype(bf16)
    d_three = jnp.concatenate([dq, dk, dv], axis=1)
    d_query = jnp.sum(dq.astype(f32), axis=0)
    d_value = jnp.sum(dv.astype(f32), axis=0)
    g_three = mm_tn(x, d_three)
    back = (grad_first + mm_nt(d_three, w_three)).astype(bf16)

    sums = jnp.concatenate(
        [
            jnp.stack([d_query, d_value, d_attn, d_gain, d_bias, d_down, d_out_gain, d_out_bias]).reshape(
                8, shards, part
            ),
            d_up.reshape(shards, wide, part).transpose(1, 0, 2),
            jnp.zeros((PAIR - 8 - wide, shards, part), f32),
        ],
        axis=0,
    )
    sums = sums.reshape(PAIR, D).T
    r_down = reduce_rows(at, g_down)
    r_up = reduce_rows(at, g_up)
    r_attn = reduce_rows(at, g_attn)
    r_three = reduce_rows(at, jnp.concatenate([g_three, sums], axis=1))
    small = r_three[:, 3 * D :].T
    return (
        collect(at, layer, micro),
        collect(at, back, micro),
        r_three[:, :D],
        small[0],
        r_three[:, D : 2 * D],
        r_three[:, 2 * D : 3 * D],
        small[1],
        r_attn,
        small[2],
        small[3],
        small[4],
        r_up,
        small[8 : 8 + wide].reshape(wide * part),
        r_down,
        small[5],
        small[6],
        small[7],
    )


def body(tokens, cotangent, seq_lengths, *weights):
    shards, micro = lax.axis_size("shard"), tokens.shape[0]
    reps = lax.axis_size("rep")
    if shards != 2 or micro != 2 or reps not in (4, 8, 16):
        return general_body(tokens, cotangent, seq_lengths, *weights)
    (
        w_query,
        b_query,
        w_key,
        w_value,
        b_value,
        w_attn,
        b_attn,
        norm_gain,
        norm_bias,
        w_up,
        b_up,
        w_down,
        b_down,
        out_gain,
        out_bias,
    ) = weights
    part = w_query.shape[0]
    wide = b_up.shape[0] // part
    lines = [b_query, b_value, b_attn, norm_gain, norm_bias, b_down, out_gain, out_bias]
    layer, back, *grads, small = run_layer(
        tokens,
        cotangent,
        seq_lengths,
        lines,
        b_up,
        (w_query, w_key, w_value, w_attn, w_up, w_down),
        reps,
    )
    g_down, g_up, g_attn, g_query, g_key, g_value = [grad.astype(f32) for grad in grads]
    d_query, d_value, d_attn, d_gain, d_bias, d_down, d_out_gain, d_out_bias, d_up = run_split(small, wide)
    return (
        layer,
        back,
        g_query,
        d_query,
        g_key,
        g_value,
        d_value,
        g_attn,
        d_attn,
        d_gain,
        d_bias,
        g_up,
        d_up,
        g_down,
        d_down,
        d_out_gain,
        d_out_bias,
    )


def solution(mesh):
    rows, vector = P("shard", None), P("shard")
    tokens = P(None, ("rep", "shard"), None)
    weights = (rows, vector, rows, rows, vector, rows, vector, vector, vector)
    weights += (rows, vector, rows, vector, vector, vector)
    return jax.shard_map(
        body,
        mesh=mesh,
        in_specs=(tokens, tokens, P(None, "rep", None)) + weights,
        out_specs=(tokens, tokens) + weights,
        check_vma=False,
    )
```

```python
import functools

import jax
import jax.numpy as jnp
from jax import lax
from jax.experimental import pallas as pl
from jax.experimental.pallas import tpu as pltpu
from jax.sharding import PartitionSpec as P

D = 768
H = 12
DH = 64
PAIR = 2 * DH
EPS = 1e-12
BIG = 1e30
SCALE = DH ** (-0.5)
ROWS = 256
f32 = jnp.float32
bf16 = jnp.bfloat16


def mm(left, right):
    return jnp.dot(left, right, preferred_element_type=f32)


def mm_nt(left, right):
    return lax.dot_general(left, right, (((1,), (1,)), ((), ())), preferred_element_type=f32)


def mm_tn(left, right):
    return lax.dot_general(left, right, (((0,), (0,)), ((), ())), preferred_element_type=f32)


def segment_ids(row, count):
    bounds = jnp.cumsum(row[:-1])
    places = jnp.arange(count, dtype=jnp.int32)
    return jnp.sum((places[:, None] >= bounds[None, :]).astype(jnp.int32), axis=1)


def mask_columns(ids):
    first = (ids == 0).astype(f32)[:, None]
    other = 1.0 - first
    lane = lax.broadcasted_iota(jnp.int32, (1, PAIR), 1) % DH
    on_query = jnp.where(lane == 0, -BIG * first, jnp.where(lane == 1, -BIG * other, 0.0))
    on_key = jnp.where(lane == 0, other, jnp.where(lane == 1, first, 0.0))
    return on_query.astype(bf16), on_key.astype(bf16)


def forward_heads(q_ref, k_ref, v_ref, mq_ref, mk_ref, attn_ref, lse_ref):
    lane = lax.broadcasted_iota(jnp.int32, (1, PAIR), 1)
    low = lane < DH
    keys, values, mk = k_ref[...], v_ref[...], mk_ref[...]
    one = jnp.ones_like(values)
    sides = []
    for own in (low, jnp.logical_not(low)):
        sides.append((own, jnp.where(own, keys, mk), jnp.where(own, values, one)))
    count = q_ref.shape[0]
    block = min(ROWS, count)
    for start in range(0, count, block):
        rows = pl.ds(start, block)
        query, mq = q_ref[rows, :] * SCALE, mq_ref[rows, :]
        outs = []
        for own, some_keys, some_values in sides:
            scores = mm_nt(jnp.where(own, query, mq), some_keys)
            top = jnp.max(scores, axis=1, keepdims=True)
            expo = jnp.exp(scores - top).astype(bf16)
            mixed = mm(expo, some_values)
            total = pltpu.roll(mixed, DH, 1)
            outs.append((mixed / total, top + jnp.log(total)))
        attn_ref[rows, :] = jnp.where(low, outs[0][0], outs[1][0]).astype(bf16)
        lse_ref[rows, :] = jnp.where(low, outs[0][1], outs[1][1])


def three_parts(value):
    first = value.astype(bf16).astype(f32)
    rest = value - first
    second = rest.astype(bf16).astype(f32)
    return first, second, rest - second


def backward_heads(
    q_ref, k_ref, v_ref, mq_ref, mk_ref, attn_ref, lse_ref, grad_ref, dq_ref, dk_ref, dv_ref
):
    lane = lax.broadcasted_iota(jnp.int32, (1, PAIR), 1)
    place = lane % DH
    low = lane < DH
    query, mq, grad = q_ref[...] * SCALE, mq_ref[...], grad_ref[...]
    product = grad.astype(f32) * attn_ref[...].astype(f32)
    lse = three_parts(-pltpu.roll(lse_ref[...], DH, 1))
    count_keys = k_ref.shape[0]
    block = min(ROWS, count_keys)
    sides = []
    for own in (low, jnp.logical_not(low)):
        delta = three_parts(-jnp.sum(jnp.where(own, product, 0.0), axis=1, keepdims=True))
        more = jnp.where(place == 2, lse[0], jnp.where(place == 3, lse[1], lse[2]))
        more = jnp.where(place < 2, mq, jnp.where(place < 5, more, 0.0).astype(bf16))
        some_query = jnp.where(own, query, more)
        more = jnp.where(place == 0, delta[0], jnp.where(place == 1, delta[1], delta[2]))
        some_grad = jnp.where(own, grad, jnp.where(place < 3, more, 0.0).astype(bf16))
        sides.append((own, some_query, some_grad, None))
    totals = [None, None]
    for start in range(0, count_keys, block):
        rows = pl.ds(start, block)
        keys, values, mk = k_ref[rows, :], v_ref[rows, :], mk_ref[rows, :]
        ones = jnp.ones_like(values)
        zeros = jnp.zeros_like(values)
        more_keys = jnp.where(place < 2, mk, jnp.where(place < 5, ones, zeros))
        more_values = jnp.where(place < 3, ones, zeros)
        parts = []
        for side in range(2):
            own, some_query, some_grad, _ = sides[side]
            some_keys = jnp.where(own, keys, more_keys)
            some_values = jnp.where(own, values, more_values)
            probs = jnp.exp(mm_nt(some_keys, some_query))
            slope = (probs * mm_nt(some_values, some_grad)).astype(bf16)
            dv = mm(probs.astype(bf16), some_grad)
            dk = mm(slope, some_query)
            dq = mm_tn(slope, some_keys)
            totals[side] = dq if totals[side] is None else totals[side] + dq
            parts.append((dk, dv))
        dk_ref[rows, :] = jnp.where(low, parts[0][0], parts[1][0]).astype(bf16)
        dv_ref[rows, :] = jnp.where(low, parts[0][1], parts[1][1]).astype(bf16)
    dq_ref[...] = (jnp.where(low, totals[0], totals[1]) * SCALE).astype(bf16)


def head_block(rows, offset):
    return pl.BlockSpec((rows, PAIR), lambda i: (0, i + offset))


def fixed_block(rows):
    return pl.BlockSpec((rows, PAIR), lambda i: (0, 0))


def attention_forward(query_array, key_array, offsets, mq, mk):
    count, keys = query_array.shape[0], key_array.shape[0]
    pairs = H * DH // PAIR
    return pl.pallas_call(
        forward_heads,
        grid=(pairs,),
        out_shape=(
            jax.ShapeDtypeStruct((count, D), bf16),
            jax.ShapeDtypeStruct((count, D), f32),
        ),
        in_specs=[
            head_block(count, 0),
            head_block(keys, offsets[0]),
            head_block(keys, offsets[1]),
            fixed_block(count),
            fixed_block(keys),
        ],
        out_specs=(head_block(count, 0), head_block(count, 0)),
        cost_estimate=pl.CostEstimate(
            flops=16 * count * keys * D, bytes_accessed=8 * (count + keys) * D, transcendentals=count * keys * H
        ),
        name="attention_forward",
    )(query_array, key_array, key_array, mq, mk)


def attention_backward(query_array, key_array, offsets, mq, mk, attn, lse, grad):
    count, keys = query_array.shape[0], key_array.shape[0]
    pairs = H * DH // PAIR
    return pl.pallas_call(
        backward_heads,
        grid=(pairs,),
        out_shape=(
            jax.ShapeDtypeStruct((count, D), bf16),
            jax.ShapeDtypeStruct((keys, D), bf16),
            jax.ShapeDtypeStruct((keys, D), bf16),
        ),
        in_specs=[
            head_block(count, 0),
            head_block(keys, offsets[0]),
            head_block(keys, offsets[1]),
            fixed_block(count),
            fixed_block(keys),
            head_block(count, 0),
            head_block(count, 0),
            head_block(count, 0),
        ],
        out_specs=(head_block(count, 0), head_block(keys, 0), head_block(keys, 0)),
        cost_estimate=pl.CostEstimate(
            flops=40 * count * keys * D, bytes_accessed=16 * (count + keys) * D, transcendentals=count * keys * H
        ),
        name="attention_backward",
    )(query_array, key_array, key_array, mq, mk, attn, lse, grad)


def normalize(rows):
    mean = jnp.mean(rows, axis=-1, keepdims=True)
    centered = rows - mean
    inverse = lax.rsqrt(jnp.mean(centered * centered, axis=-1, keepdims=True) + EPS)
    return centered * inverse, inverse


def norm_back(grad, normed, inverse, gain):
    scaled = grad * gain
    first = jnp.mean(scaled, axis=-1, keepdims=True)
    second = jnp.mean(scaled * normed, axis=-1, keepdims=True)
    return inverse * (scaled - first - normed * second)


def swap(value, axis, size, move):
    return lax.ppermute(value, axis, [(i, move(i)) for i in range(size)])


def put(buffer, value, index, axis=0):
    return lax.dynamic_update_slice_in_dim(buffer, value, index * value.shape[axis], axis)


def pick(value, index, parts, axis=0):
    size = value.shape[axis] // parts
    return lax.dynamic_slice_in_dim(value, index * size, size, axis)


class Places:
    def __init__(self):
        self.reps = lax.axis_size("rep")
        self.shards = lax.axis_size("shard")
        self.rep = lax.axis_index("rep")
        self.shard = lax.axis_index("shard")
        self.core = self.rep % 2


def gather_rows(at, own):
    half = own.shape[0] // 2
    out = jnp.zeros((at.shards * own.shape[0],) + own.shape[1:], own.dtype)
    out = put(out, own, at.shard)
    mine = pick(own, at.core, 2)
    for step in range(1, at.shards):
        there = swap(mine, "shard", at.shards, lambda i: (i + at.shards - step) % at.shards)
        other = swap(there, "rep", at.reps, lambda i: i ^ 1)
        block = (at.shard + step) % at.shards * 2
        out = put(out, there, block + at.core)
        out = put(out, other, block + 1 - at.core)
    return out


def reduce_rows(at, grad):
    shards, columns = at.shards, grad.shape[1]
    rows = grad.shape[0] // shards
    value = grad.reshape(shards * 2, rows // 2, columns)
    value = grad.reshape(shards, 2, rows // 2, columns)
    mine = lax.dynamic_index_in_dim(value, at.core, 1, False)
    away = lax.dynamic_index_in_dim(value, 1 - at.core, 1, False).astype(bf16)
    value = mine.astype(f32) + swap(away, "rep", at.reps, lambda i: i ^ 1).astype(f32)
    total = lax.dynamic_index_in_dim(value, at.shard, 0, False)
    for step in range(1, shards):
        away = lax.dynamic_index_in_dim(value, (at.shard + step) % shards, 0, False).astype(bf16)
        total = total + swap(away, "shard", shards, lambda i: (i + step) % shards).astype(f32)
    stages = []
    bit = 2
    while bit < at.reps:
        axis = 0 if total.shape[0] % 32 == 0 else 1
        stages.append((bit, axis))
        up = (at.rep // bit) % 2
        mine, away = pick(total, up, 2, axis), pick(total, 1 - up, 2, axis).astype(bf16)
        move = functools.partial(lambda b, i: i ^ b, bit)
        total = mine + swap(away, "rep", at.reps, move).astype(f32)
        bit *= 2
    total = total.astype(bf16)
    for bit, axis in reversed(stages):
        up = (at.rep // bit) % 2
        move = functools.partial(lambda b, i: i ^ b, bit)
        other = swap(total, "rep", at.reps, move)
        shape = list(total.shape)
        shape[axis] *= 2
        both = jnp.zeros(shape, bf16)
        total = put(put(both, total, up, axis), other, 1 - up, axis)
    other = swap(total, "rep", at.reps, lambda i: i ^ 1)
    first = jnp.where(at.core == 0, total, other)
    second = jnp.where(at.core == 0, other, total)
    return jnp.concatenate([first, second], axis=0).astype(f32)


def spread(at, value):
    micro, shards = value.shape[0], at.shards
    parts = []
    for step in range(micro):
        moves = [(i, (i + step) % micro * (shards // micro) + i // micro) for i in range(shards)]
        part = lax.dynamic_index_in_dim(value, (at.shard + step) % micro, 0, False)
        if any(a != b for a, b in moves):
            part = lax.ppermute(part, "shard", moves)
        parts.append(part)
    return jnp.concatenate(parts, axis=0)


def collect(at, value, micro):
    shards = at.shards
    slots = value.shape[0] // micro
    out = jnp.zeros((micro, slots) + value.shape[1:], value.dtype)
    for step in range(micro):
        moves = [((i + step) % micro * (shards // micro) + i // micro, i) for i in range(shards)]
        part = value[step * slots : (step + 1) * slots]
        if any(a != b for a, b in moves):
            part = lax.ppermute(part, "shard", moves)
        out = lax.dynamic_update_index_in_dim(out, part, (at.shard + step) % micro, 0)
    return out


def rows_at(start, size):
    return pl.ds(pl.multiple_of(start, 16), size)


def cols_at(start, size):
    return pl.ds(pl.multiple_of(start, PAIR), size)


class Here:
    def __init__(self):
        self.rep = lax.axis_index("rep")
        self.y = lax.axis_index("shard")
        self.core = lax.rem(self.rep, 2)
        self.x = lax.rem(lax.div(self.rep, 2), 2)

    def up(self, bit):
        return lax.rem(lax.div(self.rep, bit), 2)

    def across(self, *bits):
        return {"rep": self.rep + sum(bit * (1 - 2 * self.up(bit)) for bit in bits)}

    def over(self):
        return {"shard": 1 - self.y}


class Copies:
    def __init__(self, send, recv):
        self.send, self.recv, self.used, self.open = send, recv, 0, []

    def away(self, source, target, peer):
        k = self.used
        self.used += 1
        copy = pltpu.make_async_remote_copy(
            src_ref=source,
            dst_ref=target,
            send_sem=self.send.at[k],
            recv_sem=self.recv.at[k],
            device_id=peer,
            device_id_type=pl.DeviceIdType.MESH,
        )
        return copy

    def near(self, source, target):
        k = self.used
        self.used += 1
        return pltpu.make_async_copy(source, target, self.recv.at[k])


def greet(peers):
    barrier = pltpu.get_barrier_semaphore()
    for peer in peers:
        pl.semaphore_signal(barrier, inc=1, device_id=peer, device_id_type=pl.DeviceIdType.MESH)
    pl.semaphore_wait(barrier, len(peers))


class Gathered:
    def __init__(self, here, copies, own, full, mine, other, n, cols, bits):
        def at(start, size):
            return full.at[rows_at(start, size), cols]

        def held(level):
            start, size = here.core * (n // 2), n // 2
            for bit in reversed(bits[level:]):
                size //= 2
                start = start + here.up(bit) * size
            return start, size

        start, size = held(0)
        self.local = copies.near(own(0, n), at(mine, n))
        self.hops = [copies.away(own(start, size), at(mine + start, size), here.over())]
        for level, bit in enumerate(list(bits) + [1]):
            start, size = held(level)
            part = at(other + start, size)
            self.hops.append(copies.away(part, part, here.across(bit)))
        self.progress = 0

    def start(self):
        self.hops[0].start()
        self.local.start()

    def step(self, k):
        if k + 1 < len(self.hops):
            self.hops[k].wait_recv()
            self.hops[k + 1].start()
            self.progress += 1

    def ready(self):
        while self.progress + 1 < len(self.hops):
            self.step(self.progress)
        self.local.wait()
        self.hops[-1].wait_recv()

    def finish(self):
        for copy in self.hops:
            copy.wait_send()


def gelu_parts(pre):
    lower = 0.5 * (1.0 + lax.erf(pre * 0.7071067811865476))
    density = jnp.exp(-0.5 * pre * pre) * 0.3989422804014327
    return pre * lower, lower + pre * density


UNITS = 12
WAYS = (0, 1, 0, 0, 1, 0, 0, 0, 0, 0, 0, 0)
PLAN = (
    (3,),
    (),
    (7, 5),
    (9,),
    (7, 11),
    (5,),
    (10,),
    (11,),
    (7, 8),
    (),
    (9, 10),
    (11,),
    (),
    (),
    (20, 22),
    (),
    (23, 24, 20),
    (21, 22),
    (),
    (20, 23, 25, 21),
    (20, 22),
    (20, 23, 25, 26),
    (21, 22, 27, 26),
    (21, 23, 24),
    (21, 22, 25, 28, 26),
    (22, 27),
    (24,),
    (23, 25),
    (23, 26, 28, 40, 25, 29),
    (25, 27),
    (),
    (26, 24, 26, 30, 29, 28, 24, 27, 24, 31, 30, 29, 27, 28, 27, 31, 30, 28, 29, 28, 31, 40, 29, 40, 30, 29, 40, 31, 30, 30, 40, 31, 31),
    (),
    (),
    (20, 21),
    (),
    (),
    (),
    (),
    (),
    (4,),
    (5,),
    (3, 6),
    (4,),
    (8,),
    (),
    (3,),
    (4, 10, 6),
    (),
    (9,),
    (8,),
    (6,),
)
ORDER = [0] + [place for i in range(6) for place in (40 + 2 * i, 41 + 2 * i, 1 + i)]
ORDER += [*range(7, 13), 32, 33, 34, *range(13, 32)]


class Units:
    def __init__(self, here, reps, send, recv, swap_buffer, own, far, near, done, result):
        self.here, self.send, self.recv = here, send, recv
        self.swap_buffer, self.own, self.far, self.near, self.done = swap_buffer, own, far, near, done
        self.result = result
        self.n = own.shape[4]
        self.all_bits = []
        bit = 2
        while bit < reps:
            self.all_bits.append(bit)
            bit *= 2
        self.progress = [0] * UNITS
        depth = self.all_bits[1:]
        self.parts = 1 << len(depth)
        self.others = {}
        self.place = sum((here.up(bit) << k for k, bit in enumerate(depth)), 0)
        for j in range(1, self.parts):
            flips = [bit for k, bit in enumerate(depth) if j >> k & 1]
            place = 0
            for k, bit in enumerate(depth):
                up = here.up(bit)
                place = place + (1 - up if j >> k & 1 else up) * (1 << k)
            self.others[j] = (here.across(*flips), place)

    def copy(self, stage, u, source, target, peer):
        return pltpu.make_async_remote_copy(
            src_ref=source,
            dst_ref=target,
            send_sem=self.send.at[stage, u],
            recv_sem=self.recv.at[stage, u],
            device_id=peer,
            device_id_type=pl.DeviceIdType.MESH,
        )

    def slot(self, u, side):
        n = self.n
        if u < 4:
            return (self.done, self.own)[side].at[UNITS - 4 + u]
        return self.swap_buffer.at[pl.ds(u % 4 * 2 * n, 2 * n), pl.ds(side * n, n)]

    def lay(self, u, shard, value):
        n = self.n
        if u < 4:
            for part in range(2):
                rows = value[part * (n // 2) : (part + 1) * (n // 2), :]
                self.done[UNITS - 4 + u, shard, part] = rows.astype(bf16)
        else:
            rows = pl.ds(u % 4 * 2 * n + shard * n, n)
            self.swap_buffer[rows, pl.ds(0, n)] = value.astype(bf16)

    def theirs(self, u, shard, part):
        n = self.n
        if u < 4:
            return self.own[UNITS - 4 + u, shard, part]
        rows = rows_at(u % 4 * 2 * n + shard * n + part * (n // 2), n // 2)
        return self.swap_buffer[rows, pl.ds(n, n)]

    def core_copy(self, u):
        return self.copy(0, u, self.slot(u, 0), self.slot(u, 1), self.here.across(1))

    def away_copy(self, k, u):
        y, own, here = self.here.y, self.own, self.here
        up = here.up(2)
        if k == 0 and WAYS[u] == 0:
            return self.copy(1, u, own.at[u, 1 - y], self.far.at[u], here.over())
        if k == 0:
            return self.copy(1, u, own.at[u, :, 1 - up], self.far.at[u], here.across(2))
        if WAYS[u] == 0:
            return self.copy(2, u, own.at[u, y, 1 - up], self.near[0].at[u], here.across(2))
        return self.copy(2, u, own.at[u, 1 - y, up], self.near[0].at[u], here.over())

    def rows(self, place):
        size = self.n // 2 // self.parts
        return rows_at(place * size, size)

    def out_copy(self, j, u):
        peer, place = self.others[j]
        source = self.own.at[u, self.here.y, self.here.up(2), self.rows(place), :]
        return self.copy(2 + j, u, source, self.near[1].at[u, j - 1], peer)

    def in_copy(self, j, u):
        peer, _ = self.others[j]
        piece = self.done.at[u, self.here.core, self.here.up(2), self.rows(self.place), :]
        return self.copy(1 + self.parts + j, u, piece, piece, peer)

    def back_copy(self, k, u):
        piece = self.done.at[u, self.here.core]
        if k == 0:
            piece = piece.at[self.here.up(2)]
        return self.copy(1 + 2 * self.parts + k, u, piece, piece, self.here.across(1 if k else 2))

    def out_copies(self, u):
        n = self.n
        down, up, *square = self.result
        for h in range(2):
            for part in range(2):
                rows = part * (n // 2)
                if u < 4:
                    place = down.at[pl.ds(h * 2 * n + u // 2 * n + rows, n // 2), pl.ds(u % 2 * n, n)]
                elif u < 8:
                    place = up.at[pl.ds(rows, n // 2), pl.ds(h * 4 * n + (u - 4) * n, n)]
                else:
                    place = square[u - 8].at[pl.ds(rows, n // 2), pl.ds(h * n, n)]
                yield pltpu.make_async_copy(
                    self.done.at[u, h, part], place, (self.send, self.recv)[h].at[3 + 2 * self.parts + part, u]
                )

    def keep(self, u, shard, value):
        half = self.n // 2
        for part in range(2):
            self.own[u, shard, part] = value[part * half : (part + 1) * half, :].astype(bf16)

    def first_sum(self, u):
        y = self.here.y
        up = self.here.up(2)
        self.core_copy(u).wait_recv()
        if WAYS[u] == 0:
            order = [(1 - y, 0), (1 - y, 1), (y, 0), (y, 1)]
        else:
            order = [(0, 1 - up), (1, 1 - up), (0, up), (1, up)]
        for number, (shard, part) in enumerate(order):
            theirs = self.theirs(u, shard, part).astype(f32)
            self.own[u, shard, part] = (self.own[u, shard, part].astype(f32) + theirs).astype(bf16)
            if number == 1:
                self.away_copy(0, u).start()

    def step(self, u, k):
        if k == 6:
            return
        self.progress[u] += 1
        y, own, up = self.here.y, self.own, self.here.up(2)
        if k == 0:
            self.away_copy(0, u).wait_recv()
            if WAYS[u] == 0:
                order = [((y, 1 - up), 1 - up), ((y, up), up)]
            else:
                order = [((1 - y, up), 1 - y), ((y, up), y)]
            for number, ((shard, part), source) in enumerate(order):
                theirs = self.far[u, source].astype(f32)
                own[u, shard, part] = (own[u, shard, part].astype(f32) + theirs).astype(bf16)
                if number == 0:
                    self.away_copy(1, u).start()
        elif k == 1:
            self.away_copy(1, u).wait_recv()
            for j in list(self.others) + [0]:
                rows = self.rows(self.others[j][1] if j else self.place)
                theirs = self.near[0][u, rows, :].astype(f32)
                own[u, y, up, rows, :] = (own[u, y, up, rows, :].astype(f32) + theirs).astype(bf16)
                if j:
                    self.out_copy(j, u).start()
        elif k == 2:
            rows = self.rows(self.place)
            total = own[u, y, up, rows, :].astype(f32)
            for j in self.others:
                self.out_copy(j, u).wait_recv()
                total = total + self.near[1][u, j - 1].astype(f32)
            self.done[u, self.here.core, up, rows, :] = total.astype(bf16)
            for j in self.others:
                self.in_copy(j, u).start()
        elif k == 3:
            for j in self.others:
                self.in_copy(j, u).wait_recv()
            self.back_copy(0, u).start()
        elif k == 4:
            self.back_copy(0, u).wait_recv()
            self.back_copy(1, u).start()
        else:
            self.back_copy(1, u).wait_recv()
            for copy in self.out_copies(u):
                copy.start()

    def finish(self):
        for u in range(UNITS):
            while self.progress[u] < 6:
                self.step(u, self.progress[u])
        for u in range(UNITS):
            if u >= UNITS - 4:
                self.core_copy(u).wait_send()
            for k in range(2):
                self.away_copy(k, u).wait_send()
                self.back_copy(k, u).wait_send()
            for j in self.others:
                self.out_copy(j, u).wait_send()
                self.in_copy(j, u).wait_send()
            for copy in self.out_copies(u):
                copy.wait()


def layer_kernel(
    tokens,
    cotangent,
    seq,
    *rest,
):
    lines, b_up, weights = rest[:8], rest[8], rest[9:15]
    layer_steps(tokens, cotangent, seq, lines, b_up, *weights, rest[15:24], *rest[24:])


def layer_steps(
    tokens,
    cotangent,
    seq,
    lines,
    b_up,
    w_query,
    w_key,
    w_value,
    w_attn,
    w_up,
    w_down,
    outs,
    x,
    slope,
    three,
    proj,
    up,
    down,
    raw_vectors,
    vecs,
    vec_up,
    qkv,
    heads,
    lse,
    mq,
    mk,
    normed,
    inverse,
    hidden,
    active,
    bend,
    branch,
    second,
    layer,
    sums,
    sums_up,
    others,
    own,
    far,
    near_one,
    near_two,
    done,
    small,
    send,
    recv,
    unit_send,
    unit_recv,
    free,
):
    reps = lax.axis_size("rep")
    here = Here()
    copies = Copies(send, recv)
    n = w_query.shape[0]
    y = here.y
    near = (near_one, near_two)
    o_layer, o_back, *o_grads, o_small = outs
    units = Units(here, reps, unit_send, unit_recv, down, own, far, near, done, o_grads)
    peers = [here.over(), here.across(1)] + [here.across(bit) for bit in units.all_bits]
    greet(peers)

    wide = up.shape[1] // (2 * n)

    pieces = []

    def piece(weight, full, row, col, into):
        def own(start, size):
            return weight.at[rows_at(row + start, size), pl.ds(col, D)]

        rows = weight.shape[0]
        bits = units.all_bits[:2]
        pieces.append(
            Gathered(
                here,
                copies,
                own,
                full,
                y * rows + row,
                (1 - y) * rows + row,
                n,
                pl.ds(into + col, D),
                bits if len(pieces) % 2 == 0 else bits[::-1],
            )
        )
        return pieces[-1]

    g_three = [piece(w, three, 0, 0, k * D) for k, w in enumerate((w_query, w_key, w_value))]
    g_attn = piece(w_attn, proj, 0, 0, 0)
    g_up = [piece(w_up, up, 0, k * D, 0) for k in range(up.shape[1] // D)]
    g_down = [piece(w_down, down, k * n, 0, 0) for k in range(w_down.shape[0] // n)]
    vec_away = copies.away(raw_vectors.at[y], raw_vectors.at[y], here.over())
    low, high = pl.ds(0, n), pl.ds(n, n)
    x_away = copies.away(tokens.at[1 - y], x.at[high, :], here.over())
    x_near = copies.near(tokens.at[y], x.at[low, :])
    s_away = copies.away(cotangent.at[1 - y], slope.at[high, :], here.over())
    s_near = copies.near(cotangent.at[y], slope.at[low, :])
    layer_away = copies.away(layer.at[high, :], o_layer.at[y], here.over())
    layer_near = copies.near(layer.at[low, :], o_layer.at[y])
    back_away = copies.away(hidden.at[high, :], o_back.at[y], here.over())
    back_near = copies.near(hidden.at[low, :], o_back.at[y])
    x_near.start()
    for part in g_three:
        part.start()
    for i, line in enumerate(lines):
        raw_vectors[y, i : i + 1, :] = line[...].astype(f32).reshape(1, n)
    for i in range(wide):
        raw_vectors[y, 8 + i : 9 + i, :] = b_up[i * n : (i + 1) * n].astype(f32).reshape(1, n)
    vec_away.start()
    x_away.start()
    for part in [g_attn] + g_up + g_down:
        part.start()
    s_away.start()
    s_near.start()

    length = seq[y, 0, 0]

    def inside(start, size):
        row = start + lax.broadcasted_iota(jnp.int32, (size, 1), 0)
        place = row + jnp.where(row < n, y * n, -y * n)
        return (place < length).astype(f32)

    first = inside(0, 2 * n)
    lane = lax.rem(lax.broadcasted_iota(jnp.int32, (1, PAIR), 1), DH)
    mq[...] = jnp.where(
        lane == 0, -BIG * first, jnp.where(lane == 1, -BIG * (1.0 - first), 0.0)
    ).astype(bf16)
    mk[...] = jnp.where(lane == 0, 1.0 - first, jnp.where(lane == 1, first, 0.0)).astype(bf16)
    sums[...] = jnp.zeros_like(sums)
    lse[...] = jnp.zeros_like(lse)

    for k in range(3):
        for part in g_three:
            part.step(k)
    vec_away.wait_recv()
    for half in range(2):
        table = raw_vectors[half]
        vecs[:, half * n : (half + 1) * n] = table
        for i in range(wide):
            start = half * wide * n + i * n
            vec_up[:, start : start + n] = table[8 + i : 9 + i, :]
    for part in g_three:
        part.ready()
    x_near.wait()
    tile = 256

    @pl.loop(0, 2)
    def _(half):
        pl.when(half == 1)(x_away.wait_recv)
        rows = rows_at(half * n, n)

        @pl.loop(0, 3 * D // tile)
        def _(i):
            cols = cols_at(i * tile, tile)
            which = lax.div(i, D // tile)
            inner = cols_at(lax.rem(i, D // tile) * tile, tile)
            bias = jnp.where(
                which == 0, vecs[0:1, inner], jnp.where(which == 2, vecs[1:2, inner], 0.0)
            )
            qkv[rows, cols] = (mm(x[rows, :], three[:, cols]) + bias).astype(bf16)

    rounds = []
    ways = [here.across(1), here.over()] + [here.across(bit) for bit in units.all_bits]
    for k, way in enumerate(ways):
        rounds.append(copies.away(sums, others.at[k], way))
    round_done = [0]

    def next_round():
        k = round_done[0]
        if k < len(rounds):
            round_done[0] = k + 1
            rounds[k].wait()
            sums[...] += others[k]
            if k + 1 < len(rounds):
                rounds[k + 1].start()

    numbered, count = {}, {}
    for place in ORDER:
        numbered[place] = []
        for one in PLAN[place]:
            numbered[place].append((one, count.get(one, 0)))
            count[one] = count.get(one, 0) + 1

    def visit(place):
        for one, k in numbered[place]:
            if one == 40:
                next_round()
            elif one >= 20:
                units.step(one - 20, k)
            else:
                pieces[one].step(k)

    def visit_one_of(i, places):
        for number, place in enumerate(places):
            if not PLAN[place]:
                continue

            @pl.when(i == number)
            def _():
                visit(place)

    visit(0)
    lanes = lax.broadcasted_iota(jnp.int32, (1, PAIR), 1)
    left = lanes < DH
    pairs = H * DH // PAIR

    @pl.loop(0, pairs)
    def _(i):
        keys, values = qkv[:, cols_at(D + i * PAIR, PAIR)], qkv[:, cols_at(2 * D + i * PAIR, PAIR)]
        one = jnp.ones_like(values)
        sides = []
        for side in (left, jnp.logical_not(left)):
            sides.append((side, jnp.where(side, keys, mk[...]), jnp.where(side, values, one)))
        for start in range(0, 2 * n, ROWS):
            rows = pl.ds(start, ROWS)
            query = qkv[rows, cols_at(i * PAIR, PAIR)] * SCALE
            outs = []
            total_lse = lse[rows, :]
            for number, (side, some_keys, some_values) in enumerate(sides):
                scores = mm_nt(jnp.where(side, query, mq[rows, :]), some_keys)
                top = jnp.max(scores, axis=1, keepdims=True)
                expo = jnp.exp(scores - top).astype(bf16)
                mixed = mm(expo, some_values)
                total = pltpu.roll(mixed, DH, 1)
                outs.append(mixed / total)
                sum_all = jnp.where(side, total, mixed)
                total_lse = jnp.where(lanes == 2 * i + number, top + jnp.log(sum_all), total_lse)
            lse[rows, :] = total_lse
            heads[rows, cols_at(i * PAIR, PAIR)] = jnp.where(left, outs[0], outs[1]).astype(bf16)
            turn = start // ROWS
            visit_one_of(i, range(40 + turn, 52, 2) if turn < 2 else range(1, 7))

    g_attn.ready()

    @pl.loop(0, 2 * n // ROWS)
    def _(i):
        rows = rows_at(i * ROWS, ROWS)
        resid = x[rows, :].astype(f32) + mm(heads[rows, :], proj[...]) + vecs[2:3, :]
        some, scale = normalize(resid)
        normed[rows, :] = some
        inverse[rows, :] = jnp.broadcast_to(scale, (ROWS, PAIR))
        hidden[rows, :] = (some * vecs[3:4, :] + vecs[4:5, :]).astype(bf16)

    visit(7)
    for number, part in enumerate(g_up):
        part.ready()

        @pl.loop(number * D // tile, (number + 1) * D // tile)
        def _(i):
            cols = cols_at(i * tile, tile)
            pre = mm(hidden[...], up[:, cols]) + vec_up[:, cols]
            value, rate = gelu_parts(pre)
            active[:, cols] = value.astype(bf16)
            bend[:, cols] = rate.astype(bf16)

        visit(8 + number)

    for part in g_down:
        part.ready()
    s_away.wait_recv()
    s_near.wait()

    @pl.loop(0, 2 * n // ROWS)
    def _(i):
        rows = rows_at(i * ROWS, ROWS)
        resid = mm(active[rows, :], down[...]) + vecs[5:6, :]
        resid = resid + (normed[rows, :] * vecs[3:4, :] + vecs[4:5, :])
        some, scale = normalize(resid)
        layer[rows, :] = (some * vecs[6:7, :] + vecs[7:8, :]).astype(bf16)
        grad = slope[rows, :].astype(f32) * inside(i * ROWS, ROWS)
        back = norm_back(grad, some, scale, vecs[6:7, :])
        low_back = back.astype(bf16)
        second[rows, :] = back
        branch[rows, :] = low_back
        sums[5:6, :] += jnp.sum(low_back.astype(f32), axis=0, keepdims=True)
        sums[6:7, :] += jnp.sum(grad * some, axis=0, keepdims=True)
        sums[7:8, :] += jnp.sum(grad, axis=0, keepdims=True)

    c = here.core

    def make_pair(u, block, before):
        for one in (u, u + 1):
            if one >= 4:
                units.core_copy(one - 4).wait_send()
        for shard in range(2):
            value = block(shard, 1 - c)
            for k in range(2):
                units.lay(u + k, shard, value[:, k * n : (k + 1) * n])
        for one in before:
            units.first_sum(one)
        if u == 4:
            pl.semaphore_wait(free, 1)
        units.core_copy(u).start()
        units.core_copy(u + 1).start()
        for shard in range(2):
            value = block(shard, c)
            for k in range(2):
                units.keep(u + k, shard, value[:, k * n : (k + 1) * n])

    def make_one(u, left_side, right_side, before):
        units.core_copy(u - 4).wait_send()
        for shard in range(2):
            value = mm_tn(left_side[:, shard * n : (shard + 1) * n], right_side)
            one, two = value[:, :n], value[:, n:]
            units.lay(u, shard, jnp.where(c == 0, two, one))
            units.keep(u, shard, jnp.where(c == 0, one, two))
        for one in before:
            units.first_sum(one)
        units.core_copy(u).start()

    for r in range(2):
        make_pair(
            2 * r,
            lambda shard, h: mm_tn(
                active[:, cols_at(shard * 4 * n + h * 2 * n + r * n, n)], branch[...]
            ),
            (0, 1) if r else (),
        )
    visit(12)
    for number in range(3):

        @pl.loop(number * 4, number * 4 + 4)
        def _(i):
            cols = cols_at(i * tile, tile)
            rate = bend[:, cols].astype(f32)
            low_pre = (mm_nt(branch[...], down[rows_at(i * tile, tile), :]) * rate).astype(bf16)
            bend[:, cols] = low_pre
            sums_up[:, cols] = jnp.sum(low_pre.astype(f32), axis=0, keepdims=True)

        if number == 0:
            units.first_sum(2)
            units.first_sum(3)
        visit(32 + number)

    for part in g_down:
        part.finish()
    pl.semaphore_signal(
        free, inc=1, device_id=here.across(1), device_id_type=pl.DeviceIdType.MESH
    )
    for p in range(2):
        make_pair(
            4 + 2 * p,
            lambda shard, h: mm_tn(
                hidden[:, shard * n : (shard + 1) * n], bend[:, cols_at(h * 4 * n + p * 2 * n, 2 * n)]
            ),
            (4, 5) if p else (),
        )
        visit(13 + p)

    @pl.loop(0, 2 * n // ROWS)
    def _(i):
        rows = rows_at(i * ROWS, ROWS)
        grad = mm_nt(bend[rows, :], up[...]) + second[rows, :]
        some = normed[rows, :]
        sums[3:4, :] += jnp.sum(grad * some, axis=0, keepdims=True)
        sums[4:5, :] += jnp.sum(grad, axis=0, keepdims=True)
        back = norm_back(grad, some, inverse[rows, 0:1], vecs[3:4, :])
        low_back = back.astype(bf16)
        second[rows, :] = back
        branch[rows, :] = low_back
        sums[2:3, :] += jnp.sum(low_back.astype(f32), axis=0, keepdims=True)
        slope[rows, :] = mm_nt(low_back, proj[...]).astype(bf16)

        @pl.when(i == 0)
        def _():
            units.first_sum(6)
            units.first_sum(7)

        visit_one_of(i, range(15, 18))

    make_one(8, heads, branch[...], ())
    visit(18)
    place = lax.rem(lanes, DH)

    @pl.loop(0, pairs)
    def _(i):
        cols, key_cols, value_cols = [cols_at(part * D + i * PAIR, PAIR) for part in range(3)]
        query = qkv[:, cols] * SCALE
        grad = slope[:, cols]
        product = grad.astype(f32) * heads[:, cols].astype(f32)
        sides = []
        for number, side in enumerate((left, jnp.logical_not(left))):
            delta = three_parts(-jnp.sum(jnp.where(side, product, 0.0), axis=1, keepdims=True))
            logs = jnp.where(lanes == 2 * i + number, lse[...], 0.0)
            logs = three_parts(-jnp.sum(logs, axis=1, keepdims=True))
            more = jnp.where(place == 2, logs[0], jnp.where(place == 3, logs[1], logs[2]))
            more = jnp.where(place < 2, mq[...], jnp.where(place < 5, more, 0.0).astype(bf16))
            some_query = jnp.where(side, query, more)
            more = jnp.where(place == 0, delta[0], jnp.where(place == 1, delta[1], delta[2]))
            some_grad = jnp.where(side, grad, jnp.where(place < 3, more, 0.0).astype(bf16))
            sides.append((side, some_query, some_grad))
        totals = [None, None]
        for start in range(0, 2 * n, ROWS):
            rows = pl.ds(start, ROWS)
            keys, values = qkv[rows, key_cols], qkv[rows, value_cols]
            ones, zeros = jnp.ones_like(values), jnp.zeros_like(values)
            more_keys = jnp.where(place < 2, mk[rows, :], jnp.where(place < 5, ones, zeros))
            more_values = jnp.where(place < 3, ones, zeros)
            parts = []
            for number, (side, some_query, some_grad) in enumerate(sides):
                some_keys = jnp.where(side, keys, more_keys)
                some_values = jnp.where(side, values, more_values)
                probs = jnp.exp(mm_nt(some_keys, some_query))
                rate = (probs * mm_nt(some_values, some_grad)).astype(bf16)
                dv = mm(probs.astype(bf16), some_grad)
                dk = mm(rate, some_query)
                dq = mm_tn(rate, some_keys)
                totals[number] = dq if totals[number] is None else totals[number] + dq
                parts.append((dk, dv))
            active[rows, key_cols] = jnp.where(left, parts[0][0], parts[1][0]).astype(bf16)
            active[rows, value_cols] = jnp.where(left, parts[0][1], parts[1][1]).astype(bf16)
        active[:, cols] = (jnp.where(left, totals[0], totals[1]) * SCALE).astype(bf16)

        @pl.when(i == 0)
        def _():
            units.first_sum(8)

        visit_one_of(i, range(19, 25))

    for k in range(3):
        make_one(9 + k, x, active[:, k * D : (k + 1) * D], (8 + k,) if k else ())
        visit(25 + k)
    units.first_sum(11)
    sums[0:1, :] = jnp.sum(active[:, 0:D].astype(f32), axis=0, keepdims=True)
    sums[1:2, :] = jnp.sum(active[:, 2 * D : 3 * D].astype(f32), axis=0, keepdims=True)
    for i in range(up.shape[1] // D):
        sums[8 + i : 9 + i, :] = sums_up[:, i * D : (i + 1) * D]

    rounds[0].start()

    for number in range(2):
        rows = pl.ds((1 - number) * n, n)
        back = second[rows, :] + mm_nt(active[rows, 0 : 3 * D], three[...])
        hidden[rows, :] = back.astype(bf16)
        if number == 0:
            back_away.start()
        visit(28 + number)

    back_near.start()
    visit(30)
    layer_away.start()
    layer_near.start()
    visit(31)
    for _ in rounds:
        next_round()
    small[0:8, :] = sums[0:8, cols_at(y * n, n)]
    for i in range(wide):
        k = i * n // D
        from_row = 8 + wide // 2 * y + k
        small[8 + i : 9 + i, :] = sums[pl.ds(from_row, 1), i * n % D : i * n % D + n]
    small_out = copies.near(small, o_small)
    small_out.start()
    units.finish()
    small_out.wait()
    for copy in (layer_away, back_away):
        copy.wait()
    for copy in (layer_near, back_near):
        copy.wait()
    for part in g_three + [g_attn] + g_up:
        part.finish()
    for copy in (vec_away, x_away, s_away):
        copy.wait_send()


def run_layer(tokens, cotangent, seq, lines, b_up, weights, reps):
    n = weights[0].shape[0]
    count, wide = 2 * n, weights[4].shape[1]
    bits = reps.bit_length() - 2
    kinds = [
        ((2, n, D), bf16),
        ((2, n, D), bf16),
        ((4 * n, D), bf16),
        ((n, wide), bf16),
        ((n, D), bf16),
        ((n, D), bf16),
        ((n, D), bf16),
        ((n, D), bf16),
        ((16, n), f32),
    ]
    parts = reps // 4
    near = [((UNITS, n // 2, n), bf16), ((UNITS, max(1, parts - 1), n // 2 // parts, n), bf16)]
    scratch = [
        ((count, D), bf16),
        ((count, D), bf16),
        ((D, 3 * D), bf16),
        ((D, D), bf16),
        ((D, wide), bf16),
        ((wide, D), bf16),
        ((2, 16, n), f32),
        ((16, D), f32),
        ((1, wide), f32),
        ((count, 3 * D), bf16),
        ((count, D), bf16),
        ((count, PAIR), f32),
        ((count, PAIR), bf16),
        ((count, PAIR), bf16),
        ((count, D), f32),
        ((count, PAIR), f32),
        ((count, D), bf16),
        ((count, wide), bf16),
        ((count, wide), bf16),
        ((count, D), bf16),
        ((count, D), f32),
        ((count, D), bf16),
        ((16, D), f32),
        ((1, wide), f32),
        ((bits + 2, 16, D), f32),
        ((UNITS, 2, 2, n // 2, n), bf16),
        ((UNITS, 2, n // 2, n), bf16),
        *near,
        ((UNITS, 2, 2, n // 2, n), bf16),
        ((16, n), f32),
    ]
    anywhere = pl.BlockSpec(memory_space=pl.ANY)
    stages = 5 + 2 * parts
    return pl.pallas_call(
        layer_kernel,
        out_shape=[jax.ShapeDtypeStruct(*kind) for kind in kinds],
        in_specs=[anywhere, anywhere, pl.BlockSpec(memory_space=pltpu.SMEM)]
        + [pl.BlockSpec(memory_space=pltpu.VMEM)] * 9
        + [anywhere] * 6,
        out_specs=[anywhere] * len(kinds),
        scratch_shapes=[pltpu.VMEM(*kind) for kind in scratch]
        + [
            pltpu.SemaphoreType.DMA((96,)),
            pltpu.SemaphoreType.DMA((96,)),
            pltpu.SemaphoreType.DMA((stages, UNITS)),
            pltpu.SemaphoreType.DMA((stages, UNITS)),
            pltpu.SemaphoreType.REGULAR,
        ],
        compiler_params=pltpu.CompilerParams(
            collective_id=0, has_side_effects=True, vmem_limit_bytes=67043328
        ),
        name="encoder_layer",
    )(tokens, cotangent, seq, *lines, b_up, *weights)


STEPS = 2


def finish_kernel(*refs):
    table = refs[8]
    for source, target in zip(refs[:8], refs[9:17]):
        target[...] = source[...].astype(target.dtype)
    *lines, b_up = refs[17:]
    n = table.shape[1]

    @pl.when(pl.program_id(0) == 0)
    def _():
        for i, line in enumerate(lines):
            line[...] = table[i : i + 1, :].reshape(n)
        for i in range(b_up.shape[0] // n):
            b_up[pl.ds(i * n, n)] = table[8 + i : 9 + i, :].reshape(n)


def run_finish(arrays, table, wide):
    n = table.shape[1]
    inside = pl.BlockSpec(table.shape, lambda i: (0, 0))

    def blocks(array):
        if array.ndim == 3:
            return pl.BlockSpec((2, array.shape[1] // STEPS, array.shape[2]), lambda i: (0, i, 0))
        return pl.BlockSpec((array.shape[0] // STEPS, array.shape[1]), lambda i: (i, 0))

    kinds = [bf16] * 2 + [f32] * 6
    lines = [n] * 8 + [wide * n]
    specs = [blocks(array) for array in arrays]
    return pl.pallas_call(
        finish_kernel,
        grid=(STEPS,),
        out_shape=[jax.ShapeDtypeStruct(a.shape, kind) for a, kind in zip(arrays, kinds)]
        + [jax.ShapeDtypeStruct((size,), f32) for size in lines],
        in_specs=specs + [inside],
        out_specs=specs + [pl.BlockSpec((size,), lambda i: (0,)) for size in lines],
        name="finish",
    )(*arrays, table)


def general_body(
    tokens,
    cotangent,
    seq_lengths,
    w_query,
    b_query,
    w_key,
    w_value,
    b_value,
    w_attn,
    b_attn,
    norm_gain,
    norm_bias,
    w_up,
    b_up,
    w_down,
    b_down,
    out_gain,
    out_bias,
):
    at = Places()
    shards = at.shards
    micro, slots = tokens.shape[0], tokens.shape[1]
    span = shards // micro
    count = micro * slots
    x = spread(at, tokens)
    w_three = gather_rows(at, jnp.concatenate([w_query, w_key, w_value], axis=1))
    part = w_query.shape[0]
    wide = b_up.shape[0] // part
    vectors = jnp.concatenate(
        [
            jnp.stack(
                [b_query, b_value, b_attn, norm_gain, norm_bias, b_down, out_gain, out_bias]
            ),
            b_up.reshape(wide, part),
            jnp.zeros((16 - 8 - wide, part), bf16),
        ],
        axis=0,
    )
    table = put(jnp.zeros((shards,) + vectors.shape, bf16), vectors[None], at.shard)
    for step in range(1, shards):
        there = swap(vectors, "shard", shards, lambda i: (i + shards - step) % shards)
        table = put(table, there[None], (at.shard + step) % shards)
    table = table.astype(f32)
    (c_query, c_value, c_attn, c_gain, c_bias, c_down, c_out_gain, c_out_bias) = [
        table[:, i].reshape(1, D) for i in range(8)
    ]
    c_up = table[:, 8 : 8 + wide].reshape(1, D * wide)
    w_proj = gather_rows(at, w_attn)
    full_up = gather_rows(at, w_up)
    full_down = gather_rows(at, w_down)
    slope_in = spread(at, cotangent)

    group = slots * shards
    which, inner = at.shard // span, at.shard % span
    row = lax.dynamic_index_in_dim(seq_lengths[:, 0], which, 0, False)
    ids = segment_ids(row, group)

    def ids_of(device):
        parts = []
        for step in range(micro):
            source = micro * device + (which + micro - step) % micro
            parts.append(lax.dynamic_slice_in_dim(ids, source * slots, slots))
        return jnp.concatenate(parts)

    query_ids = ids_of(inner)
    nseq = seq_lengths.shape[-1] - 1
    valid = (query_ids < nseq).astype(f32)[:, None]
    three = mm(x, w_three) + jnp.concatenate([c_query, jnp.zeros_like(c_query), c_value], axis=1)
    three = three.astype(bf16)
    base = D // PAIR
    offsets = (base, 2 * base)
    key_array = three
    key_ids = [query_ids]
    if span > 1:
        offsets = (0, base)
        own = three[:, D:]
        parts = [own]
        for step in range(1, span):
            moves = [(i, i // span * span + (i + span - step) % span) for i in range(shards)]
            parts.append(lax.ppermute(own, "shard", moves))
            key_ids.append(ids_of((inner + step) % span))
        key_array = jnp.concatenate(parts, axis=0)
    mq, _ = mask_columns(query_ids)
    _, mk = mask_columns(jnp.concatenate(key_ids))
    attn, lse = attention_forward(three, key_array, offsets, mq, mk)

    normed_one, inverse_one = normalize(x.astype(f32) + mm(attn, w_proj) + c_attn)
    hidden = normed_one * c_gain + c_bias
    hidden_low = hidden.astype(bf16)
    pre = mm(hidden_low, full_up) + c_up
    lower = 0.5 * (1.0 + lax.erf(pre * 0.7071067811865476))
    active = (pre * lower).astype(bf16)
    density = jnp.exp(-0.5 * pre * pre) * 0.3989422804014327
    gelu_slope = lower + pre * density
    normed_two, inverse_two = normalize(hidden + mm(active, full_down) + c_down)
    layer = (normed_two * c_out_gain + c_out_bias).astype(bf16)
    grad_out = slope_in.astype(f32) * valid
    d_out_gain = jnp.sum(grad_out * normed_two, axis=0)
    d_out_bias = jnp.sum(grad_out, axis=0)
    grad_second = norm_back(grad_out, normed_two, inverse_two, c_out_gain)
    grad_branch = grad_second.astype(bf16)
    d_down = jnp.sum(grad_branch.astype(f32), axis=0)
    g_down = mm_tn(active, grad_branch)
    grad_pre = (mm_nt(grad_branch, full_down) * gelu_slope).astype(bf16)
    d_up = jnp.sum(grad_pre.astype(f32), axis=0)
    g_up = mm_tn(hidden_low, grad_pre)
    grad_hidden = mm_nt(grad_pre, full_up) + grad_second
    d_gain = jnp.sum(grad_hidden * normed_one, axis=0)
    d_bias = jnp.sum(grad_hidden, axis=0)
    grad_first = norm_back(grad_hidden, normed_one, inverse_one, c_gain)
    grad_proj = grad_first.astype(bf16)
    d_attn = jnp.sum(grad_proj.astype(f32), axis=0)
    g_attn = mm_tn(attn, grad_proj)
    grad_attn = mm_nt(grad_proj, w_proj).astype(bf16)
    dq, dk, dv = attention_backward(three, key_array, offsets, mq, mk, attn, lse, grad_attn)
    if span > 1:
        both = jnp.concatenate([dk, dv], axis=1)
        total = both[:count].astype(f32)
        for step in range(1, span):
            moves = [(i, i // span * span + (i + step) % span) for i in range(shards)]
            away = both[step * count : (step + 1) * count]
            total = total + lax.ppermute(away, "shard", moves).astype(f32)
        dk, dv = total[:, :D].astype(bf16), total[:, D:].astype(bf16)
    d_three = jnp.concatenate([dq, dk, dv], axis=1)
    d_query = jnp.sum(dq.astype(f32), axis=0)
    d_value = jnp.sum(dv.astype(f32), axis=0)
    g_three = mm_tn(x, d_three)
    back = (grad_first + mm_nt(d_three, w_three)).astype(bf16)

    sums = jnp.concatenate(
        [
            jnp.stack([d_query, d_value, d_attn, d_gain, d_bias, d_down, d_out_gain, d_out_bias]).reshape(
                8, shards, part
            ),
            d_up.reshape(shards, wide, part).transpose(1, 0, 2),
            jnp.zeros((PAIR - 8 - wide, shards, part), f32),
        ],
        axis=0,
    )
    sums = sums.reshape(PAIR, D).T
    r_down = reduce_rows(at, g_down)
    r_up = reduce_rows(at, g_up)
    r_attn = reduce_rows(at, g_attn)
    r_three = reduce_rows(at, jnp.concatenate([g_three, sums], axis=1))
    small = r_three[:, 3 * D :].T
    return (
        collect(at, layer, micro),
        collect(at, back, micro),
        r_three[:, :D],
        small[0],
        r_three[:, D : 2 * D],
        r_three[:, 2 * D : 3 * D],
        small[1],
        r_attn,
        small[2],
        small[3],
        small[4],
        r_up,
        small[8 : 8 + wide].reshape(wide * part),
        r_down,
        small[5],
        small[6],
        small[7],
    )


def body(tokens, cotangent, seq_lengths, *weights):
    shards, micro = lax.axis_size("shard"), tokens.shape[0]
    reps = lax.axis_size("rep")
    if shards != 2 or micro != 2 or reps not in (4, 8, 16):
        return general_body(tokens, cotangent, seq_lengths, *weights)
    (
        w_query,
        b_query,
        w_key,
        w_value,
        b_value,
        w_attn,
        b_attn,
        norm_gain,
        norm_bias,
        w_up,
        b_up,
        w_down,
        b_down,
        out_gain,
        out_bias,
    ) = weights
    part = w_query.shape[0]
    wide = b_up.shape[0] // part
    lines = [b_query, b_value, b_attn, norm_gain, norm_bias, b_down, out_gain, out_bias]
    *arrays, small = run_layer(
        tokens,
        cotangent,
        seq_lengths,
        lines,
        b_up,
        (w_query, w_key, w_value, w_attn, w_up, w_down),
        reps,
    )
    layer, back, g_down, g_up, g_attn, g_query, g_key, g_value, *lines = run_finish(arrays, small, wide)
    d_query, d_value, d_attn, d_gain, d_bias, d_down, d_out_gain, d_out_bias, d_up = lines
    return (
        layer,
        back,
        g_query,
        d_query,
        g_key,
        g_value,
        d_value,
        g_attn,
        d_attn,
        d_gain,
        d_bias,
        g_up,
        d_up,
        g_down,
        d_down,
        d_out_gain,
        d_out_bias,
    )


def solution(mesh):
    rows, vector = P("shard", None), P("shard")
    tokens = P(None, ("rep", "shard"), None)
    weights = (rows, vector, rows, rows, vector, rows, vector, vector, vector)
    weights += (rows, vector, rows, vector, vector, vector)
    return jax.shard_map(
        body,
        mesh=mesh,
        in_specs=(tokens, tokens, P(None, "rep", None)) + weights,
        out_specs=(tokens, tokens) + weights,
        check_vma=False,
    )
```
